256 devices in a mesh: gx: 4 (over y_lo, core), gy: 16 (over y_hi, z), gz: 4 (over x).
Axes of the slice: x: 4, y: 4 (y_hi: 2, y_lo: 2; y = y_hi * 2 + y_lo), z: 8, core: 2. Of those that a mesh axis runs over, the one named last changes fastest.
Arguments:
- adjoint: float32 [19, 32, 256, 512], P(None, 'gx', 'gy', 'gz'), may hold values from -6 to 6
- density: float32 [2, 32, 256, 512], P(None, 'gx', 'gy', 'gz'), may hold values from 0.8 to 1.2
- velocity: float32 [2, 3, 32, 256, 512], P(None, None, 'gx', 'gy', 'gz'), may hold values from -0.25 to 0.25
- pore_mask: int32 [32, 256, 512], P('gx', 'gy', 'gz'), may hold values from 0 to 1, as said below
Outputs:
- adjoint_out: float32 [19, 32, 256, 512], P(None, 'gx', 'gy', 'gz')
- sensitivity: float32 [32, 256, 512], P('gx', 'gy', 'gz')
The draws below stay inside these ranges and needn't reach their ends.
Inputs may be any that keep to these rules, and one draw needn't show every extreme that they name: `pore_mask`: 1 marks a pore voxel and 0 a solid one.
All inputs are finite; a program needn't handle non-finite values.
Results may differ from the reference program's by a relative error of at most 0.00002.
Values sent between devices are 32-bit elements; how exact they have to be, the bound alone decides.
A program may use at most 128 MiB of HBM per device.

```python
import jax
import jax.numpy as jnp

CX = 8
CY = 16
CZ = 128
NX = 32
NY = 256
NZ = 512


def draw_pore_mask(key, part):
    first, second = jax.random.split(jax.random.fold_in(key, 7))
    levels = jax.random.randint(first, (NX // CX, NY // CY, NZ // CZ), 15, 96)
    levels = jnp.repeat(jnp.repeat(jnp.repeat(levels, CX, axis=0), CY, axis=1), CZ, axis=2)
    ticket = jax.random.randint(second, (NX, NY, NZ), 0, 100)
    return jnp.where(ticket < levels, 1, 0).astype(jnp.int32)


def block_levels(key, dims, cuts, low, top_value):
    def one(axis_at, parts):
        draws = jax.random.uniform(jax.random.fold_in(jax.random.fold_in(key, 6), axis_at), (parts,), jnp.float32, low / len(cuts), top_value / len(cuts))
        return jnp.repeat(jnp.exp(draws), dims[axis_at] // parts).reshape((-1,) + (1,) * (len(dims) - axis_at - 1))

    gain = one(*cuts[0])
    for cut in cuts[1:]:
        gain = gain * one(*cut)
    return gain


def bell_draw(rng, extent, scale, limit, shards=(), kind=jnp.bfloat16):
    factor_of = block_levels(rng, extent, shards, -0.22, 0.18) if shards else 1.0
    drawn = jax.random.normal(rng, extent, jnp.float32) * scale * factor_of
    return jnp.minimum(jnp.maximum(drawn, -limit), limit).astype(kind)


def setup_inputs(seed: int = 0) -> dict:
    key_of = jax.random.split(jax.random.key(seed), 5)
    adjoint = bell_draw(key_of[0], (19, NX, NY, NZ), 1.0, 6.0, ((1, 4), (2, 16), (3, 4)), jnp.float32)
    density = jnp.clip(0.8 + 0.40000004 * jax.random.uniform(key_of[1], (2, NX, NY, NZ), jnp.float32) ** block_levels(key_of[1], (2, NX, NY, NZ), ((1, 4), (2, 16), (3, 4)), -0.2, 0.2), 0.8, 1.2)
    velocity = bell_draw(key_of[2], (2, 3, NX, NY, NZ), 0.05, 0.25, ((2, 4), (3, 16), (4, 4)), jnp.float32)
    pore_mask = draw_pore_mask(jax.random.fold_in(key_of[4], 71), 0)
    return dict(adjoint=adjoint, density=density, velocity=velocity, pore_mask=pore_mask)


VELOCITIES = [(0, 0, 0), (1, 0, 0), (-1, 0, 0), (0, 1, 0), (0, -1, 0), (0, 0, 1), (0, 0, -1),
              (1, 1, 0), (-1, -1, 0), (1, -1, 0), (-1, 1, 0), (1, 0, 1), (-1, 0, -1),
              (1, 0, -1), (-1, 0, 1), (0, 1, 1), (0, -1, -1), (0, 1, -1), (0, -1, 1)]
WEIGHTS = [1.0 / 3.0] + [1.0 / 18.0] * 6 + [1.0 / 36.0] * 12
OPPOSITE = [0, 2, 1, 4, 3, 6, 5, 8, 7, 10, 9, 12, 11, 14, 13, 16, 15, 18, 17]
OMEGA = 1.25


def collide(pulled, rho, speed, pores):
    ux, uy, uz = speed[0], speed[1], speed[2]
    usq = ux * ux + uy * uy + uz * uz
    shapes = []
    moment = jnp.zeros_like(rho)
    vec_x = jnp.zeros_like(rho)
    vec_y = jnp.zeros_like(rho)
    vec_z = jnp.zeros_like(rho)
    for index in range(19):
        cx, cy, cz = VELOCITIES[index]
        weight = WEIGHTS[index]
        along = cx * ux + cy * uy + cz * uz
        shaped = weight * (1.0 + 3.0 * along + 4.5 * along * along - 1.5 * usq)
        shapes.append(shaped)
        moment = moment + pulled[index] * shaped
        common = pulled[index] * weight
        vec_x = vec_x + common * (3.0 * cx + 9.0 * along * cx - 3.0 * ux)
        vec_y = vec_y + common * (3.0 * cy + 9.0 * along * cy - 3.0 * uy)
        vec_z = vec_z + common * (3.0 * cz + 9.0 * along * cz - 3.0 * uz)
    fluid = pores > 0
    layers = []
    change = jnp.zeros_like(rho)
    for index in range(19):
        cx, cy, cz = VELOCITIES[index]
        project = vec_x * (cx - ux) + vec_y * (cy - uy) + vec_z * (cz - uz)
        collided = (1.0 - OMEGA) * pulled[index] + OMEGA * (moment + project) + (cx - ux) / rho
        layers.append(jnp.where(fluid, collided, pulled[OPPOSITE[index]]))
        change = change + (pulled[OPPOSITE[index]] - pulled[index]) * rho * shapes[index]
    return jnp.stack(layers), jnp.where(fluid, change, 0.0)


def reference(adjoint, density, velocity, pore_mask):
    field = adjoint
    total = jnp.zeros(pore_mask.shape, jnp.float32)
    ext_x, ext_y, ext_z = pore_mask.shape
    for level in (1, 0):
        padded = jnp.pad(field, ((0, 0), (1, 1), (1, 1), (1, 1)))
        pulled = jnp.stack([padded[index, 1 + VELOCITIES[index][0]:1 + VELOCITIES[index][0] + ext_x,
                                   1 + VELOCITIES[index][1]:1 + VELOCITIES[index][1] + ext_y,
                                   1 + VELOCITIES[index][2]:1 + VELOCITIES[index][2] + ext_z] for index in range(19)])
        field, change = collide(pulled, density[level], velocity[level], pore_mask)
        total = total + change
    return field, total
```

```python
import functools

import jax
import jax.numpy as jnp
from jax import lax
from jax.experimental import pallas as pl
from jax.experimental.pallas import tpu as pltpu
from jax.sharding import PartitionSpec as P

VELOCITIES = [
    (0, 0, 0),
    (1, 0, 0),
    (-1, 0, 0),
    (0, 1, 0),
    (0, -1, 0),
    (0, 0, 1),
    (0, 0, -1),
    (1, 1, 0),
    (-1, -1, 0),
    (1, -1, 0),
    (-1, 1, 0),
    (1, 0, 1),
    (-1, 0, -1),
    (1, 0, -1),
    (-1, 0, 1),
    (0, 1, 1),
    (0, -1, -1),
    (0, 1, -1),
    (0, -1, 1),
]
WEIGHTS = [1.0 / 3.0] + [1.0 / 18.0] * 6 + [1.0 / 36.0] * 12
OPPOSITE = [0, 2, 1, 4, 3, 6, 5, 8, 7, 10, 9, 12, 11, 14, 13, 16, 15, 18, 17]
OMEGA = 1.25
MESH = pl.DeviceIdType.MESH

CXP = [1, 7, 9, 11, 13]
CXM = [2, 8, 10, 12, 14]
CYP = [3, 7, 10, 15, 17]
CYM = [4, 8, 9, 16, 18]
ZCOLS = [(5, 0), (11, 0), (14, 0), (15, 0), (18, 0), (6, -1), (12, -1), (13, -1), (16, -1), (17, -1)]
ZFACE_COL = {5: 0, 11: 8, 14: 16, 15: 24, 18: 32, 6: 0, 12: 8, 13: 16, 16: 24, 17: 32}
XZ_EDGE = {11: (40, 0), 14: (48, -16), 12: (40, -16), 13: (48, 0)}
YZ_CORNER = {15: (56, 0), 18: (64, -1), 16: (56, -1), 17: (64, 0)}
XY_EDGE = {7: (0, 0), 8: (1, 7), 9: (2, 7), 10: (3, 0)}


def _messages(cx, cy):
    rows = cx * cy
    msgs = []
    for k, pop in enumerate(CXP):
        msgs.append(((-1, 0, 0), ("S", pop, 0, cy), ("XH", 1, k)))
    for k, pop in enumerate(CXM):
        msgs.append(((1, 0, 0), ("S", pop, rows - cy, cy), ("XH", 0, k)))
    msgs.append(((0, -1, 0), ("SY", 0), ("YH", 1)))
    msgs.append(((0, 1, 0), ("SY", 1), ("YH", 0)))
    msgs.append(((-1, -1, 0), ("S", 7, 0, 8), ("EXY", 0)))
    msgs.append(((1, 1, 0), ("S", 8, rows - 8, 8), ("EXY", 1)))
    msgs.append(((-1, 1, 0), ("S", 9, cy - 8, 8), ("EXY", 2)))
    msgs.append(((1, -1, 0), ("S", 10, rows - cy, 8), ("EXY", 3)))
    msgs.append(((0, 0, -1), ("NT", 0, 40), ("MH", 1, 0, 40)))
    msgs.append(((0, 0, 1), ("NT", 40, 40), ("MH", 0, 0, 40)))
    msgs.append(((-1, 0, -1), ("NT", 8, 8), ("MH", 1, 40, 8)))
    msgs.append(((1, 0, -1), ("NT", 16, 8), ("MH", 1, 48, 8)))
    msgs.append(((1, 0, 1), ("NT", 48, 8), ("MH", 0, 40, 8)))
    msgs.append(((-1, 0, 1), ("NT", 56, 8), ("MH", 0, 48, 8)))
    msgs.append(((0, -1, -1), ("NT", 24, 8), ("MH", 1, 56, 8)))
    msgs.append(((0, 1, -1), ("NT", 32, 8), ("MH", 1, 64, 8)))
    msgs.append(((0, 1, 1), ("NT", 64, 8), ("MH", 0, 56, 8)))
    msgs.append(((0, -1, 1), ("NT", 72, 8), ("MH", 0, 64, 8)))
    return msgs


NEIGHBOURS = sorted(
    {d for d, _, _ in _messages(8, 16)} | {tuple(-v for v in d) for d, _, _ in _messages(8, 16)}
)


def _comb(vals, fn):
    total = None
    for weight in (1.0 / 3.0, 1.0 / 18.0, 1.0 / 36.0):
        part = None
        for i in range(19):
            if WEIGHTS[i] != weight:
                continue
            k = fn(VELOCITIES[i])
            if k == 0:
                continue
            if part is None:
                part = vals[i] if k > 0 else -vals[i]
            else:
                part = part + vals[i] if k > 0 else part - vals[i]
        if part is not None:
            term = part * weight
            total = term if total is None else total + term
    return total


def _collide(pulled, rho, ux, uy, uz, fluid):
    p0 = _comb(pulled, lambda c: 1)
    p1 = [_comb(pulled, lambda c, a=a: c[a]) for a in range(3)]
    q = {}
    for a in range(3):
        for b in range(a, 3):
            q[a, b] = _comb(pulled, lambda c, a=a, b=b: c[a] * c[b])
            q[b, a] = q[a, b]
    u = (ux, uy, uz)
    usq = ux * ux + uy * uy + uz * uz
    qu = [q[a, 0] * ux + q[a, 1] * uy + q[a, 2] * uz for a in range(3)]
    p1u = p1[0] * ux + p1[1] * uy + p1[2] * uz
    uqu = ux * qu[0] + uy * qu[1] + uz * qu[2]
    moment = p0 * (1.0 - 1.5 * usq) + 3.0 * p1u + 4.5 * uqu
    vec = [3.0 * p1[a] + 9.0 * qu[a] - 3.0 * u[a] * p0 for a in range(3)]
    vu = vec[0] * ux + vec[1] * uy + vec[2] * uz
    inv = 1.0 / rho
    base = OMEGA * (moment - vu) - ux * inv
    bases = {0: base, 1: base + inv, -1: base - inv}
    wv = [OMEGA * v for v in vec]
    combos = {}
    layers = []
    for i in range(19):
        c = VELOCITIES[i]
        key = tuple(c)
        terms = [(a, c[a]) for a in range(3) if c[a] != 0]
        cv = None
        if terms:
            if len(terms) == 1:
                a, s = terms[0]
                cv = wv[a] if s > 0 else -wv[a]
            else:
                (a, s), (b, t) = terms
                pos = (a, b, s * t)
                if pos not in combos:
                    combos[pos] = wv[a] + wv[b] if s * t > 0 else wv[a] - wv[b]
                cv = combos[pos] if s > 0 else -combos[pos]
        val = (1.0 - OMEGA) * pulled[i] + bases[c[0]]
        if cv is not None:
            val = val + cv
        layers.append(jnp.where(fluid, val, pulled[OPPOSITE[i]]))
    sens = None
    for i in range(1, 19, 2):
        c = VELOCITIES[i]
        along = None
        for a in range(3):
            if c[a] == 0:
                continue
            if along is None:
                along = u[a] if c[a] > 0 else -u[a]
            else:
                along = along + u[a] if c[a] > 0 else along - u[a]
        term = (6.0 * WEIGHTS[i]) * along * (pulled[OPPOSITE[i]] - pulled[i])
        sens = term if sens is None else sens + term
    sens = jnp.where(fluid, rho * sens, 0.0)
    return layers, sens


def _kernel(dims, adj_ref, rho_ref, vel_ref, mask_ref, out_ref, sens_ref,
            mid, xh, yh, exy, sy, nt, mh, mt, send_sem, recv_sem):
    nx, ny, nz = dims
    cx, cy, cz = 8, 16, 128
    rows = cx * cy
    me = (lax.axis_index("gx"), lax.axis_index("gy"), lax.axis_index("gz"))
    sizes = (nx, ny, nz)

    def exists(d):
        cond = None
        for a in range(3):
            if d[a] == 0:
                continue
            v = me[a] + d[a]
            c = (v >= 0) if d[a] < 0 else (v < sizes[a])
            cond = c if cond is None else jnp.logical_and(cond, c)
        return cond

    def target(d):
        return tuple(me[a] + d[a] for a in range(3))

    xh[...] = jnp.zeros(xh.shape, jnp.float32)
    yh[...] = jnp.zeros(yh.shape, jnp.float32)
    exy[...] = jnp.zeros(exy.shape, jnp.float32)
    mh[...] = jnp.zeros(mh.shape, jnp.float32)

    barrier = pltpu.get_barrier_semaphore()
    for d in NEIGHBOURS:
        @pl.when(exists(d))
        def _():
            pl.semaphore_signal(barrier, inc=1, device_id=target(d), device_id_type=MESH)

    lane = lax.broadcasted_iota(jnp.int32, (cy, cz), 1)
    lane1 = lax.broadcasted_iota(jnp.int32, (1, cz), 1)
    row = lax.broadcasted_iota(jnp.int32, (cy, cz), 0)
    lane_big = lax.broadcasted_iota(jnp.int32, (rows, cz), 1)

    msgs = _messages(cx, cy)

    def prepare(s, src):
        for side, pops, y in ((0, CYP, 0), (1, CYM, cy - 1)):
            for k, pop in enumerate(pops):
                sy[s, side, k] = src[pop, pl.ds(y, cx, stride=cy), :]
        n = jnp.zeros((rows, cz), jnp.float32)
        for j, (pop, z) in enumerate(ZCOLS):
            zz = z % cz
            n = jnp.where(lane_big == 8 * j, pltpu.roll(src[pop], (8 * j - zz) % cz, 1), n)
        nt[s] = n.T

    def descriptor(s, src, m, t):
        d, so, de = msgs[t]
        if so[0] == "S":
            sref = src.at[so[1], pl.ds(so[2] % rows, so[3]), :]
        elif so[0] == "SY":
            sref = sy.at[s, so[1]]
        else:
            sref = nt.at[s, pl.ds(so[1], so[2]), :]
        if de[0] == "XH":
            dref = xh.at[s, de[1], de[2]]
        elif de[0] == "YH":
            dref = yh.at[s, de[1]]
        elif de[0] == "EXY":
            dref = exy.at[s, de[1]]
        else:
            dref = mh.at[s, de[1], pl.ds(de[2], de[3]), :]
        return pltpu.make_async_remote_copy(
            src_ref=sref, dst_ref=dref, send_sem=send_sem.at[s, t], recv_sem=recv_sem.at[s, t],
            device_id=target(d), device_id_type=MESH)

    def send(s, src):
        for t in range(len(msgs)):
            d = msgs[t][0]

            @pl.when(exists(d))
            def _():
                descriptor(s, src, msgs, t).start()

    def finish(s, src):
        for t in range(len(msgs)):
            d = msgs[t][0]
            back = tuple(-v for v in d)

            @pl.when(exists(back))
            def _():
                descriptor(s, src, msgs, t).wait_recv()

            @pl.when(exists(d))
            def _():
                descriptor(s, src, msgs, t).wait_send()
        for side in range(2):
            mt[s, side] = mh[s, side].T

    def pulled_plane(s, src, p):
        out = []
        for i in range(19):
            vx, vy, vz = VELOCITIES[i]
            q = p + vx
            if 0 <= q < cx:
                plane = src[i, pl.ds(q * cy, cy), :]
            elif q == cx:
                plane = xh[s, 1, CXP.index(i)]
            else:
                plane = xh[s, 0, CXM.index(i)]
            if vz != 0:
                side = 1 if vz > 0 else 0
                if 0 <= q < cx:
                    zc = mt[s, side, pl.ds(q * cy, cy), :]
                    col = ZFACE_COL[i]
                else:
                    col, r0 = XZ_EDGE[i]
                    zc = mt[s, side, pl.ds(r0 % rows, cy), :]
                if vz > 0:
                    plane = jnp.where(lane == cz - 1, pltpu.roll(zc, (cz - 1 - col) % cz, 1),
                                      pltpu.roll(plane, cz - 1, 1))
                else:
                    plane = jnp.where(lane == 0, pltpu.roll(zc, (cz - col) % cz, 1),
                                      pltpu.roll(plane, 1, 1))
            if vy != 0:
                side_y = 1 if vy > 0 else 0
                ky = CYP.index(i) if vy > 0 else CYM.index(i)
                if 0 <= q < cx:
                    yrow = yh[s, side_y, ky, pl.ds(q, 1), :]
                else:
                    e, r = XY_EDGE[i]
                    yrow = exy[s, e, pl.ds(r, 1), :]
                if vz != 0:
                    side = 1 if vz > 0 else 0
                    colc, yoff = YZ_CORNER[i]
                    crow = mt[s, side, pl.ds(p * cy + yoff % cy, 1), :]
                    if vz > 0:
                        yrow = jnp.where(lane1 == cz - 1, pltpu.roll(crow, (cz - 1 - colc) % cz, 1),
                                         pltpu.roll(yrow, cz - 1, 1))
                    else:
                        yrow = jnp.where(lane1 == 0, pltpu.roll(crow, (cz - colc) % cz, 1),
                                         pltpu.roll(yrow, 1, 1))
                if vy > 0:
                    plane = jnp.where(row == cy - 1, yrow, pltpu.roll(plane, cy - 1, 0))
                else:
                    plane = jnp.where(row == 0, yrow, pltpu.roll(plane, 1, 0))
            out.append(plane)
        return out

    def step(s, src, dst, level):
        for p in range(cx):
            rs = pl.ds(p * cy, cy)
            pulled = pulled_plane(s, src, p)
            rho = rho_ref[level, rs, :]
            ux = vel_ref[level, 0, rs, :]
            uy = vel_ref[level, 1, rs, :]
            uz = vel_ref[level, 2, rs, :]
            fluid = mask_ref[rs, :] > 0
            layers, sens = _collide(pulled, rho, ux, uy, uz, fluid)
            for i in range(19):
                dst[i, rs, :] = layers[i]
            if s == 0:
                sens_ref[rs, :] = sens
            else:
                sens_ref[rs, :] = sens_ref[rs, :] + sens

    def indicator(a, off):
        n = sizes[a]
        if off < 0:
            return (me[a] + n - 1) // n
        if off > 0:
            return (2 * n - 2 - me[a]) // n
        return 1

    peers = 0
    for d in NEIGHBOURS:
        term = 1
        for a in range(3):
            term = term * indicator(a, d[a])
        peers = peers + term
    prepare(0, adj_ref)
    pl.semaphore_wait(barrier, peers)
    send(0, adj_ref)
    finish(0, adj_ref)
    step(0, adj_ref, mid, 1)
    prepare(1, mid)
    send(1, mid)
    finish(1, mid)
    step(1, mid, out_ref, 0)


def solution(mesh):
    nx, ny, nz = mesh.shape["gx"], mesh.shape["gy"], mesh.shape["gz"]
    nmsg = len(_messages(8, 16))

    def shards(adjoint, density, velocity, pore_mask):
        npop, cx, cy, cz = adjoint.shape
        assert (cx, cy, cz) == (8, 16, 128)
        rows = cx * cy
        adj = adjoint.reshape(npop, rows, cz)
        rho = density.reshape(2, rows, cz)
        vel = velocity.reshape(2, 3, rows, cz)
        mask = pore_mask.reshape(rows, cz)
        vspec = pl.BlockSpec(memory_space=pltpu.VMEM)
        out, sens = pl.pallas_call(
            functools.partial(_kernel, (nx, ny, nz)),
            out_shape=(
                jax.ShapeDtypeStruct((npop, rows, cz), jnp.float32),
                jax.ShapeDtypeStruct((rows, cz), jnp.float32),
            ),
            in_specs=[vspec] * 4,
            out_specs=(vspec, vspec),
            scratch_shapes=[
                pltpu.VMEM((npop, rows, cz), jnp.float32),
                pltpu.VMEM((2, 2, 5, cy, cz), jnp.float32),
                pltpu.VMEM((2, 2, 5, cx, cz), jnp.float32),
                pltpu.VMEM((2, 4, 8, cz), jnp.float32),
                pltpu.VMEM((2, 2, 5, cx, cz), jnp.float32),
                pltpu.VMEM((2, rows, cz), jnp.float32),
                pltpu.VMEM((2, 2, rows, cz), jnp.float32),
                pltpu.VMEM((2, 2, rows, cz), jnp.float32),
                pltpu.SemaphoreType.DMA((2, nmsg)),
                pltpu.SemaphoreType.DMA((2, nmsg)),
            ],
            compiler_params=pltpu.CompilerParams(
                collective_id=0, has_side_effects=True, vmem_limit_bytes=48 * 1024 * 1024
            ),
        )(adj, rho, vel, mask)
        return out.reshape(npop, cx, cy, cz), sens.reshape(cx, cy, cz)

    placed = (
        P(None, "gx", "gy", "gz"),
        P(None, "gx", "gy", "gz"),
        P(None, None, "gx", "gy", "gz"),
        P("gx", "gy", "gz"),
    )
    return jax.shard_map(
        shards,
        mesh=mesh,
        in_specs=placed,
        out_specs=(P(None, "gx", "gy", "gz"), P("gx", "gy", "gz")),
        check_vma=False,
    )
```

```python
import functools

import jax
import jax.numpy as jnp
from jax import lax
from jax.experimental import pallas as pl
from jax.experimental.pallas import tpu as pltpu
from jax.sharding import PartitionSpec as P

VELOCITIES = [
    (0, 0, 0),
    (1, 0, 0),
    (-1, 0, 0),
    (0, 1, 0),
    (0, -1, 0),
    (0, 0, 1),
    (0, 0, -1),
    (1, 1, 0),
    (-1, -1, 0),
    (1, -1, 0),
    (-1, 1, 0),
    (1, 0, 1),
    (-1, 0, -1),
    (1, 0, -1),
    (-1, 0, 1),
    (0, 1, 1),
    (0, -1, -1),
    (0, 1, -1),
    (0, -1, 1),
]
WEIGHTS = [1.0 / 3.0] + [1.0 / 18.0] * 6 + [1.0 / 36.0] * 12
OPPOSITE = [0, 2, 1, 4, 3, 6, 5, 8, 7, 10, 9, 12, 11, 14, 13, 16, 15, 18, 17]
OMEGA = 1.25
MESH = pl.DeviceIdType.MESH

CXP = [1, 7, 9, 11, 13]
CXM = [2, 8, 10, 12, 14]
CYP = [3, 7, 10, 15, 17]
CYM = [4, 8, 9, 16, 18]
ZCOLS = [(5, 0), (11, 0), (14, 0), (15, 0), (18, 0), (6, -1), (12, -1), (13, -1), (16, -1), (17, -1)]
ZFACE_COL = {5: 0, 11: 8, 14: 16, 15: 24, 18: 32, 6: 0, 12: 8, 13: 16, 16: 24, 17: 32}
XZ_EDGE = {11: (40, 0), 14: (48, -16), 12: (40, -16), 13: (48, 0)}
YZ_CORNER = {15: (56, 0), 18: (64, -1), 16: (56, -1), 17: (64, 0)}
XY_EDGE = {7: (0, 0), 8: (1, 7), 9: (2, 7), 10: (3, 0)}


def _messages(cx, cy):
    rows = cx * cy
    msgs = []
    for k, pop in enumerate(CXP):
        msgs.append(((-1, 0, 0), ("S", pop, 0, cy), ("XH", 1, k)))
    for k, pop in enumerate(CXM):
        msgs.append(((1, 0, 0), ("S", pop, rows - cy, cy), ("XH", 0, k)))
    msgs.append(((0, -1, 0), ("SY", 0), ("YH", 1)))
    msgs.append(((0, 1, 0), ("SY", 1), ("YH", 0)))
    msgs.append(((-1, -1, 0), ("S", 7, 0, 8), ("EXY", 0)))
    msgs.append(((1, 1, 0), ("S", 8, rows - 8, 8), ("EXY", 1)))
    msgs.append(((-1, 1, 0), ("S", 9, cy - 8, 8), ("EXY", 2)))
    msgs.append(((1, -1, 0), ("S", 10, rows - cy, 8), ("EXY", 3)))
    msgs.append(((0, 0, -1), ("NT", 0, 40), ("MH", 1, 0, 40)))
    msgs.append(((0, 0, 1), ("NT", 40, 40), ("MH", 0, 0, 40)))
    msgs.append(((-1, 0, -1), ("NT", 8, 8), ("MH", 1, 40, 8)))
    msgs.append(((1, 0, -1), ("NT", 16, 8), ("MH", 1, 48, 8)))
    msgs.append(((1, 0, 1), ("NT", 48, 8), ("MH", 0, 40, 8)))
    msgs.append(((-1, 0, 1), ("NT", 56, 8), ("MH", 0, 48, 8)))
    msgs.append(((0, -1, -1), ("NT", 24, 8), ("MH", 1, 56, 8)))
    msgs.append(((0, 1, -1), ("NT", 32, 8), ("MH", 1, 64, 8)))
    msgs.append(((0, 1, 1), ("NT", 64, 8), ("MH", 0, 56, 8)))
    msgs.append(((0, -1, 1), ("NT", 72, 8), ("MH", 0, 64, 8)))
    return msgs


NEIGHBOURS = sorted(
    {d for d, _, _ in _messages(8, 16)} | {tuple(-v for v in d) for d, _, _ in _messages(8, 16)}
)


def _comb(vals, fn):
    total = None
    for weight in (1.0 / 3.0, 1.0 / 18.0, 1.0 / 36.0):
        part = None
        for i in range(19):
            if WEIGHTS[i] != weight:
                continue
            k = fn(VELOCITIES[i])
            if k == 0:
                continue
            if part is None:
                part = vals[i] if k > 0 else -vals[i]
            else:
                part = part + vals[i] if k > 0 else part - vals[i]
        if part is not None:
            term = part * weight
            total = term if total is None else total + term
    return total


def _collide(pulled, rho, ux, uy, uz, fluid):
    p0 = _comb(pulled, lambda c: 1)
    p1 = [_comb(pulled, lambda c, a=a: c[a]) for a in range(3)]
    q = {}
    for a in range(3):
        for b in range(a, 3):
            q[a, b] = _comb(pulled, lambda c, a=a, b=b: c[a] * c[b])
            q[b, a] = q[a, b]
    u = (ux, uy, uz)
    usq = ux * ux + uy * uy + uz * uz
    qu = [q[a, 0] * ux + q[a, 1] * uy + q[a, 2] * uz for a in range(3)]
    p1u = p1[0] * ux + p1[1] * uy + p1[2] * uz
    uqu = ux * qu[0] + uy * qu[1] + uz * qu[2]
    moment = p0 * (1.0 - 1.5 * usq) + 3.0 * p1u + 4.5 * uqu
    vec = [3.0 * p1[a] + 9.0 * qu[a] - 3.0 * u[a] * p0 for a in range(3)]
    vu = vec[0] * ux + vec[1] * uy + vec[2] * uz
    inv = 1.0 / rho
    base = OMEGA * (moment - vu) - ux * inv
    bases = {0: base, 1: base + inv, -1: base - inv}
    wv = [OMEGA * v for v in vec]
    combos = {}
    layers = []
    for i in range(19):
        c = VELOCITIES[i]
        key = tuple(c)
        terms = [(a, c[a]) for a in range(3) if c[a] != 0]
        cv = None
        if terms:
            if len(terms) == 1:
                a, s = terms[0]
                cv = wv[a] if s > 0 else -wv[a]
            else:
                (a, s), (b, t) = terms
                pos = (a, b, s * t)
                if pos not in combos:
                    combos[pos] = wv[a] + wv[b] if s * t > 0 else wv[a] - wv[b]
                cv = combos[pos] if s > 0 else -combos[pos]
        val = (1.0 - OMEGA) * pulled[i] + bases[c[0]]
        if cv is not None:
            val = val + cv
        layers.append(jnp.where(fluid, val, pulled[OPPOSITE[i]]))
    sens = None
    for i in range(1, 19, 2):
        c = VELOCITIES[i]
        along = None
        for a in range(3):
            if c[a] == 0:
                continue
            if along is None:
                along = u[a] if c[a] > 0 else -u[a]
            else:
                along = along + u[a] if c[a] > 0 else along - u[a]
        term = (6.0 * WEIGHTS[i]) * along * (pulled[OPPOSITE[i]] - pulled[i])
        sens = term if sens is None else sens + term
    sens = jnp.where(fluid, rho * sens, 0.0)
    return layers, sens


def _kernel(dims, adj_hbm, rho_hbm, vel_hbm, mask_hbm, out_ref, sens_ref,
            adj_ref, rho_ref, vel_ref, mask_ref, load_sem,
            mid, xh, yh, exy, sy, nt, mh, mt, send_sem, recv_sem):
    nx, ny, nz = dims
    cx, cy, cz = 8, 16, 128
    rows = cx * cy
    me = (lax.axis_index("gx"), lax.axis_index("gy"), lax.axis_index("gz"))
    sizes = (nx, ny, nz)

    def exists(d):
        cond = None
        for a in range(3):
            if d[a] == 0:
                continue
            v = me[a] + d[a]
            c = (v >= 0) if d[a] < 0 else (v < sizes[a])
            cond = c if cond is None else jnp.logical_and(cond, c)
        return cond

    def target(d):
        return tuple(me[a] + d[a] for a in range(3))

    loads = [
        pltpu.make_async_copy(src, dst, load_sem.at[k])
        for k, (src, dst) in enumerate(
            ((adj_hbm, adj_ref), (vel_hbm, vel_ref), (rho_hbm, rho_ref), (mask_hbm, mask_ref))
        )
    ]
    for copy in loads:
        copy.start()

    xh[...] = jnp.zeros(xh.shape, jnp.float32)
    yh[...] = jnp.zeros(yh.shape, jnp.float32)
    exy[...] = jnp.zeros(exy.shape, jnp.float32)
    mh[...] = jnp.zeros(mh.shape, jnp.float32)

    barrier = pltpu.get_barrier_semaphore()
    for d in NEIGHBOURS:
        @pl.when(exists(d))
        def _():
            pl.semaphore_signal(barrier, inc=1, device_id=target(d), device_id_type=MESH)

    lane = lax.broadcasted_iota(jnp.int32, (cy, cz), 1)
    lane1 = lax.broadcasted_iota(jnp.int32, (1, cz), 1)
    row = lax.broadcasted_iota(jnp.int32, (cy, cz), 0)
    lane_big = lax.broadcasted_iota(jnp.int32, (rows, cz), 1)

    msgs = _messages(cx, cy)

    def prepare(s, src):
        for side, pops, y in ((0, CYP, 0), (1, CYM, cy - 1)):
            for k, pop in enumerate(pops):
                sy[s, side, k] = src[pop, pl.ds(y, cx, stride=cy), :]
        n = jnp.zeros((rows, cz), jnp.float32)
        for j, (pop, z) in enumerate(ZCOLS):
            zz = z % cz
            n = jnp.where(lane_big == 8 * j, pltpu.roll(src[pop], (8 * j - zz) % cz, 1), n)
        nt[s] = n.T

    def descriptor(s, src, m, t):
        d, so, de = msgs[t]
        if so[0] == "S":
            sref = src.at[so[1], pl.ds(so[2] % rows, so[3]), :]
        elif so[0] == "SY":
            sref = sy.at[s, so[1]]
        else:
            sref = nt.at[s, pl.ds(so[1], so[2]), :]
        if de[0] == "XH":
            dref = xh.at[s, de[1], de[2]]
        elif de[0] == "YH":
            dref = yh.at[s, de[1]]
        elif de[0] == "EXY":
            dref = exy.at[s, de[1]]
        else:
            dref = mh.at[s, de[1], pl.ds(de[2], de[3]), :]
        return pltpu.make_async_remote_copy(
            src_ref=sref, dst_ref=dref, send_sem=send_sem.at[s, t], recv_sem=recv_sem.at[s, t],
            device_id=target(d), device_id_type=MESH)

    def send(s, src):
        for t in range(len(msgs)):
            d = msgs[t][0]

            @pl.when(exists(d))
            def _():
                descriptor(s, src, msgs, t).start()

    def finish(s, src):
        for t in range(len(msgs)):
            d = msgs[t][0]
            back = tuple(-v for v in d)

            @pl.when(exists(back))
            def _():
                descriptor(s, src, msgs, t).wait_recv()

            @pl.when(exists(d))
            def _():
                descriptor(s, src, msgs, t).wait_send()
        for side in range(2):
            mt[s, side] = mh[s, side].T

    def pulled_plane(s, src, p):
        out = []
        for i in range(19):
            vx, vy, vz = VELOCITIES[i]
            q = p + vx
            if 0 <= q < cx:
                plane = src[i, pl.ds(q * cy, cy), :]
            elif q == cx:
                plane = xh[s, 1, CXP.index(i)]
            else:
                plane = xh[s, 0, CXM.index(i)]
            if vz != 0:
                side = 1 if vz > 0 else 0
                if 0 <= q < cx:
                    zc = mt[s, side, pl.ds(q * cy, cy), :]
                    col = ZFACE_COL[i]
                else:
                    col, r0 = XZ_EDGE[i]
                    zc = mt[s, side, pl.ds(r0 % rows, cy), :]
                if vz > 0:
                    plane = jnp.where(lane == cz - 1, pltpu.roll(zc, (cz - 1 - col) % cz, 1),
                                      pltpu.roll(plane, cz - 1, 1))
                else:
                    plane = jnp.where(lane == 0, pltpu.roll(zc, (cz - col) % cz, 1),
                                      pltpu.roll(plane, 1, 1))
            if vy != 0:
                side_y = 1 if vy > 0 else 0
                ky = CYP.index(i) if vy > 0 else CYM.index(i)
                if 0 <= q < cx:
                    yrow = yh[s, side_y, ky, pl.ds(q, 1), :]
                else:
                    e, r = XY_EDGE[i]
                    yrow = exy[s, e, pl.ds(r, 1), :]
                if vz != 0:
                    side = 1 if vz > 0 else 0
                    colc, yoff = YZ_CORNER[i]
                    crow = mt[s, side, pl.ds(p * cy + yoff % cy, 1), :]
                    if vz > 0:
                        yrow = jnp.where(lane1 == cz - 1, pltpu.roll(crow, (cz - 1 - colc) % cz, 1),
                                         pltpu.roll(yrow, cz - 1, 1))
                    else:
                        yrow = jnp.where(lane1 == 0, pltpu.roll(crow, (cz - colc) % cz, 1),
                                         pltpu.roll(yrow, 1, 1))
                if vy > 0:
                    plane = jnp.where(row == cy - 1, yrow, pltpu.roll(plane, cy - 1, 0))
                else:
                    plane = jnp.where(row == 0, yrow, pltpu.roll(plane, 1, 0))
            out.append(plane)
        return out

    def step(s, src, dst, level):
        for p in range(cx):
            rs = pl.ds(p * cy, cy)
            pulled = pulled_plane(s, src, p)
            rho = rho_ref[level, rs, :]
            ux = vel_ref[level, 0, rs, :]
            uy = vel_ref[level, 1, rs, :]
            uz = vel_ref[level, 2, rs, :]
            fluid = mask_ref[rs, :] > 0
            layers, sens = _collide(pulled, rho, ux, uy, uz, fluid)
            for i in range(19):
                dst[i, rs, :] = layers[i]
            if s == 0:
                sens_ref[rs, :] = sens
            else:
                sens_ref[rs, :] = sens_ref[rs, :] + sens

    def indicator(a, off):
        n = sizes[a]
        if off < 0:
            return (me[a] + n - 1) // n
        if off > 0:
            return (2 * n - 2 - me[a]) // n
        return 1

    peers = 0
    for d in NEIGHBOURS:
        term = 1
        for a in range(3):
            term = term * indicator(a, d[a])
        peers = peers + term
    loads[0].wait()
    prepare(0, adj_ref)
    pl.semaphore_wait(barrier, peers)
    send(0, adj_ref)
    for copy in loads[1:]:
        copy.wait()
    finish(0, adj_ref)
    step(0, adj_ref, mid, 1)
    prepare(1, mid)
    send(1, mid)
    finish(1, mid)
    step(1, mid, out_ref, 0)


def solution(mesh):
    nx, ny, nz = mesh.shape["gx"], mesh.shape["gy"], mesh.shape["gz"]
    nmsg = len(_messages(8, 16))

    def shards(adjoint, density, velocity, pore_mask):
        npop, cx, cy, cz = adjoint.shape
        assert (cx, cy, cz) == (8, 16, 128)
        rows = cx * cy
        adj = adjoint.reshape(npop, rows, cz)
        rho = density.reshape(2, rows, cz)
        vel = velocity.reshape(2, 3, rows, cz)
        mask = pore_mask.reshape(rows, cz)
        vspec = pl.BlockSpec(memory_space=pltpu.VMEM)
        out, sens = pl.pallas_call(
            functools.partial(_kernel, (nx, ny, nz)),
            out_shape=(
                jax.ShapeDtypeStruct((npop, rows, cz), jnp.float32),
                jax.ShapeDtypeStruct((rows, cz), jnp.float32),
            ),
            in_specs=[pl.BlockSpec(memory_space=pltpu.HBM)] * 4,
            out_specs=(vspec, vspec),
            scratch_shapes=[
                pltpu.VMEM((npop, rows, cz), jnp.float32),
                pltpu.VMEM((2, rows, cz), jnp.float32),
                pltpu.VMEM((2, 3, rows, cz), jnp.float32),
                pltpu.VMEM((rows, cz), jnp.int32),
                pltpu.SemaphoreType.DMA((4,)),
                pltpu.VMEM((npop, rows, cz), jnp.float32),
                pltpu.VMEM((2, 2, 5, cy, cz), jnp.float32),
                pltpu.VMEM((2, 2, 5, cx, cz), jnp.float32),
                pltpu.VMEM((2, 4, 8, cz), jnp.float32),
                pltpu.VMEM((2, 2, 5, cx, cz), jnp.float32),
                pltpu.VMEM((2, rows, cz), jnp.float32),
                pltpu.VMEM((2, 2, rows, cz), jnp.float32),
                pltpu.VMEM((2, 2, rows, cz), jnp.float32),
                pltpu.SemaphoreType.DMA((2, nmsg)),
                pltpu.SemaphoreType.DMA((2, nmsg)),
            ],
            compiler_params=pltpu.CompilerParams(
                collective_id=0, has_side_effects=True, vmem_limit_bytes=67043328
            ),
        )(adj, rho, vel, mask)
        return out.reshape(npop, cx, cy, cz), sens.reshape(cx, cy, cz)

    placed = (
        P(None, "gx", "gy", "gz"),
        P(None, "gx", "gy", "gz"),
        P(None, None, "gx", "gy", "gz"),
        P("gx", "gy", "gz"),
    )
    return jax.shard_map(
        shards,
        mesh=mesh,
        in_specs=placed,
        out_specs=(P(None, "gx", "gy", "gz"), P("gx", "gy", "gz")),
        check_vma=False,
    )
```

```python
import functools

import jax
import jax.numpy as jnp
from jax import lax
from jax.experimental import pallas as pl
from jax.experimental.pallas import tpu as pltpu
from jax.sharding import PartitionSpec as P

VELOCITIES = [
    (0, 0, 0),
    (1, 0, 0),
    (-1, 0, 0),
    (0, 1, 0),
    (0, -1, 0),
    (0, 0, 1),
    (0, 0, -1),
    (1, 1, 0),
    (-1, -1, 0),
    (1, -1, 0),
    (-1, 1, 0),
    (1, 0, 1),
    (-1, 0, -1),
    (1, 0, -1),
    (-1, 0, 1),
    (0, 1, 1),
    (0, -1, -1),
    (0, 1, -1),
    (0, -1, 1),
]
WEIGHTS = [1.0 / 3.0] + [1.0 / 18.0] * 6 + [1.0 / 36.0] * 12
OPPOSITE = [0, 2, 1, 4, 3, 6, 5, 8, 7, 10, 9, 12, 11, 14, 13, 16, 15, 18, 17]
OMEGA = 1.25
MESH = pl.DeviceIdType.MESH

CXP = [1, 7, 9, 11, 13]
CXM = [2, 8, 10, 12, 14]
CYP = [3, 7, 10, 15, 17]
CYM = [4, 8, 9, 16, 18]
ZCOLS = [(5, 0), (11, 0), (14, 0), (15, 0), (18, 0), (6, -1), (12, -1), (13, -1), (16, -1), (17, -1)]
ZFACE_COL = {5: 0, 11: 8, 14: 16, 15: 24, 18: 32, 6: 0, 12: 8, 13: 16, 16: 24, 17: 32}
XZ_EDGE = {11: (40, 0), 14: (48, -16), 12: (40, -16), 13: (48, 0)}
YZ_CORNER = {15: (56, 0), 18: (64, -1), 16: (56, -1), 17: (64, 0)}
XY_EDGE = {7: (0, 0), 8: (1, 7), 9: (2, 7), 10: (3, 0)}


def _messages(cx, cy):
    rows = cx * cy
    msgs = []
    for k, pop in enumerate(CXP):
        msgs.append(((-1, 0, 0), ("S", pop, 0, cy), ("XH", 1, k)))
    for k, pop in enumerate(CXM):
        msgs.append(((1, 0, 0), ("S", pop, rows - cy, cy), ("XH", 0, k)))
    msgs.append(((0, -1, 0), ("SY", 0), ("YH", 1)))
    msgs.append(((0, 1, 0), ("SY", 1), ("YH", 0)))
    msgs.append(((-1, -1, 0), ("S", 7, 0, 8), ("EXY", 0)))
    msgs.append(((1, 1, 0), ("S", 8, rows - 8, 8), ("EXY", 1)))
    msgs.append(((-1, 1, 0), ("S", 9, cy - 8, 8), ("EXY", 2)))
    msgs.append(((1, -1, 0), ("S", 10, rows - cy, 8), ("EXY", 3)))
    msgs.append(((0, 0, -1), ("NT", 0, 40), ("MH", 1, 0, 40)))
    msgs.append(((0, 0, 1), ("NT", 40, 40), ("MH", 0, 0, 40)))
    msgs.append(((-1, 0, -1), ("NT", 8, 8), ("MH", 1, 40, 8)))
    msgs.append(((1, 0, -1), ("NT", 16, 8), ("MH", 1, 48, 8)))
    msgs.append(((1, 0, 1), ("NT", 48, 8), ("MH", 0, 40, 8)))
    msgs.append(((-1, 0, 1), ("NT", 56, 8), ("MH", 0, 48, 8)))
    msgs.append(((0, -1, -1), ("NT", 24, 8), ("MH", 1, 56, 8)))
    msgs.append(((0, 1, -1), ("NT", 32, 8), ("MH", 1, 64, 8)))
    msgs.append(((0, 1, 1), ("NT", 64, 8), ("MH", 0, 56, 8)))
    msgs.append(((0, -1, 1), ("NT", 72, 8), ("MH", 0, 64, 8)))
    return msgs


NEIGHBOURS = sorted(
    {d for d, _, _ in _messages(8, 16)} | {tuple(-v for v in d) for d, _, _ in _messages(8, 16)}
)


def _comb(vals, fn):
    total = None
    for weight in (1.0 / 3.0, 1.0 / 18.0, 1.0 / 36.0):
        part = None
        for i in range(19):
            if WEIGHTS[i] != weight:
                continue
            k = fn(VELOCITIES[i])
            if k == 0:
                continue
            if part is None:
                part = vals[i] if k > 0 else -vals[i]
            else:
                part = part + vals[i] if k > 0 else part - vals[i]
        if part is not None:
            term = part * weight
            total = term if total is None else total + term
    return total


def _collide(pulled, rho, ux, uy, uz, fluid, with_rho=True):
    p0 = _comb(pulled, lambda c: 1)
    p1 = [_comb(pulled, lambda c, a=a: c[a]) for a in range(3)]
    q = {}
    for a in range(3):
        for b in range(a, 3):
            q[a, b] = _comb(pulled, lambda c, a=a, b=b: c[a] * c[b])
            q[b, a] = q[a, b]
    u = (ux, uy, uz)
    usq = ux * ux + uy * uy + uz * uz
    qu = [q[a, 0] * ux + q[a, 1] * uy + q[a, 2] * uz for a in range(3)]
    p1u = p1[0] * ux + p1[1] * uy + p1[2] * uz
    uqu = ux * qu[0] + uy * qu[1] + uz * qu[2]
    moment = p0 * (1.0 - 1.5 * usq) + 3.0 * p1u + 4.5 * uqu
    vec = [3.0 * p1[a] + 9.0 * qu[a] - 3.0 * u[a] * p0 for a in range(3)]
    vu = vec[0] * ux + vec[1] * uy + vec[2] * uz
    if with_rho:
        inv = 1.0 / rho
        base = OMEGA * (moment - vu) - ux * inv
        bases = {0: base, 1: base + inv, -1: base - inv}
    else:
        base = OMEGA * (moment - vu)
        bases = {0: base, 1: base, -1: base}
    wv = [OMEGA * v for v in vec]
    combos = {}
    layers = []
    for i in range(19):
        c = VELOCITIES[i]
        key = tuple(c)
        terms = [(a, c[a]) for a in range(3) if c[a] != 0]
        cv = None
        if terms:
            if len(terms) == 1:
                a, s = terms[0]
                cv = wv[a] if s > 0 else -wv[a]
            else:
                (a, s), (b, t) = terms
                pos = (a, b, s * t)
                if pos not in combos:
                    combos[pos] = wv[a] + wv[b] if s * t > 0 else wv[a] - wv[b]
                cv = combos[pos] if s > 0 else -combos[pos]
        val = (1.0 - OMEGA) * pulled[i] + bases[c[0]]
        if cv is not None:
            val = val + cv
        layers.append(jnp.where(fluid, val, pulled[OPPOSITE[i]]))
    sens = None
    for i in range(1, 19, 2):
        c = VELOCITIES[i]
        along = None
        for a in range(3):
            if c[a] == 0:
                continue
            if along is None:
                along = u[a] if c[a] > 0 else -u[a]
            else:
                along = along + u[a] if c[a] > 0 else along - u[a]
        term = (6.0 * WEIGHTS[i]) * along * (pulled[OPPOSITE[i]] - pulled[i])
        sens = term if sens is None else sens + term
    sens = jnp.where(fluid, rho * sens, 0.0)
    return layers, sens


def _kernel(dims, adj_hbm, rho_hbm, vel_hbm, mask_hbm, out_ref, sens_ref, sens2_ref,
            adj_ref, rho_ref, vel_ref, mask_ref, load_sem,
            mid, xh, yh, exy, sy, nt, mh, mt, send_sem, recv_sem):
    nx, ny, nz = dims
    cx, cy, cz = 8, 16, 128
    rows = cx * cy
    me = (lax.axis_index("gx"), lax.axis_index("gy"), lax.axis_index("gz"))
    sizes = (nx, ny, nz)

    def exists(d):
        cond = None
        for a in range(3):
            if d[a] == 0:
                continue
            v = me[a] + d[a]
            c = (v >= 0) if d[a] < 0 else (v < sizes[a])
            cond = c if cond is None else jnp.logical_and(cond, c)
        return cond

    def target(d):
        return tuple(me[a] + d[a] for a in range(3))

    loads = [
        pltpu.make_async_copy(src, dst, load_sem.at[k])
        for k, (src, dst) in enumerate(
            ((adj_hbm, adj_ref), (vel_hbm, vel_ref), (rho_hbm, rho_ref), (mask_hbm, mask_ref))
        )
    ]
    for copy in loads:
        copy.start()

    xh[...] = jnp.zeros(xh.shape, jnp.float32)
    yh[...] = jnp.zeros(yh.shape, jnp.float32)
    exy[...] = jnp.zeros(exy.shape, jnp.float32)
    mh[...] = jnp.zeros(mh.shape, jnp.float32)

    barrier = pltpu.get_barrier_semaphore()
    for d in NEIGHBOURS:
        @pl.when(exists(d))
        def _():
            pl.semaphore_signal(barrier, inc=1, device_id=target(d), device_id_type=MESH)

    lane = lax.broadcasted_iota(jnp.int32, (cy, cz), 1)
    lane1 = lax.broadcasted_iota(jnp.int32, (1, cz), 1)
    row = lax.broadcasted_iota(jnp.int32, (cy, cz), 0)
    lane_big = lax.broadcasted_iota(jnp.int32, (rows, cz), 1)

    msgs = _messages(cx, cy)

    def prepare(s, src):
        for side, pops, y in ((0, CYP, 0), (1, CYM, cy - 1)):
            for k, pop in enumerate(pops):
                sy[s, side, k] = src[pop, pl.ds(y, cx, stride=cy), :]
        n = jnp.zeros((rows, cz), jnp.float32)
        for j, (pop, z) in enumerate(ZCOLS):
            zz = z % cz
            n = jnp.where(lane_big == 8 * j, pltpu.roll(src[pop], (8 * j - zz) % cz, 1), n)
        nt[s] = n.T

    def descriptor(s, src, m, t):
        d, so, de = msgs[t]
        if so[0] == "S":
            sref = src.at[so[1], pl.ds(so[2] % rows, so[3]), :]
        elif so[0] == "SY":
            sref = sy.at[s, so[1]]
        else:
            sref = nt.at[s, pl.ds(so[1], so[2]), :]
        if de[0] == "XH":
            dref = xh.at[s, de[1], de[2]]
        elif de[0] == "YH":
            dref = yh.at[s, de[1]]
        elif de[0] == "EXY":
            dref = exy.at[s, de[1]]
        else:
            dref = mh.at[s, de[1], pl.ds(de[2], de[3]), :]
        return pltpu.make_async_remote_copy(
            src_ref=sref, dst_ref=dref, send_sem=send_sem.at[s, t], recv_sem=recv_sem.at[s, t],
            device_id=target(d), device_id_type=MESH)

    def send(s, src):
        for t in range(len(msgs)):
            d = msgs[t][0]

            @pl.when(exists(d))
            def _():
                descriptor(s, src, msgs, t).start()

    def finish(s, src):
        for t in range(len(msgs)):
            d = msgs[t][0]
            back = tuple(-v for v in d)

            @pl.when(exists(back))
            def _():
                descriptor(s, src, msgs, t).wait_recv()

            @pl.when(exists(d))
            def _():
                descriptor(s, src, msgs, t).wait_send()
        for side in range(2):
            mt[s, side] = mh[s, side].T

    def pulled_plane(s, src, p):
        out = []
        for i in range(19):
            vx, vy, vz = VELOCITIES[i]
            q = p + vx
            if 0 <= q < cx:
                plane = src[i, pl.ds(q * cy, cy), :]
            elif q == cx:
                plane = xh[s, 1, CXP.index(i)]
            else:
                plane = xh[s, 0, CXM.index(i)]
            if vz != 0:
                side = 1 if vz > 0 else 0
                if 0 <= q < cx:
                    zc = mt[s, side, pl.ds(q * cy, cy), :]
                    col = ZFACE_COL[i]
                else:
                    col, r0 = XZ_EDGE[i]
                    zc = mt[s, side, pl.ds(r0 % rows, cy), :]
                if vz > 0:
                    plane = jnp.where(lane == cz - 1, pltpu.roll(zc, (cz - 1 - col) % cz, 1),
                                      pltpu.roll(plane, cz - 1, 1))
                else:
                    plane = jnp.where(lane == 0, pltpu.roll(zc, (cz - col) % cz, 1),
                                      pltpu.roll(plane, 1, 1))
            if vy != 0:
                side_y = 1 if vy > 0 else 0
                ky = CYP.index(i) if vy > 0 else CYM.index(i)
                if 0 <= q < cx:
                    yrow = yh[s, side_y, ky, pl.ds(q, 1), :]
                else:
                    e, r = XY_EDGE[i]
                    yrow = exy[s, e, pl.ds(r, 1), :]
                if vz != 0:
                    side = 1 if vz > 0 else 0
                    colc, yoff = YZ_CORNER[i]
                    crow = mt[s, side, pl.ds(p * cy + yoff % cy, 1), :]
                    if vz > 0:
                        yrow = jnp.where(lane1 == cz - 1, pltpu.roll(crow, (cz - 1 - colc) % cz, 1),
                                         pltpu.roll(yrow, cz - 1, 1))
                    else:
                        yrow = jnp.where(lane1 == 0, pltpu.roll(crow, (cz - colc) % cz, 1),
                                         pltpu.roll(yrow, 1, 1))
                if vy > 0:
                    plane = jnp.where(row == cy - 1, yrow, pltpu.roll(plane, cy - 1, 0))
                else:
                    plane = jnp.where(row == 0, yrow, pltpu.roll(plane, 1, 0))
            out.append(plane)
        return out

    def step(s, src, dst, level):
        for p in range(cx):
            rs = pl.ds(p * cy, cy)
            pulled = pulled_plane(s, src, p)
            rho = rho_ref[level, rs, :]
            ux = vel_ref[level, 0, rs, :]
            uy = vel_ref[level, 1, rs, :]
            uz = vel_ref[level, 2, rs, :]
            fluid = mask_ref[rs, :] > 0
            layers, sens = _collide(pulled, rho, ux, uy, uz, fluid, with_rho=(s == 0))
            for i in range(19):
                dst[i, rs, :] = layers[i]
            if s == 0:
                sens_ref[rs, :] = sens
            else:
                sens2_ref[rs, :] = sens

    def indicator(a, off):
        n = sizes[a]
        if off < 0:
            return (me[a] + n - 1) // n
        if off > 0:
            return (2 * n - 2 - me[a]) // n
        return 1

    peers = 0
    for d in NEIGHBOURS:
        term = 1
        for a in range(3):
            term = term * indicator(a, d[a])
        peers = peers + term
    loads[0].wait()
    prepare(0, adj_ref)
    pl.semaphore_wait(barrier, peers)
    send(0, adj_ref)
    for copy in loads[1:]:
        copy.wait()
    finish(0, adj_ref)
    step(0, adj_ref, mid, 1)
    prepare(1, mid)
    send(1, mid)
    finish(1, mid)
    step(1, mid, out_ref, 0)


def solution(mesh):
    nx, ny, nz = mesh.shape["gx"], mesh.shape["gy"], mesh.shape["gz"]
    nmsg = len(_messages(8, 16))

    def shards(adjoint, density, velocity, pore_mask):
        npop, cx, cy, cz = adjoint.shape
        assert (cx, cy, cz) == (8, 16, 128)
        rows = cx * cy
        adj = adjoint.reshape(npop, rows, cz)
        rho = density.reshape(2, rows, cz)
        vel = velocity.reshape(2, 3, rows, cz)
        mask = pore_mask.reshape(rows, cz)
        vspec = pl.BlockSpec(memory_space=pltpu.VMEM)
        part, sens1, sens2 = pl.pallas_call(
            functools.partial(_kernel, (nx, ny, nz)),
            out_shape=(
                jax.ShapeDtypeStruct((npop, rows, cz), jnp.float32),
                jax.ShapeDtypeStruct((rows, cz), jnp.float32),
                jax.ShapeDtypeStruct((rows, cz), jnp.float32),
            ),
            in_specs=[pl.BlockSpec(memory_space=pltpu.HBM)] * 4,
            out_specs=(vspec, vspec, vspec),
            scratch_shapes=[
                pltpu.VMEM((npop, rows, cz), jnp.float32),
                pltpu.VMEM((2, rows, cz), jnp.float32),
                pltpu.VMEM((2, 3, rows, cz), jnp.float32),
                pltpu.VMEM((rows, cz), jnp.int32),
                pltpu.SemaphoreType.DMA((4,)),
                pltpu.VMEM((npop, rows, cz), jnp.float32),
                pltpu.VMEM((2, 2, 5, cy, cz), jnp.float32),
                pltpu.VMEM((2, 2, 5, cx, cz), jnp.float32),
                pltpu.VMEM((2, 4, 8, cz), jnp.float32),
                pltpu.VMEM((2, 2, 5, cx, cz), jnp.float32),
                pltpu.VMEM((2, rows, cz), jnp.float32),
                pltpu.VMEM((2, 2, rows, cz), jnp.float32),
                pltpu.VMEM((2, 2, rows, cz), jnp.float32),
                pltpu.SemaphoreType.DMA((2, nmsg)),
                pltpu.SemaphoreType.DMA((2, nmsg)),
            ],
            compiler_params=pltpu.CompilerParams(
                collective_id=0, has_side_effects=True, vmem_limit_bytes=67043328
            ),
        )(adj, rho, vel, mask)
        part = part.reshape(npop, cx, cy, cz)
        speed_x = jnp.array([c[0] for c in VELOCITIES], jnp.float32).reshape(npop, 1, 1, 1)
        drive = (speed_x - velocity[0, 0][None]) / density[0][None]
        out = jnp.where(pore_mask[None] > 0, part + drive, part)
        return out, (sens1 + sens2).reshape(cx, cy, cz)

    placed = (
        P(None, "gx", "gy", "gz"),
        P(None, "gx", "gy", "gz"),
        P(None, None, "gx", "gy", "gz"),
        P("gx", "gy", "gz"),
    )
    return jax.shard_map(
        shards,
        mesh=mesh,
        in_specs=placed,
        out_specs=(P(None, "gx", "gy", "gz"), P("gx", "gy", "gz")),
        check_vma=False,
    )
```

```python
import functools

import jax
import jax.numpy as jnp
from jax import lax
from jax.experimental import pallas as pl
from jax.experimental.pallas import tpu as pltpu
from jax.sharding import PartitionSpec as P

VELOCITIES = [
    (0, 0, 0),
    (1, 0, 0),
    (-1, 0, 0),
    (0, 1, 0),
    (0, -1, 0),
    (0, 0, 1),
    (0, 0, -1),
    (1, 1, 0),
    (-1, -1, 0),
    (1, -1, 0),
    (-1, 1, 0),
    (1, 0, 1),
    (-1, 0, -1),
    (1, 0, -1),
    (-1, 0, 1),
    (0, 1, 1),
    (0, -1, -1),
    (0, 1, -1),
    (0, -1, 1),
]
WEIGHTS = [1.0 / 3.0] + [1.0 / 18.0] * 6 + [1.0 / 36.0] * 12
OPPOSITE = [0, 2, 1, 4, 3, 6, 5, 8, 7, 10, 9, 12, 11, 14, 13, 16, 15, 18, 17]
OMEGA = 1.25
MESH = pl.DeviceIdType.MESH

CXP = [1, 7, 9, 11, 13]
CXM = [2, 8, 10, 12, 14]
CYP = [3, 7, 10, 15, 17]
CYM = [4, 8, 9, 16, 18]
ZCOLS = [(5, 0), (11, 0), (14, 0), (15, 0), (18, 0), (6, -1), (12, -1), (13, -1), (16, -1), (17, -1)]
ZFACE_COL = {5: 0, 11: 8, 14: 16, 15: 24, 18: 32, 6: 0, 12: 8, 13: 16, 16: 24, 17: 32}
XZ_EDGE = {11: (40, 0), 14: (48, -16), 12: (40, -16), 13: (48, 0)}
YZ_CORNER = {15: (56, 0), 18: (64, -1), 16: (56, -1), 17: (64, 0)}
XY_EDGE = {7: (0, 0), 8: (1, 7), 9: (2, 7), 10: (3, 0)}


def _messages(cx, cy):
    rows = cx * cy
    msgs = []
    for k, pop in enumerate(CXP):
        msgs.append(((-1, 0, 0), ("S", pop, 0, cy), ("XH", 1, k)))
    for k, pop in enumerate(CXM):
        msgs.append(((1, 0, 0), ("S", pop, rows - cy, cy), ("XH", 0, k)))
    msgs.append(((0, -1, 0), ("SY", 0), ("YH", 1)))
    msgs.append(((0, 1, 0), ("SY", 1), ("YH", 0)))
    msgs.append(((-1, -1, 0), ("S", 7, 0, 8), ("EXY", 0)))
    msgs.append(((1, 1, 0), ("S", 8, rows - 8, 8), ("EXY", 1)))
    msgs.append(((-1, 1, 0), ("S", 9, cy - 8, 8), ("EXY", 2)))
    msgs.append(((1, -1, 0), ("S", 10, rows - cy, 8), ("EXY", 3)))
    msgs.append(((0, 0, -1), ("NT", 0, 40), ("MH", 1, 0, 40)))
    msgs.append(((0, 0, 1), ("NT", 40, 40), ("MH", 0, 0, 40)))
    msgs.append(((-1, 0, -1), ("NT", 8, 8), ("MH", 1, 40, 8)))
    msgs.append(((1, 0, -1), ("NT", 16, 8), ("MH", 1, 48, 8)))
    msgs.append(((1, 0, 1), ("NT", 48, 8), ("MH", 0, 40, 8)))
    msgs.append(((-1, 0, 1), ("NT", 56, 8), ("MH", 0, 48, 8)))
    msgs.append(((0, -1, -1), ("NT", 24, 8), ("MH", 1, 56, 8)))
    msgs.append(((0, 1, -1), ("NT", 32, 8), ("MH", 1, 64, 8)))
    msgs.append(((0, 1, 1), ("NT", 64, 8), ("MH", 0, 56, 8)))
    msgs.append(((0, -1, 1), ("NT", 72, 8), ("MH", 0, 64, 8)))
    return msgs


NEIGHBOURS = sorted(
    {d for d, _, _ in _messages(8, 16)} | {tuple(-v for v in d) for d, _, _ in _messages(8, 16)}
)


def _comb(vals, fn):
    total = None
    for weight in (1.0 / 3.0, 1.0 / 18.0, 1.0 / 36.0):
        part = None
        for i in range(19):
            if WEIGHTS[i] != weight:
                continue
            k = fn(VELOCITIES[i])
            if k == 0:
                continue
            if part is None:
                part = vals[i] if k > 0 else -vals[i]
            else:
                part = part + vals[i] if k > 0 else part - vals[i]
        if part is not None:
            term = part * weight
            total = term if total is None else total + term
    return total


def _collide(pulled, rho, ux, uy, uz, fluid):
    p0 = _comb(pulled, lambda c: 1)
    p1 = [_comb(pulled, lambda c, a=a: c[a]) for a in range(3)]
    q = {}
    for a in range(3):
        for b in range(a, 3):
            q[a, b] = _comb(pulled, lambda c, a=a, b=b: c[a] * c[b])
            q[b, a] = q[a, b]
    u = (ux, uy, uz)
    usq = ux * ux + uy * uy + uz * uz
    qu = [q[a, 0] * ux + q[a, 1] * uy + q[a, 2] * uz for a in range(3)]
    p1u = p1[0] * ux + p1[1] * uy + p1[2] * uz
    uqu = ux * qu[0] + uy * qu[1] + uz * qu[2]
    moment = p0 * (1.0 - 1.5 * usq) + 3.0 * p1u + 4.5 * uqu
    vec = [3.0 * p1[a] + 9.0 * qu[a] - 3.0 * u[a] * p0 for a in range(3)]
    vu = vec[0] * ux + vec[1] * uy + vec[2] * uz
    inv = 1.0 / rho
    base = OMEGA * (moment - vu) - ux * inv
    bases = {0: base, 1: base + inv, -1: base - inv}
    wv = [OMEGA * v for v in vec]
    combos = {}
    layers = []
    for i in range(19):
        c = VELOCITIES[i]
        key = tuple(c)
        terms = [(a, c[a]) for a in range(3) if c[a] != 0]
        cv = None
        if terms:
            if len(terms) == 1:
                a, s = terms[0]
                cv = wv[a] if s > 0 else -wv[a]
            else:
                (a, s), (b, t) = terms
                pos = (a, b, s * t)
                if pos not in combos:
                    combos[pos] = wv[a] + wv[b] if s * t > 0 else wv[a] - wv[b]
                cv = combos[pos] if s > 0 else -combos[pos]
        val = (1.0 - OMEGA) * pulled[i] + bases[c[0]]
        if cv is not None:
            val = val + cv
        layers.append(jnp.where(fluid, val, pulled[OPPOSITE[i]]))
    sens = None
    for i in range(1, 19, 2):
        c = VELOCITIES[i]
        along = None
        for a in range(3):
            if c[a] == 0:
                continue
            if along is None:
                along = u[a] if c[a] > 0 else -u[a]
            else:
                along = along + u[a] if c[a] > 0 else along - u[a]
        term = (6.0 * WEIGHTS[i]) * along * (pulled[OPPOSITE[i]] - pulled[i])
        sens = term if sens is None else sens + term
    sens = jnp.where(fluid, rho * sens, 0.0)
    return layers, sens


def _kernel(dims, adj_hbm, rho_hbm, vel_hbm, mask_hbm, out_ref, sens_ref,
            adj_ref, rho_ref, vel_ref, mask_ref, load_sem,
            mid, xh, yh, exy, sy, nt, mh, mt, send_sem, recv_sem):
    nx, ny, nz = dims
    cx, cy, cz = 8, 16, 128
    rows = cx * cy
    me = (lax.axis_index("gx"), lax.axis_index("gy"), lax.axis_index("gz"))
    sizes = (nx, ny, nz)

    def exists(d):
        cond = None
        for a in range(3):
            if d[a] == 0:
                continue
            v = me[a] + d[a]
            c = (v >= 0) if d[a] < 0 else (v < sizes[a])
            cond = c if cond is None else jnp.logical_and(cond, c)
        return cond

    def target(d):
        return tuple(me[a] + d[a] for a in range(3))

    loads = [
        pltpu.make_async_copy(src, dst, load_sem.at[k])
        for k, (src, dst) in enumerate(
            ((adj_hbm, adj_ref), (vel_hbm, vel_ref), (rho_hbm, rho_ref), (mask_hbm, mask_ref))
        )
    ]
    for copy in loads:
        copy.start()

    xh[...] = jnp.zeros(xh.shape, jnp.float32)
    yh[...] = jnp.zeros(yh.shape, jnp.float32)
    exy[...] = jnp.zeros(exy.shape, jnp.float32)
    mh[...] = jnp.zeros(mh.shape, jnp.float32)

    barrier = pltpu.get_barrier_semaphore()
    for d in NEIGHBOURS:
        @pl.when(exists(d))
        def _():
            pl.semaphore_signal(barrier, inc=1, device_id=target(d), device_id_type=MESH)

    lane = lax.broadcasted_iota(jnp.int32, (cy, cz), 1)
    lane1 = lax.broadcasted_iota(jnp.int32, (1, cz), 1)
    row = lax.broadcasted_iota(jnp.int32, (cy, cz), 0)
    lane_big = lax.broadcasted_iota(jnp.int32, (rows, cz), 1)

    msgs = _messages(cx, cy)

    def prepare(s, src):
        for side, pops, y in ((0, CYP, 0), (1, CYM, cy - 1)):
            for k, pop in enumerate(pops):
                sy[s, side, k] = src[pop, pl.ds(y, cx, stride=cy), :]
        n = jnp.zeros((rows, cz), jnp.float32)
        for j, (pop, z) in enumerate(ZCOLS):
            zz = z % cz
            n = jnp.where(lane_big == 8 * j, pltpu.roll(src[pop], (8 * j - zz) % cz, 1), n)
        nt[s] = n.T

    def descriptor(s, src, m, t):
        d, so, de = msgs[t]
        if so[0] == "S":
            sref = src.at[so[1], pl.ds(so[2] % rows, so[3]), :]
        elif so[0] == "SY":
            sref = sy.at[s, so[1]]
        else:
            sref = nt.at[s, pl.ds(so[1], so[2]), :]
        if de[0] == "XH":
            dref = xh.at[s, de[1], de[2]]
        elif de[0] == "YH":
            dref = yh.at[s, de[1]]
        elif de[0] == "EXY":
            dref = exy.at[s, de[1]]
        else:
            dref = mh.at[s, de[1], pl.ds(de[2], de[3]), :]
        return pltpu.make_async_remote_copy(
            src_ref=sref, dst_ref=dref, send_sem=send_sem.at[s, t], recv_sem=recv_sem.at[s, t],
            device_id=target(d), device_id_type=MESH)

    def send(s, src):
        for t in range(len(msgs)):
            d = msgs[t][0]

            @pl.when(exists(d))
            def _():
                descriptor(s, src, msgs, t).start()

    def finish(s, src):
        for t in range(len(msgs)):
            d = msgs[t][0]
            back = tuple(-v for v in d)

            @pl.when(exists(back))
            def _():
                descriptor(s, src, msgs, t).wait_recv()

            @pl.when(exists(d))
            def _():
                descriptor(s, src, msgs, t).wait_send()
        for side in range(2):
            mt[s, side] = mh[s, side].T

    def pulled_plane(s, src, p):
        out = []
        for i in range(19):
            vx, vy, vz = VELOCITIES[i]
            q = p + vx
            if 0 <= q < cx:
                plane = src[i, pl.ds(q * cy, cy), :]
            elif q == cx:
                plane = xh[s, 1, CXP.index(i)]
            else:
                plane = xh[s, 0, CXM.index(i)]
            if vz != 0:
                side = 1 if vz > 0 else 0
                if 0 <= q < cx:
                    zc = mt[s, side, pl.ds(q * cy, cy), :]
                    col = ZFACE_COL[i]
                else:
                    col, r0 = XZ_EDGE[i]
                    zc = mt[s, side, pl.ds(r0 % rows, cy), :]
                if vz > 0:
                    plane = jnp.where(lane == cz - 1, pltpu.roll(zc, (cz - 1 - col) % cz, 1),
                                      pltpu.roll(plane, cz - 1, 1))
                else:
                    plane = jnp.where(lane == 0, pltpu.roll(zc, (cz - col) % cz, 1),
                                      pltpu.roll(plane, 1, 1))
            if vy != 0:
                side_y = 1 if vy > 0 else 0
                ky = CYP.index(i) if vy > 0 else CYM.index(i)
                if 0 <= q < cx:
                    yrow = yh[s, side_y, ky, pl.ds(q, 1), :]
                else:
                    e, r = XY_EDGE[i]
                    yrow = exy[s, e, pl.ds(r, 1), :]
                if vz != 0:
                    side = 1 if vz > 0 else 0
                    colc, yoff = YZ_CORNER[i]
                    crow = mt[s, side, pl.ds(p * cy + yoff % cy, 1), :]
                    if vz > 0:
                        yrow = jnp.where(lane1 == cz - 1, pltpu.roll(crow, (cz - 1 - colc) % cz, 1),
                                         pltpu.roll(yrow, cz - 1, 1))
                    else:
                        yrow = jnp.where(lane1 == 0, pltpu.roll(crow, (cz - colc) % cz, 1),
                                         pltpu.roll(yrow, 1, 1))
                if vy > 0:
                    plane = jnp.where(row == cy - 1, yrow, pltpu.roll(plane, cy - 1, 0))
                else:
                    plane = jnp.where(row == 0, yrow, pltpu.roll(plane, 1, 0))
            out.append(plane)
        return out

    def step(s, src, dst, level):
        for p in range(cx):
            rs = pl.ds(p * cy, cy)
            pulled = pulled_plane(s, src, p)
            rho = rho_ref[level, rs, :]
            ux = vel_ref[level, 0, rs, :]
            uy = vel_ref[level, 1, rs, :]
            uz = vel_ref[level, 2, rs, :]
            fluid = mask_ref[rs, :] > 0
            layers, sens = _collide(pulled, rho, ux, uy, uz, fluid)
            for i in range(19):
                dst[i, rs, :] = layers[i]
            if s == 0:
                sens_ref[rs, :] = sens
            else:
                sens_ref[rs, :] = sens_ref[rs, :] + sens

    def indicator(a, off):
        n = sizes[a]
        if off < 0:
            return (me[a] + n - 1) // n
        if off > 0:
            return (2 * n - 2 - me[a]) // n
        return 1

    peers = 0
    for d in NEIGHBOURS:
        term = 1
        for a in range(3):
            term = term * indicator(a, d[a])
        peers = peers + term
    loads[0].wait()
    prepare(0, adj_ref)
    pl.semaphore_wait(barrier, peers)
    send(0, adj_ref)
    for copy in loads[1:]:
        copy.wait()
    finish(0, adj_ref)
    step(0, adj_ref, mid, 1)
    prepare(1, mid)
    send(1, mid)
    finish(1, mid)
    step(1, mid, out_ref, 0)


def _writer(chunks, part_hbm, sens_hbm, out_hbm, sens_out, buf, sbuf, sems):
    npop = part_hbm.shape[0]
    step = -(-npop // chunks)
    spans = [(k, min(k + step, npop)) for k in range(0, npop, step)]
    ins = [
        pltpu.make_async_copy(part_hbm.at[pl.ds(a, b - a)], buf.at[pl.ds(a, b - a)], sems.at[0, j])
        for j, (a, b) in enumerate(spans)
    ]
    outs = [
        pltpu.make_async_copy(buf.at[pl.ds(a, b - a)], out_hbm.at[pl.ds(a, b - a)], sems.at[1, j])
        for j, (a, b) in enumerate(spans)
    ]
    sin = pltpu.make_async_copy(sens_hbm, sbuf, sems.at[0, len(spans)])
    sout = pltpu.make_async_copy(sbuf, sens_out, sems.at[1, len(spans)])
    sin.start()
    for copy in ins:
        copy.start()
    sin.wait()
    sout.start()
    for cin, cout in zip(ins, outs):
        cin.wait()
        cout.start()
    sout.wait()
    for copy in outs:
        copy.wait()


def _write_out(part, sens, chunks=4):
    npop, rows, cz = part.shape
    nspan = len(range(0, npop, -(-npop // chunks)))
    hbm = pl.BlockSpec(memory_space=pltpu.HBM)
    return pl.pallas_call(
        functools.partial(_writer, chunks),
        out_shape=(
            jax.ShapeDtypeStruct(part.shape, jnp.float32),
            jax.ShapeDtypeStruct(sens.shape, jnp.float32),
        ),
        in_specs=[hbm, hbm],
        out_specs=(hbm, hbm),
        scratch_shapes=[
            pltpu.VMEM(part.shape, jnp.float32),
            pltpu.VMEM(sens.shape, jnp.float32),
            pltpu.SemaphoreType.DMA((2, nspan + 1)),
        ],
        compiler_params=pltpu.CompilerParams(vmem_limit_bytes=67043328),
    )(part, sens)


def solution(mesh):
    nx, ny, nz = mesh.shape["gx"], mesh.shape["gy"], mesh.shape["gz"]
    nmsg = len(_messages(8, 16))

    def shards(adjoint, density, velocity, pore_mask):
        npop, cx, cy, cz = adjoint.shape
        assert (cx, cy, cz) == (8, 16, 128)
        rows = cx * cy
        adj = adjoint.reshape(npop, rows, cz)
        rho = density.reshape(2, rows, cz)
        vel = velocity.reshape(2, 3, rows, cz)
        mask = pore_mask.reshape(rows, cz)
        vspec = pl.BlockSpec(memory_space=pltpu.VMEM)
        out, sens = pl.pallas_call(
            functools.partial(_kernel, (nx, ny, nz)),
            out_shape=(
                jax.ShapeDtypeStruct((npop, rows, cz), jnp.float32),
                jax.ShapeDtypeStruct((rows, cz), jnp.float32),
            ),
            in_specs=[pl.BlockSpec(memory_space=pltpu.HBM)] * 4,
            out_specs=(vspec, vspec),
            scratch_shapes=[
                pltpu.VMEM((npop, rows, cz), jnp.float32),
                pltpu.VMEM((2, rows, cz), jnp.float32),
                pltpu.VMEM((2, 3, rows, cz), jnp.float32),
                pltpu.VMEM((rows, cz), jnp.int32),
                pltpu.SemaphoreType.DMA((4,)),
                pltpu.VMEM((npop, rows, cz), jnp.float32),
                pltpu.VMEM((2, 2, 5, cy, cz), jnp.float32),
                pltpu.VMEM((2, 2, 5, cx, cz), jnp.float32),
                pltpu.VMEM((2, 4, 8, cz), jnp.float32),
                pltpu.VMEM((2, 2, 5, cx, cz), jnp.float32),
                pltpu.VMEM((2, rows, cz), jnp.float32),
                pltpu.VMEM((2, 2, rows, cz), jnp.float32),
                pltpu.VMEM((2, 2, rows, cz), jnp.float32),
                pltpu.SemaphoreType.DMA((2, nmsg)),
                pltpu.SemaphoreType.DMA((2, nmsg)),
            ],
            compiler_params=pltpu.CompilerParams(
                collective_id=0, has_side_effects=True, vmem_limit_bytes=67043328
            ),
        )(adj, rho, vel, mask)
        out, sens = _write_out(out, sens)
        return out.reshape(npop, cx, cy, cz), sens.reshape(cx, cy, cz)

    placed = (
        P(None, "gx", "gy", "gz"),
        P(None, "gx", "gy", "gz"),
        P(None, None, "gx", "gy", "gz"),
        P("gx", "gy", "gz"),
    )
    return jax.shard_map(
        shards,
        mesh=mesh,
        in_specs=placed,
        out_specs=(P(None, "gx", "gy", "gz"), P("gx", "gy", "gz")),
        check_vma=False,
    )
```

```python
import functools

import jax
import jax.numpy as jnp
from jax import lax
from jax.experimental import pallas as pl
from jax.experimental.pallas import tpu as pltpu
from jax.sharding import PartitionSpec as P

VELOCITIES = [
    (0, 0, 0),
    (1, 0, 0),
    (-1, 0, 0),
    (0, 1, 0),
    (0, -1, 0),
    (0, 0, 1),
    (0, 0, -1),
    (1, 1, 0),
    (-1, -1, 0),
    (1, -1, 0),
    (-1, 1, 0),
    (1, 0, 1),
    (-1, 0, -1),
    (1, 0, -1),
    (-1, 0, 1),
    (0, 1, 1),
    (0, -1, -1),
    (0, 1, -1),
    (0, -1, 1),
]
WEIGHTS = [1.0 / 3.0] + [1.0 / 18.0] * 6 + [1.0 / 36.0] * 12
OPPOSITE = [0, 2, 1, 4, 3, 6, 5, 8, 7, 10, 9, 12, 11, 14, 13, 16, 15, 18, 17]
OMEGA = 1.25
MESH = pl.DeviceIdType.MESH

CXP = [1, 7, 9, 11, 13]
CXM = [2, 8, 10, 12, 14]
CYP = [3, 7, 10, 15, 17]
CYM = [4, 8, 9, 16, 18]
ZCOLS = [(5, 0), (11, 0), (14, 0), (15, 0), (18, 0), (6, -1), (12, -1), (13, -1), (16, -1), (17, -1)]
ZFACE_COL = {5: 0, 11: 8, 14: 16, 15: 24, 18: 32, 6: 0, 12: 8, 13: 16, 16: 24, 17: 32}
XZ_EDGE = {11: (40, 0), 14: (48, -16), 12: (40, -16), 13: (48, 0)}
YZ_CORNER = {15: (56, 0), 18: (64, -1), 16: (56, -1), 17: (64, 0)}
XY_EDGE = {7: (0, 0), 8: (1, 7), 9: (2, 7), 10: (3, 0)}


def _messages(cx, cy):
    rows = cx * cy
    msgs = []
    for k, pop in enumerate(CXP):
        msgs.append(((-1, 0, 0), ("S", pop, 0, cy), ("XH", 1, k)))
    for k, pop in enumerate(CXM):
        msgs.append(((1, 0, 0), ("S", pop, rows - cy, cy), ("XH", 0, k)))
    msgs.append(((0, -1, 0), ("SY", 0), ("YH", 1)))
    msgs.append(((0, 1, 0), ("SY", 1), ("YH", 0)))
    msgs.append(((-1, -1, 0), ("S", 7, 0, 8), ("EXY", 0)))
    msgs.append(((1, 1, 0), ("S", 8, rows - 8, 8), ("EXY", 1)))
    msgs.append(((-1, 1, 0), ("S", 9, cy - 8, 8), ("EXY", 2)))
    msgs.append(((1, -1, 0), ("S", 10, rows - cy, 8), ("EXY", 3)))
    msgs.append(((0, 0, -1), ("NT", 0, 40), ("MH", 1, 0, 40)))
    msgs.append(((0, 0, 1), ("NT", 40, 40), ("MH", 0, 0, 40)))
    msgs.append(((-1, 0, -1), ("NT", 8, 8), ("MH", 1, 40, 8)))
    msgs.append(((1, 0, -1), ("NT", 16, 8), ("MH", 1, 48, 8)))
    msgs.append(((1, 0, 1), ("NT", 48, 8), ("MH", 0, 40, 8)))
    msgs.append(((-1, 0, 1), ("NT", 56, 8), ("MH", 0, 48, 8)))
    msgs.append(((0, -1, -1), ("NT", 24, 8), ("MH", 1, 56, 8)))
    msgs.append(((0, 1, -1), ("NT", 32, 8), ("MH", 1, 64, 8)))
    msgs.append(((0, 1, 1), ("NT", 64, 8), ("MH", 0, 56, 8)))
    msgs.append(((0, -1, 1), ("NT", 72, 8), ("MH", 0, 64, 8)))
    return msgs


NEIGHBOURS = sorted(
    {d for d, _, _ in _messages(8, 16)} | {tuple(-v for v in d) for d, _, _ in _messages(8, 16)}
)


def _comb(vals, fn):
    total = None
    for weight in (1.0 / 3.0, 1.0 / 18.0, 1.0 / 36.0):
        part = None
        for i in range(19):
            if WEIGHTS[i] != weight:
                continue
            k = fn(VELOCITIES[i])
            if k == 0:
                continue
            if part is None:
                part = vals[i] if k > 0 else -vals[i]
            else:
                part = part + vals[i] if k > 0 else part - vals[i]
        if part is not None:
            term = part * weight
            total = term if total is None else total + term
    return total


def _collide(pulled, rho, ux, uy, uz, fluid):
    p0 = _comb(pulled, lambda c: 1)
    p1 = [_comb(pulled, lambda c, a=a: c[a]) for a in range(3)]
    q = {}
    for a in range(3):
        for b in range(a, 3):
            q[a, b] = _comb(pulled, lambda c, a=a, b=b: c[a] * c[b])
            q[b, a] = q[a, b]
    u = (ux, uy, uz)
    usq = ux * ux + uy * uy + uz * uz
    qu = [q[a, 0] * ux + q[a, 1] * uy + q[a, 2] * uz for a in range(3)]
    p1u = p1[0] * ux + p1[1] * uy + p1[2] * uz
    uqu = ux * qu[0] + uy * qu[1] + uz * qu[2]
    moment = p0 * (1.0 - 1.5 * usq) + 3.0 * p1u + 4.5 * uqu
    vec = [3.0 * p1[a] + 9.0 * qu[a] - 3.0 * u[a] * p0 for a in range(3)]
    vu = vec[0] * ux + vec[1] * uy + vec[2] * uz
    inv = 1.0 / rho
    base = OMEGA * (moment - vu) - ux * inv
    bases = {0: base, 1: base + inv, -1: base - inv}
    wv = [OMEGA * v for v in vec]
    combos = {}
    layers = []
    for i in range(19):
        c = VELOCITIES[i]
        key = tuple(c)
        terms = [(a, c[a]) for a in range(3) if c[a] != 0]
        cv = None
        if terms:
            if len(terms) == 1:
                a, s = terms[0]
                cv = wv[a] if s > 0 else -wv[a]
            else:
                (a, s), (b, t) = terms
                pos = (a, b, s * t)
                if pos not in combos:
                    combos[pos] = wv[a] + wv[b] if s * t > 0 else wv[a] - wv[b]
                cv = combos[pos] if s > 0 else -combos[pos]
        val = (1.0 - OMEGA) * pulled[i] + bases[c[0]]
        if cv is not None:
            val = val + cv
        layers.append(jnp.where(fluid, val, pulled[OPPOSITE[i]]))
    sens = None
    for i in range(1, 19, 2):
        c = VELOCITIES[i]
        along = None
        for a in range(3):
            if c[a] == 0:
                continue
            if along is None:
                along = u[a] if c[a] > 0 else -u[a]
            else:
                along = along + u[a] if c[a] > 0 else along - u[a]
        term = (6.0 * WEIGHTS[i]) * along * (pulled[OPPOSITE[i]] - pulled[i])
        sens = term if sens is None else sens + term
    sens = jnp.where(fluid, rho * sens, 0.0)
    return layers, sens


def _kernel(dims, adj_hbm, rho_hbm, vel_hbm, mask_hbm, out_ref, sens_ref,
            adj_ref, rho_ref, vel_ref, mask_ref, load_sem,
            mid, fin, sfin, out_sem, xh, yh, exy, sy, nt, mh, mt, send_sem, recv_sem):
    nx, ny, nz = dims
    cx, cy, cz = 8, 16, 128
    rows = cx * cy
    me = (lax.axis_index("gx"), lax.axis_index("gy"), lax.axis_index("gz"))
    sizes = (nx, ny, nz)

    def exists(d):
        cond = None
        for a in range(3):
            if d[a] == 0:
                continue
            v = me[a] + d[a]
            c = (v >= 0) if d[a] < 0 else (v < sizes[a])
            cond = c if cond is None else jnp.logical_and(cond, c)
        return cond

    def target(d):
        return tuple(me[a] + d[a] for a in range(3))

    loads = [
        pltpu.make_async_copy(src, dst, load_sem.at[k])
        for k, (src, dst) in enumerate(
            ((adj_hbm, adj_ref), (vel_hbm, vel_ref), (rho_hbm, rho_ref), (mask_hbm, mask_ref))
        )
    ]
    for copy in loads:
        copy.start()

    xh[...] = jnp.zeros(xh.shape, jnp.float32)
    yh[...] = jnp.zeros(yh.shape, jnp.float32)
    exy[...] = jnp.zeros(exy.shape, jnp.float32)
    mh[...] = jnp.zeros(mh.shape, jnp.float32)

    barrier = pltpu.get_barrier_semaphore()
    for d in NEIGHBOURS:
        @pl.when(exists(d))
        def _():
            pl.semaphore_signal(barrier, inc=1, device_id=target(d), device_id_type=MESH)

    lane = lax.broadcasted_iota(jnp.int32, (cy, cz), 1)
    lane1 = lax.broadcasted_iota(jnp.int32, (1, cz), 1)
    row = lax.broadcasted_iota(jnp.int32, (cy, cz), 0)
    lane_big = lax.broadcasted_iota(jnp.int32, (rows, cz), 1)

    msgs = _messages(cx, cy)

    def prepare(s, src):
        for side, pops, y in ((0, CYP, 0), (1, CYM, cy - 1)):
            for k, pop in enumerate(pops):
                sy[s, side, k] = src[pop, pl.ds(y, cx, stride=cy), :]
        n = jnp.zeros((rows, cz), jnp.float32)
        for j, (pop, z) in enumerate(ZCOLS):
            zz = z % cz
            n = jnp.where(lane_big == 8 * j, pltpu.roll(src[pop], (8 * j - zz) % cz, 1), n)
        nt[s] = n.T

    def descriptor(s, src, m, t):
        d, so, de = msgs[t]
        if so[0] == "S":
            sref = src.at[so[1], pl.ds(so[2] % rows, so[3]), :]
        elif so[0] == "SY":
            sref = sy.at[s, so[1]]
        else:
            sref = nt.at[s, pl.ds(so[1], so[2]), :]
        if de[0] == "XH":
            dref = xh.at[s, de[1], de[2]]
        elif de[0] == "YH":
            dref = yh.at[s, de[1]]
        elif de[0] == "EXY":
            dref = exy.at[s, de[1]]
        else:
            dref = mh.at[s, de[1], pl.ds(de[2], de[3]), :]
        return pltpu.make_async_remote_copy(
            src_ref=sref, dst_ref=dref, send_sem=send_sem.at[s, t], recv_sem=recv_sem.at[s, t],
            device_id=target(d), device_id_type=MESH)

    def send(s, src):
        for t in range(len(msgs)):
            d = msgs[t][0]

            @pl.when(exists(d))
            def _():
                descriptor(s, src, msgs, t).start()

    def finish(s, src):
        for t in range(len(msgs)):
            d = msgs[t][0]
            back = tuple(-v for v in d)

            @pl.when(exists(back))
            def _():
                descriptor(s, src, msgs, t).wait_recv()

            @pl.when(exists(d))
            def _():
                descriptor(s, src, msgs, t).wait_send()
        for side in range(2):
            mt[s, side] = mh[s, side].T

    def pulled_plane(s, src, p):
        out = []
        for i in range(19):
            vx, vy, vz = VELOCITIES[i]
            q = p + vx
            if 0 <= q < cx:
                plane = src[i, pl.ds(q * cy, cy), :]
            elif q == cx:
                plane = xh[s, 1, CXP.index(i)]
            else:
                plane = xh[s, 0, CXM.index(i)]
            if vz != 0:
                side = 1 if vz > 0 else 0
                if 0 <= q < cx:
                    zc = mt[s, side, pl.ds(q * cy, cy), :]
                    col = ZFACE_COL[i]
                else:
                    col, r0 = XZ_EDGE[i]
                    zc = mt[s, side, pl.ds(r0 % rows, cy), :]
                if vz > 0:
                    plane = jnp.where(lane == cz - 1, pltpu.roll(zc, (cz - 1 - col) % cz, 1),
                                      pltpu.roll(plane, cz - 1, 1))
                else:
                    plane = jnp.where(lane == 0, pltpu.roll(zc, (cz - col) % cz, 1),
                                      pltpu.roll(plane, 1, 1))
            if vy != 0:
                side_y = 1 if vy > 0 else 0
                ky = CYP.index(i) if vy > 0 else CYM.index(i)
                if 0 <= q < cx:
                    yrow = yh[s, side_y, ky, pl.ds(q, 1), :]
                else:
                    e, r = XY_EDGE[i]
                    yrow = exy[s, e, pl.ds(r, 1), :]
                if vz != 0:
                    side = 1 if vz > 0 else 0
                    colc, yoff = YZ_CORNER[i]
                    crow = mt[s, side, pl.ds(p * cy + yoff % cy, 1), :]
                    if vz > 0:
                        yrow = jnp.where(lane1 == cz - 1, pltpu.roll(crow, (cz - 1 - colc) % cz, 1),
                                         pltpu.roll(yrow, cz - 1, 1))
                    else:
                        yrow = jnp.where(lane1 == 0, pltpu.roll(crow, (cz - colc) % cz, 1),
                                         pltpu.roll(yrow, 1, 1))
                if vy > 0:
                    plane = jnp.where(row == cy - 1, yrow, pltpu.roll(plane, cy - 1, 0))
                else:
                    plane = jnp.where(row == 0, yrow, pltpu.roll(plane, 1, 0))
            out.append(plane)
        return out

    def flush(p):
        rs = pl.ds(p * cy, cy)
        pltpu.make_async_copy(fin.at[:, rs, :], out_ref.at[:, rs, :], out_sem.at[p]).start()

    def step(s, src, dst, level):
        for p in range(cx):
            if s == 1 and p >= 1:
                flush(p - 1)
            rs = pl.ds(p * cy, cy)
            pulled = pulled_plane(s, src, p)
            rho = rho_ref[level, rs, :]
            ux = vel_ref[level, 0, rs, :]
            uy = vel_ref[level, 1, rs, :]
            uz = vel_ref[level, 2, rs, :]
            fluid = mask_ref[rs, :] > 0
            layers, sens = _collide(pulled, rho, ux, uy, uz, fluid)
            for i in range(19):
                dst[i, rs, :] = layers[i]
            if s == 0:
                sfin[rs, :] = sens
            else:
                sfin[rs, :] = sfin[rs, :] + sens

    def indicator(a, off):
        n = sizes[a]
        if off < 0:
            return (me[a] + n - 1) // n
        if off > 0:
            return (2 * n - 2 - me[a]) // n
        return 1

    peers = 0
    for d in NEIGHBOURS:
        term = 1
        for a in range(3):
            term = term * indicator(a, d[a])
        peers = peers + term
    loads[0].wait()
    prepare(0, adj_ref)
    pl.semaphore_wait(barrier, peers)
    send(0, adj_ref)
    for copy in loads[1:]:
        copy.wait()
    finish(0, adj_ref)
    step(0, adj_ref, mid, 1)
    prepare(1, mid)
    send(1, mid)
    finish(1, mid)
    step(1, mid, fin, 0)
    flush(cx - 1)
    sens_copy = pltpu.make_async_copy(sfin, sens_ref, out_sem.at[cx])
    sens_copy.start()
    for p in range(cx):
        rs = pl.ds(p * cy, cy)
        pltpu.make_async_copy(fin.at[:, rs, :], out_ref.at[:, rs, :], out_sem.at[p]).wait()
    sens_copy.wait()


def _writer(chunks, part_hbm, sens_hbm, out_hbm, sens_out, buf, sbuf, sems):
    npop = part_hbm.shape[0]
    step = -(-npop // chunks)
    spans = [(k, min(k + step, npop)) for k in range(0, npop, step)]
    ins = [
        pltpu.make_async_copy(part_hbm.at[pl.ds(a, b - a)], buf.at[pl.ds(a, b - a)], sems.at[0, j])
        for j, (a, b) in enumerate(spans)
    ]
    outs = [
        pltpu.make_async_copy(buf.at[pl.ds(a, b - a)], out_hbm.at[pl.ds(a, b - a)], sems.at[1, j])
        for j, (a, b) in enumerate(spans)
    ]
    sin = pltpu.make_async_copy(sens_hbm, sbuf, sems.at[0, len(spans)])
    sout = pltpu.make_async_copy(sbuf, sens_out, sems.at[1, len(spans)])
    sin.start()
    for copy in ins:
        copy.start()
    sin.wait()
    sout.start()
    for cin, cout in zip(ins, outs):
        cin.wait()
        cout.start()
    sout.wait()
    for copy in outs:
        copy.wait()


def _write_out(part, sens, chunks=8):
    npop, rows, cz = part.shape
    nspan = len(range(0, npop, -(-npop // chunks)))
    hbm = pl.BlockSpec(memory_space=pltpu.HBM)
    return pl.pallas_call(
        functools.partial(_writer, chunks),
        out_shape=(
            jax.ShapeDtypeStruct(part.shape, jnp.float32),
            jax.ShapeDtypeStruct(sens.shape, jnp.float32),
        ),
        in_specs=[hbm, hbm],
        out_specs=(hbm, hbm),
        scratch_shapes=[
            pltpu.VMEM(part.shape, jnp.float32),
            pltpu.VMEM(sens.shape, jnp.float32),
            pltpu.SemaphoreType.DMA((2, nspan + 1)),
        ],
        compiler_params=pltpu.CompilerParams(vmem_limit_bytes=67043328),
    )(part, sens)


def solution(mesh):
    nx, ny, nz = mesh.shape["gx"], mesh.shape["gy"], mesh.shape["gz"]
    nmsg = len(_messages(8, 16))

    def shards(adjoint, density, velocity, pore_mask):
        npop, cx, cy, cz = adjoint.shape
        assert (cx, cy, cz) == (8, 16, 128)
        rows = cx * cy
        adj = adjoint.reshape(npop, rows, cz)
        rho = density.reshape(2, rows, cz)
        vel = velocity.reshape(2, 3, rows, cz)
        mask = pore_mask.reshape(rows, cz)
        vspec = pl.BlockSpec(memory_space=pltpu.VMEM)
        out, sens = pl.pallas_call(
            functools.partial(_kernel, (nx, ny, nz)),
            out_shape=(
                jax.ShapeDtypeStruct((npop, rows, cz), jnp.float32),
                jax.ShapeDtypeStruct((rows, cz), jnp.float32),
            ),
            in_specs=[pl.BlockSpec(memory_space=pltpu.HBM)] * 4,
            out_specs=(pl.BlockSpec(memory_space=pltpu.HBM), pl.BlockSpec(memory_space=pltpu.HBM)),
            scratch_shapes=[
                pltpu.VMEM((npop, rows, cz), jnp.float32),
                pltpu.VMEM((2, rows, cz), jnp.float32),
                pltpu.VMEM((2, 3, rows, cz), jnp.float32),
                pltpu.VMEM((rows, cz), jnp.int32),
                pltpu.SemaphoreType.DMA((4,)),
                pltpu.VMEM((npop, rows, cz), jnp.float32),
                pltpu.VMEM((npop, rows, cz), jnp.float32),
                pltpu.VMEM((rows, cz), jnp.float32),
                pltpu.SemaphoreType.DMA((cx + 1,)),
                pltpu.VMEM((2, 2, 5, cy, cz), jnp.float32),
                pltpu.VMEM((2, 2, 5, cx, cz), jnp.float32),
                pltpu.VMEM((2, 4, 8, cz), jnp.float32),
                pltpu.VMEM((2, 2, 5, cx, cz), jnp.float32),
                pltpu.VMEM((2, rows, cz), jnp.float32),
                pltpu.VMEM((2, 2, rows, cz), jnp.float32),
                pltpu.VMEM((2, 2, rows, cz), jnp.float32),
                pltpu.SemaphoreType.DMA((2, nmsg)),
                pltpu.SemaphoreType.DMA((2, nmsg)),
            ],
            compiler_params=pltpu.CompilerParams(
                collective_id=0, has_side_effects=True, vmem_limit_bytes=67043328
            ),
        )(adj, rho, vel, mask)
        out, sens = _write_out(out, sens)
        return out.reshape(npop, cx, cy, cz), sens.reshape(cx, cy, cz)

    placed = (
        P(None, "gx", "gy", "gz"),
        P(None, "gx", "gy", "gz"),
        P(None, None, "gx", "gy", "gz"),
        P("gx", "gy", "gz"),
    )
    return jax.shard_map(
        shards,
        mesh=mesh,
        in_specs=placed,
        out_specs=(P(None, "gx", "gy", "gz"), P("gx", "gy", "gz")),
        check_vma=False,
    )
```

```python
import functools

import jax
import jax.numpy as jnp
from jax import lax
from jax.experimental import pallas as pl
from jax.experimental.pallas import tpu as pltpu
from jax.sharding import PartitionSpec as P

VELOCITIES = [
    (0, 0, 0),
    (1, 0, 0),
    (-1, 0, 0),
    (0, 1, 0),
    (0, -1, 0),
    (0, 0, 1),
    (0, 0, -1),
    (1, 1, 0),
    (-1, -1, 0),
    (1, -1, 0),
    (-1, 1, 0),
    (1, 0, 1),
    (-1, 0, -1),
    (1, 0, -1),
    (-1, 0, 1),
    (0, 1, 1),
    (0, -1, -1),
    (0, 1, -1),
    (0, -1, 1),
]
WEIGHTS = [1.0 / 3.0] + [1.0 / 18.0] * 6 + [1.0 / 36.0] * 12
OPPOSITE = [0, 2, 1, 4, 3, 6, 5, 8, 7, 10, 9, 12, 11, 14, 13, 16, 15, 18, 17]
OMEGA = 1.25
MESH = pl.DeviceIdType.MESH

CXP = [1, 7, 9, 11, 13]
CXM = [2, 8, 10, 12, 14]
CYP = [3, 7, 10, 15, 17]
CYM = [4, 8, 9, 16, 18]
ZCOLS = [(5, 0), (11, 0), (14, 0), (15, 0), (18, 0), (6, -1), (12, -1), (13, -1), (16, -1), (17, -1)]
ZFACE_COL = {5: 0, 11: 8, 14: 16, 15: 24, 18: 32, 6: 0, 12: 8, 13: 16, 16: 24, 17: 32}
XZ_EDGE = {11: (40, 0), 14: (48, -16), 12: (40, -16), 13: (48, 0)}
YZ_CORNER = {15: (56, 0), 18: (64, -1), 16: (56, -1), 17: (64, 0)}
XY_EDGE = {7: (0, 0), 8: (1, 7), 9: (2, 7), 10: (3, 0)}


def _messages(cx, cy):
    rows = cx * cy
    msgs = []
    msgs.append(((0, -1, 0), ("SY", 0), ("YH", 1)))
    msgs.append(((0, 1, 0), ("SY", 1), ("YH", 0)))
    msgs.append(((0, -1, -1), ("NT", 24, 8), ("MH", 1, 56, 8)))
    msgs.append(((0, 1, -1), ("NT", 32, 8), ("MH", 1, 64, 8)))
    msgs.append(((0, 1, 1), ("NT", 64, 8), ("MH", 0, 56, 8)))
    msgs.append(((0, -1, 1), ("NT", 72, 8), ("MH", 0, 64, 8)))
    msgs.append(((-1, -1, 0), ("S", 7, 0, 8), ("EXY", 0)))
    msgs.append(((1, 1, 0), ("S", 8, rows - 8, 8), ("EXY", 1)))
    msgs.append(((-1, 1, 0), ("S", 9, cy - 8, 8), ("EXY", 2)))
    msgs.append(((1, -1, 0), ("S", 10, rows - cy, 8), ("EXY", 3)))
    msgs.append(((0, 0, -1), ("NT", 0, 40), ("MH", 1, 0, 40)))
    msgs.append(((0, 0, 1), ("NT", 40, 40), ("MH", 0, 0, 40)))
    msgs.append(((-1, 0, -1), ("NT", 8, 8), ("MH", 1, 40, 8)))
    msgs.append(((1, 0, -1), ("NT", 16, 8), ("MH", 1, 48, 8)))
    msgs.append(((1, 0, 1), ("NT", 48, 8), ("MH", 0, 40, 8)))
    msgs.append(((-1, 0, 1), ("NT", 56, 8), ("MH", 0, 48, 8)))
    msgs.append(((-1, 0, 0), ("SX", 0), ("XH", 1)))
    msgs.append(((1, 0, 0), ("SX", 1), ("XH", 0)))
    return msgs


NEIGHBOURS = sorted(
    {d for d, _, _ in _messages(8, 16)} | {tuple(-v for v in d) for d, _, _ in _messages(8, 16)}
)


def _comb(vals, fn):
    total = None
    for weight in (1.0 / 3.0, 1.0 / 18.0, 1.0 / 36.0):
        part = None
        for i in range(19):
            if WEIGHTS[i] != weight:
                continue
            k = fn(VELOCITIES[i])
            if k == 0:
                continue
            if part is None:
                part = vals[i] if k > 0 else -vals[i]
            else:
                part = part + vals[i] if k > 0 else part - vals[i]
        if part is not None:
            term = part * weight
            total = term if total is None else total + term
    return total


def _collide(pulled, rho, ux, uy, uz, fluid):
    p0 = _comb(pulled, lambda c: 1)
    p1 = [_comb(pulled, lambda c, a=a: c[a]) for a in range(3)]
    q = {}
    for a in range(3):
        for b in range(a, 3):
            q[a, b] = _comb(pulled, lambda c, a=a, b=b: c[a] * c[b])
            q[b, a] = q[a, b]
    u = (ux, uy, uz)
    usq = ux * ux + uy * uy + uz * uz
    qu = [q[a, 0] * ux + q[a, 1] * uy + q[a, 2] * uz for a in range(3)]
    p1u = p1[0] * ux + p1[1] * uy + p1[2] * uz
    uqu = ux * qu[0] + uy * qu[1] + uz * qu[2]
    moment = p0 * (1.0 - 1.5 * usq) + 3.0 * p1u + 4.5 * uqu
    vec = [3.0 * p1[a] + 9.0 * qu[a] - 3.0 * u[a] * p0 for a in range(3)]
    vu = vec[0] * ux + vec[1] * uy + vec[2] * uz
    inv = 1.0 / rho
    base = OMEGA * (moment - vu) - ux * inv
    bases = {0: base, 1: base + inv, -1: base - inv}
    wv = [OMEGA * v for v in vec]
    combos = {}
    layers = []
    for i in range(19):
        c = VELOCITIES[i]
        key = tuple(c)
        terms = [(a, c[a]) for a in range(3) if c[a] != 0]
        cv = None
        if terms:
            if len(terms) == 1:
                a, s = terms[0]
                cv = wv[a] if s > 0 else -wv[a]
            else:
                (a, s), (b, t) = terms
                pos = (a, b, s * t)
                if pos not in combos:
                    combos[pos] = wv[a] + wv[b] if s * t > 0 else wv[a] - wv[b]
                cv = combos[pos] if s > 0 else -combos[pos]
        val = (1.0 - OMEGA) * pulled[i] + bases[c[0]]
        if cv is not None:
            val = val + cv
        layers.append(jnp.where(fluid, val, pulled[OPPOSITE[i]]))
    sens = None
    for i in range(1, 19, 2):
        c = VELOCITIES[i]
        along = None
        for a in range(3):
            if c[a] == 0:
                continue
            if along is None:
                along = u[a] if c[a] > 0 else -u[a]
            else:
                along = along + u[a] if c[a] > 0 else along - u[a]
        term = (6.0 * WEIGHTS[i]) * along * (pulled[OPPOSITE[i]] - pulled[i])
        sens = term if sens is None else sens + term
    sens = jnp.where(fluid, rho * sens, 0.0)
    return layers, sens


def _kernel(dims, adj_hbm, rho_hbm, vel_hbm, mask_hbm, out_ref, sens_ref,
            adj_ref, rho_ref, vel_ref, mask_ref, load_sem,
            mid, fin, sfin, out_sem, xh, yh, exy, sy, sx, nt, mh, mt, send_sem, recv_sem):
    nx, ny, nz = dims
    cx, cy, cz = 8, 16, 128
    rows = cx * cy
    me = (lax.axis_index("gx"), lax.axis_index("gy"), lax.axis_index("gz"))
    sizes = (nx, ny, nz)

    def exists(d):
        cond = None
        for a in range(3):
            if d[a] == 0:
                continue
            v = me[a] + d[a]
            c = (v >= 0) if d[a] < 0 else (v < sizes[a])
            cond = c if cond is None else jnp.logical_and(cond, c)
        return cond

    def target(d):
        return tuple(me[a] + d[a] for a in range(3))

    loads = [
        pltpu.make_async_copy(src, dst, load_sem.at[k])
        for k, (src, dst) in enumerate(
            ((adj_hbm, adj_ref), (vel_hbm, vel_ref), (rho_hbm, rho_ref), (mask_hbm, mask_ref))
        )
    ]
    for copy in loads:
        copy.start()

    xh[...] = jnp.zeros(xh.shape, jnp.float32)
    yh[...] = jnp.zeros(yh.shape, jnp.float32)
    exy[...] = jnp.zeros(exy.shape, jnp.float32)
    mh[...] = jnp.zeros(mh.shape, jnp.float32)

    barrier = pltpu.get_barrier_semaphore()
    for d in NEIGHBOURS:
        @pl.when(exists(d))
        def _():
            pl.semaphore_signal(barrier, inc=1, device_id=target(d), device_id_type=MESH)

    lane = lax.broadcasted_iota(jnp.int32, (cy, cz), 1)
    lane1 = lax.broadcasted_iota(jnp.int32, (1, cz), 1)
    row = lax.broadcasted_iota(jnp.int32, (cy, cz), 0)
    lane_big = lax.broadcasted_iota(jnp.int32, (rows, cz), 1)

    msgs = _messages(cx, cy)

    def prepare(s, src):
        for side, pops, q in ((0, CXP, 0), (1, CXM, cx - 1)):
            for k, pop in enumerate(pops):
                sx[s, side, k] = src[pop, pl.ds(q * cy, cy), :]
        for side, pops, y in ((0, CYP, 0), (1, CYM, cy - 1)):
            for k, pop in enumerate(pops):
                sy[s, side, k] = src[pop, pl.ds(y, cx, stride=cy), :]
        n = jnp.zeros((rows, cz), jnp.float32)
        for j, (pop, z) in enumerate(ZCOLS):
            zz = z % cz
            n = jnp.where(lane_big == 8 * j, pltpu.roll(src[pop], (8 * j - zz) % cz, 1), n)
        nt[s] = n.T

    def descriptor(s, src, m, t):
        d, so, de = msgs[t]
        if so[0] == "S":
            sref = src.at[so[1], pl.ds(so[2] % rows, so[3]), :]
        elif so[0] == "SY":
            sref = sy.at[s, so[1]]
        elif so[0] == "SX":
            sref = sx.at[s, so[1]]
        else:
            sref = nt.at[s, pl.ds(so[1], so[2]), :]
        if de[0] == "XH":
            dref = xh.at[s, de[1]]
        elif de[0] == "YH":
            dref = yh.at[s, de[1]]
        elif de[0] == "EXY":
            dref = exy.at[s, de[1]]
        else:
            dref = mh.at[s, de[1], pl.ds(de[2], de[3]), :]
        return pltpu.make_async_remote_copy(
            src_ref=sref, dst_ref=dref, send_sem=send_sem.at[s, t], recv_sem=recv_sem.at[s, t],
            device_id=target(d), device_id_type=MESH)

    def send(s, src):
        for t in range(len(msgs)):
            d = msgs[t][0]

            @pl.when(exists(d))
            def _():
                descriptor(s, src, msgs, t).start()

    def finish(s, src):
        for t in range(len(msgs)):
            d = msgs[t][0]
            back = tuple(-v for v in d)

            @pl.when(exists(back))
            def _():
                descriptor(s, src, msgs, t).wait_recv()

            @pl.when(exists(d))
            def _():
                descriptor(s, src, msgs, t).wait_send()
        for side in range(2):
            mt[s, side] = mh[s, side].T

    def pulled_plane(s, src, p):
        out = []
        for i in range(19):
            vx, vy, vz = VELOCITIES[i]
            q = p + vx
            if 0 <= q < cx:
                plane = src[i, pl.ds(q * cy, cy), :]
            elif q == cx:
                plane = xh[s, 1, CXP.index(i)]
            else:
                plane = xh[s, 0, CXM.index(i)]
            if vz != 0:
                side = 1 if vz > 0 else 0
                if 0 <= q < cx:
                    zc = mt[s, side, pl.ds(q * cy, cy), :]
                    col = ZFACE_COL[i]
                else:
                    col, r0 = XZ_EDGE[i]
                    zc = mt[s, side, pl.ds(r0 % rows, cy), :]
                if vz > 0:
                    plane = jnp.where(lane == cz - 1, pltpu.roll(zc, (cz - 1 - col) % cz, 1),
                                      pltpu.roll(plane, cz - 1, 1))
                else:
                    plane = jnp.where(lane == 0, pltpu.roll(zc, (cz - col) % cz, 1),
                                      pltpu.roll(plane, 1, 1))
            if vy != 0:
                side_y = 1 if vy > 0 else 0
                ky = CYP.index(i) if vy > 0 else CYM.index(i)
                if 0 <= q < cx:
                    yrow = yh[s, side_y, ky, pl.ds(q, 1), :]
                else:
                    e, r = XY_EDGE[i]
                    yrow = exy[s, e, pl.ds(r, 1), :]
                if vz != 0:
                    side = 1 if vz > 0 else 0
                    colc, yoff = YZ_CORNER[i]
                    crow = mt[s, side, pl.ds(p * cy + yoff % cy, 1), :]
                    if vz > 0:
                        yrow = jnp.where(lane1 == cz - 1, pltpu.roll(crow, (cz - 1 - colc) % cz, 1),
                                         pltpu.roll(yrow, cz - 1, 1))
                    else:
                        yrow = jnp.where(lane1 == 0, pltpu.roll(crow, (cz - colc) % cz, 1),
                                         pltpu.roll(yrow, 1, 1))
                if vy > 0:
                    plane = jnp.where(row == cy - 1, yrow, pltpu.roll(plane, cy - 1, 0))
                else:
                    plane = jnp.where(row == 0, yrow, pltpu.roll(plane, 1, 0))
            out.append(plane)
        return out

    def flush(p):
        rs = pl.ds(p * cy, cy)
        pltpu.make_async_copy(fin.at[:, rs, :], out_ref.at[:, rs, :], out_sem.at[p]).start()

    def step(s, src, dst, level):
        for p in range(cx):
            if s == 1 and p >= 1:
                flush(p - 1)
            rs = pl.ds(p * cy, cy)
            pulled = pulled_plane(s, src, p)
            rho = rho_ref[level, rs, :]
            ux = vel_ref[level, 0, rs, :]
            uy = vel_ref[level, 1, rs, :]
            uz = vel_ref[level, 2, rs, :]
            fluid = mask_ref[rs, :] > 0
            layers, sens = _collide(pulled, rho, ux, uy, uz, fluid)
            for i in range(19):
                dst[i, rs, :] = layers[i]
            if s == 0:
                sfin[rs, :] = sens
            else:
                sfin[rs, :] = sfin[rs, :] + sens

    def indicator(a, off):
        n = sizes[a]
        if off < 0:
            return (me[a] + n - 1) // n
        if off > 0:
            return (2 * n - 2 - me[a]) // n
        return 1

    peers = 0
    for d in NEIGHBOURS:
        term = 1
        for a in range(3):
            term = term * indicator(a, d[a])
        peers = peers + term
    loads[0].wait()
    prepare(0, adj_ref)
    pl.semaphore_wait(barrier, peers)
    send(0, adj_ref)
    for copy in loads[1:]:
        copy.wait()
    finish(0, adj_ref)
    step(0, adj_ref, mid, 1)
    prepare(1, mid)
    send(1, mid)
    finish(1, mid)
    step(1, mid, fin, 0)
    flush(cx - 1)
    sens_copy = pltpu.make_async_copy(sfin, sens_ref, out_sem.at[cx])
    sens_copy.start()
    for p in range(cx):
        rs = pl.ds(p * cy, cy)
        pltpu.make_async_copy(fin.at[:, rs, :], out_ref.at[:, rs, :], out_sem.at[p]).wait()
    sens_copy.wait()


def _writer(chunks, part_hbm, sens_hbm, out_hbm, sens_out, buf, sbuf, sems):
    npop = part_hbm.shape[0]
    step = -(-npop // chunks)
    spans = [(k, min(k + step, npop)) for k in range(0, npop, step)]
    ins = [
        pltpu.make_async_copy(part_hbm.at[pl.ds(a, b - a)], buf.at[pl.ds(a, b - a)], sems.at[0, j])
        for j, (a, b) in enumerate(spans)
    ]
    outs = [
        pltpu.make_async_copy(buf.at[pl.ds(a, b - a)], out_hbm.at[pl.ds(a, b - a)], sems.at[1, j])
        for j, (a, b) in enumerate(spans)
    ]
    sin = pltpu.make_async_copy(sens_hbm, sbuf, sems.at[0, len(spans)])
    sout = pltpu.make_async_copy(sbuf, sens_out, sems.at[1, len(spans)])
    sin.start()
    for copy in ins:
        copy.start()
    sin.wait()
    sout.start()
    for cin, cout in zip(ins, outs):
        cin.wait()
        cout.start()
    sout.wait()
    for copy in outs:
        copy.wait()


def _write_out(part, sens, chunks=8):
    npop, rows, cz = part.shape
    nspan = len(range(0, npop, -(-npop // chunks)))
    hbm = pl.BlockSpec(memory_space=pltpu.HBM)
    return pl.pallas_call(
        functools.partial(_writer, chunks),
        out_shape=(
            jax.ShapeDtypeStruct(part.shape, jnp.float32),
            jax.ShapeDtypeStruct(sens.shape, jnp.float32),
        ),
        in_specs=[hbm, hbm],
        out_specs=(hbm, hbm),
        scratch_shapes=[
            pltpu.VMEM(part.shape, jnp.float32),
            pltpu.VMEM(sens.shape, jnp.float32),
            pltpu.SemaphoreType.DMA((2, nspan + 1)),
        ],
        compiler_params=pltpu.CompilerParams(vmem_limit_bytes=67043328),
    )(part, sens)


def solution(mesh):
    nx, ny, nz = mesh.shape["gx"], mesh.shape["gy"], mesh.shape["gz"]
    nmsg = len(_messages(8, 16))

    def shards(adjoint, density, velocity, pore_mask):
        npop, cx, cy, cz = adjoint.shape
        assert (cx, cy, cz) == (8, 16, 128)
        rows = cx * cy
        adj = adjoint.reshape(npop, rows, cz)
        rho = density.reshape(2, rows, cz)
        vel = velocity.reshape(2, 3, rows, cz)
        mask = pore_mask.reshape(rows, cz)
        vspec = pl.BlockSpec(memory_space=pltpu.VMEM)
        out, sens = pl.pallas_call(
            functools.partial(_kernel, (nx, ny, nz)),
            out_shape=(
                jax.ShapeDtypeStruct((npop, rows, cz), jnp.float32),
                jax.ShapeDtypeStruct((rows, cz), jnp.float32),
            ),
            in_specs=[pl.BlockSpec(memory_space=pltpu.HBM)] * 4,
            out_specs=(pl.BlockSpec(memory_space=pltpu.HBM), pl.BlockSpec(memory_space=pltpu.HBM)),
            scratch_shapes=[
                pltpu.VMEM((npop, rows, cz), jnp.float32),
                pltpu.VMEM((2, rows, cz), jnp.float32),
                pltpu.VMEM((2, 3, rows, cz), jnp.float32),
                pltpu.VMEM((rows, cz), jnp.int32),
                pltpu.SemaphoreType.DMA((4,)),
                pltpu.VMEM((npop, rows, cz), jnp.float32),
                pltpu.VMEM((npop, rows, cz), jnp.float32),
                pltpu.VMEM((rows, cz), jnp.float32),
                pltpu.SemaphoreType.DMA((cx + 1,)),
                pltpu.VMEM((2, 2, 5, cy, cz), jnp.float32),
                pltpu.VMEM((2, 2, 5, cx, cz), jnp.float32),
                pltpu.VMEM((2, 4, 8, cz), jnp.float32),
                pltpu.VMEM((2, 2, 5, cx, cz), jnp.float32),
                pltpu.VMEM((2, 2, 5, cy, cz), jnp.float32),
                pltpu.VMEM((2, rows, cz), jnp.float32),
                pltpu.VMEM((2, 2, rows, cz), jnp.float32),
                pltpu.VMEM((2, 2, rows, cz), jnp.float32),
                pltpu.SemaphoreType.DMA((2, nmsg)),
                pltpu.SemaphoreType.DMA((2, nmsg)),
            ],
            compiler_params=pltpu.CompilerParams(
                collective_id=0, has_side_effects=True, vmem_limit_bytes=67043328
            ),
        )(adj, rho, vel, mask)
        out, sens = _write_out(out, sens)
        return out.reshape(npop, cx, cy, cz), sens.reshape(cx, cy, cz)

    placed = (
        P(None, "gx", "gy", "gz"),
        P(None, "gx", "gy", "gz"),
        P(None, None, "gx", "gy", "gz"),
        P("gx", "gy", "gz"),
    )
    return jax.shard_map(
        shards,
        mesh=mesh,
        in_specs=placed,
        out_specs=(P(None, "gx", "gy", "gz"), P("gx", "gy", "gz")),
        check_vma=False,
    )
```

```python
import functools

import jax
import jax.numpy as jnp
from jax import lax
from jax.experimental import pallas as pl
from jax.experimental.pallas import tpu as pltpu
from jax.sharding import PartitionSpec as P

VELOCITIES = [
    (0, 0, 0),
    (1, 0, 0),
    (-1, 0, 0),
    (0, 1, 0),
    (0, -1, 0),
    (0, 0, 1),
    (0, 0, -1),
    (1, 1, 0),
    (-1, -1, 0),
    (1, -1, 0),
    (-1, 1, 0),
    (1, 0, 1),
    (-1, 0, -1),
    (1, 0, -1),
    (-1, 0, 1),
    (0, 1, 1),
    (0, -1, -1),
    (0, 1, -1),
    (0, -1, 1),
]
WEIGHTS = [1.0 / 3.0] + [1.0 / 18.0] * 6 + [1.0 / 36.0] * 12
OPPOSITE = [0, 2, 1, 4, 3, 6, 5, 8, 7, 10, 9, 12, 11, 14, 13, 16, 15, 18, 17]
OMEGA = 1.25
MESH = pl.DeviceIdType.MESH

CXP = [1, 7, 9, 11, 13]
CXM = [2, 8, 10, 12, 14]
CYP = [3, 7, 10, 15, 17]
CYM = [4, 8, 9, 16, 18]
ZCOLS = [(5, 0), (11, 0), (14, 0), (15, 0), (18, 0), (6, -1), (12, -1), (13, -1), (16, -1), (17, -1)]
ZFACE_COL = {5: 0, 11: 8, 14: 16, 15: 24, 18: 32, 6: 0, 12: 8, 13: 16, 16: 24, 17: 32}
XZ_EDGE = {11: (40, 0), 14: (48, -16), 12: (40, -16), 13: (48, 0)}
YZ_CORNER = {15: (56, 0), 18: (64, -1), 16: (56, -1), 17: (64, 0)}
XY_EDGE = {7: (0, 0), 8: (1, 7), 9: (2, 7), 10: (3, 0)}


def _messages(cx, cy):
    rows = cx * cy
    msgs = []
    msgs.append(((0, -1, 0), ("SY", 0), ("YH", 1)))
    msgs.append(((0, 1, 0), ("SY", 1), ("YH", 0)))
    msgs.append(((0, -1, -1), ("NT", 24, 8), ("MH", 1, 56, 8)))
    msgs.append(((0, 1, -1), ("NT", 32, 8), ("MH", 1, 64, 8)))
    msgs.append(((0, 1, 1), ("NT", 64, 8), ("MH", 0, 56, 8)))
    msgs.append(((0, -1, 1), ("NT", 72, 8), ("MH", 0, 64, 8)))
    msgs.append(((-1, -1, 0), ("S", 7, 0, 8), ("EXY", 0)))
    msgs.append(((1, 1, 0), ("S", 8, rows - 8, 8), ("EXY", 1)))
    msgs.append(((-1, 1, 0), ("S", 9, cy - 8, 8), ("EXY", 2)))
    msgs.append(((1, -1, 0), ("S", 10, rows - cy, 8), ("EXY", 3)))
    msgs.append(((0, 0, -1), ("NT", 0, 40), ("MH", 1, 0, 40)))
    msgs.append(((0, 0, 1), ("NT", 40, 40), ("MH", 0, 0, 40)))
    msgs.append(((-1, 0, -1), ("NT", 8, 8), ("MH", 1, 40, 8)))
    msgs.append(((1, 0, -1), ("NT", 16, 8), ("MH", 1, 48, 8)))
    msgs.append(((1, 0, 1), ("NT", 48, 8), ("MH", 0, 40, 8)))
    msgs.append(((-1, 0, 1), ("NT", 56, 8), ("MH", 0, 48, 8)))
    msgs.append(((-1, 0, 0), ("SX", 0), ("XH", 1)))
    msgs.append(((1, 0, 0), ("SX", 1), ("XH", 0)))
    return msgs


NEIGHBOURS = sorted(
    {d for d, _, _ in _messages(8, 16)} | {tuple(-v for v in d) for d, _, _ in _messages(8, 16)}
)


def _comb(vals, fn):
    total = None
    for weight in (1.0 / 3.0, 1.0 / 18.0, 1.0 / 36.0):
        part = None
        for i in range(19):
            if WEIGHTS[i] != weight:
                continue
            k = fn(VELOCITIES[i])
            if k == 0:
                continue
            if part is None:
                part = vals[i] if k > 0 else -vals[i]
            else:
                part = part + vals[i] if k > 0 else part - vals[i]
        if part is not None:
            term = part * weight
            total = term if total is None else total + term
    return total


def _collide(pulled, rho, ux, uy, uz, fluid):
    p0 = _comb(pulled, lambda c: 1)
    p1 = [_comb(pulled, lambda c, a=a: c[a]) for a in range(3)]
    q = {}
    for a in range(3):
        for b in range(a, 3):
            q[a, b] = _comb(pulled, lambda c, a=a, b=b: c[a] * c[b])
            q[b, a] = q[a, b]
    u = (ux, uy, uz)
    usq = ux * ux + uy * uy + uz * uz
    qu = [q[a, 0] * ux + q[a, 1] * uy + q[a, 2] * uz for a in range(3)]
    p1u = p1[0] * ux + p1[1] * uy + p1[2] * uz
    uqu = ux * qu[0] + uy * qu[1] + uz * qu[2]
    moment = p0 * (1.0 - 1.5 * usq) + 3.0 * p1u + 4.5 * uqu
    vec = [3.0 * p1[a] + 9.0 * qu[a] - 3.0 * u[a] * p0 for a in range(3)]
    vu = vec[0] * ux + vec[1] * uy + vec[2] * uz
    inv = 1.0 / rho
    base = OMEGA * (moment - vu) - ux * inv
    bases = {0: base, 1: base + inv, -1: base - inv}
    wv = [OMEGA * v for v in vec]
    combos = {}
    layers = []
    for i in range(19):
        c = VELOCITIES[i]
        key = tuple(c)
        terms = [(a, c[a]) for a in range(3) if c[a] != 0]
        cv = None
        if terms:
            if len(terms) == 1:
                a, s = terms[0]
                cv = wv[a] if s > 0 else -wv[a]
            else:
                (a, s), (b, t) = terms
                pos = (a, b, s * t)
                if pos not in combos:
                    combos[pos] = wv[a] + wv[b] if s * t > 0 else wv[a] - wv[b]
                cv = combos[pos] if s > 0 else -combos[pos]
        val = (1.0 - OMEGA) * pulled[i] + bases[c[0]]
        if cv is not None:
            val = val + cv
        layers.append(jnp.where(fluid, val, pulled[OPPOSITE[i]]))
    sens = None
    for i in range(1, 19, 2):
        c = VELOCITIES[i]
        along = None
        for a in range(3):
            if c[a] == 0:
                continue
            if along is None:
                along = u[a] if c[a] > 0 else -u[a]
            else:
                along = along + u[a] if c[a] > 0 else along - u[a]
        term = (6.0 * WEIGHTS[i]) * along * (pulled[OPPOSITE[i]] - pulled[i])
        sens = term if sens is None else sens + term
    sens = jnp.where(fluid, rho * sens, 0.0)
    return layers, sens


def _kernel(dims, adj_hbm, rho_hbm, vel_hbm, mask_hbm, out_ref, sens_ref,
            adj_ref, rho_ref, vel_ref, mask_ref, load_sem,
            mid, fin, sfin, out_sem, xh, yh, exy, sy, sx, nt, mh, mt, send_sem, recv_sem):
    nx, ny, nz = dims
    cx, cy, cz = 8, 16, 128
    rows = cx * cy
    me = (lax.axis_index("gx"), lax.axis_index("gy"), lax.axis_index("gz"))
    sizes = (nx, ny, nz)

    def exists(d):
        cond = None
        for a in range(3):
            if d[a] == 0:
                continue
            v = me[a] + d[a]
            c = (v >= 0) if d[a] < 0 else (v < sizes[a])
            cond = c if cond is None else jnp.logical_and(cond, c)
        return cond

    def target(d):
        return tuple(me[a] + d[a] for a in range(3))

    loads = [
        pltpu.make_async_copy(src, dst, load_sem.at[k])
        for k, (src, dst) in enumerate(
            ((adj_hbm, adj_ref), (vel_hbm, vel_ref), (rho_hbm, rho_ref), (mask_hbm, mask_ref))
        )
    ]
    for copy in loads:
        copy.start()

    xh[...] = jnp.zeros(xh.shape, jnp.float32)
    yh[...] = jnp.zeros(yh.shape, jnp.float32)
    exy[...] = jnp.zeros(exy.shape, jnp.float32)
    mh[...] = jnp.zeros(mh.shape, jnp.float32)

    barrier = pltpu.get_barrier_semaphore()
    for d in NEIGHBOURS:
        @pl.when(exists(d))
        def _():
            pl.semaphore_signal(barrier, inc=1, device_id=target(d), device_id_type=MESH)

    lane = lax.broadcasted_iota(jnp.int32, (cy, cz), 1)
    lane1 = lax.broadcasted_iota(jnp.int32, (1, cz), 1)
    row = lax.broadcasted_iota(jnp.int32, (cy, cz), 0)
    lane_big = lax.broadcasted_iota(jnp.int32, (rows, cz), 1)

    msgs = _messages(cx, cy)

    def prepare(s, src):
        for side, pops, q in ((0, CXP, 0), (1, CXM, cx - 1)):
            for k, pop in enumerate(pops):
                sx[s, side, k] = src[pop, pl.ds(q * cy, cy), :]
        for side, pops, y in ((0, CYP, 0), (1, CYM, cy - 1)):
            for k, pop in enumerate(pops):
                sy[s, side, k] = src[pop, pl.ds(y, cx, stride=cy), :]
        n = jnp.zeros((rows, cz), jnp.float32)
        for j, (pop, z) in enumerate(ZCOLS):
            zz = z % cz
            n = jnp.where(lane_big == 8 * j, pltpu.roll(src[pop], (8 * j - zz) % cz, 1), n)
        nt[s] = n.T

    def descriptor(s, src, m, t):
        d, so, de = msgs[t]
        if so[0] == "S":
            sref = src.at[so[1], pl.ds(so[2] % rows, so[3]), :]
        elif so[0] == "SY":
            sref = sy.at[s, so[1]]
        elif so[0] == "SX":
            sref = sx.at[s, so[1]]
        else:
            sref = nt.at[s, pl.ds(so[1], so[2]), :]
        if de[0] == "XH":
            dref = xh.at[s, de[1]]
        elif de[0] == "YH":
            dref = yh.at[s, de[1]]
        elif de[0] == "EXY":
            dref = exy.at[s, de[1]]
        else:
            dref = mh.at[s, de[1], pl.ds(de[2], de[3]), :]
        return pltpu.make_async_remote_copy(
            src_ref=sref, dst_ref=dref, send_sem=send_sem.at[s, t], recv_sem=recv_sem.at[s, t],
            device_id=target(d), device_id_type=MESH)

    def send(s, src):
        for t in range(len(msgs)):
            d = msgs[t][0]

            @pl.when(exists(d))
            def _():
                descriptor(s, src, msgs, t).start()

    def finish(s, src):
        for t in range(len(msgs)):
            d = msgs[t][0]
            back = tuple(-v for v in d)

            @pl.when(exists(back))
            def _():
                descriptor(s, src, msgs, t).wait_recv()

            @pl.when(exists(d))
            def _():
                descriptor(s, src, msgs, t).wait_send()
        for side in range(2):
            mt[s, side] = mh[s, side].T

    def pulled_plane(s, src, p):
        out = []
        for i in range(19):
            vx, vy, vz = VELOCITIES[i]
            q = p + vx
            if 0 <= q < cx:
                plane = src[i, pl.ds(q * cy, cy), :]
            elif q == cx:
                plane = xh[s, 1, CXP.index(i)]
            else:
                plane = xh[s, 0, CXM.index(i)]
            if vz != 0:
                side = 1 if vz > 0 else 0
                if 0 <= q < cx:
                    zc = mt[s, side, pl.ds(q * cy, cy), :]
                    col = ZFACE_COL[i]
                else:
                    col, r0 = XZ_EDGE[i]
                    zc = mt[s, side, pl.ds(r0 % rows, cy), :]
                if vz > 0:
                    plane = jnp.where(lane == cz - 1, pltpu.roll(zc, (cz - 1 - col) % cz, 1),
                                      pltpu.roll(plane, cz - 1, 1))
                else:
                    plane = jnp.where(lane == 0, pltpu.roll(zc, (cz - col) % cz, 1),
                                      pltpu.roll(plane, 1, 1))
            if vy != 0:
                side_y = 1 if vy > 0 else 0
                ky = CYP.index(i) if vy > 0 else CYM.index(i)
                if 0 <= q < cx:
                    yrow = yh[s, side_y, ky, pl.ds(q, 1), :]
                else:
                    e, r = XY_EDGE[i]
                    yrow = exy[s, e, pl.ds(r, 1), :]
                if vz != 0:
                    side = 1 if vz > 0 else 0
                    colc, yoff = YZ_CORNER[i]
                    crow = mt[s, side, pl.ds(p * cy + yoff % cy, 1), :]
                    if vz > 0:
                        yrow = jnp.where(lane1 == cz - 1, pltpu.roll(crow, (cz - 1 - colc) % cz, 1),
                                         pltpu.roll(yrow, cz - 1, 1))
                    else:
                        yrow = jnp.where(lane1 == 0, pltpu.roll(crow, (cz - colc) % cz, 1),
                                         pltpu.roll(yrow, 1, 1))
                if vy > 0:
                    plane = jnp.where(row == cy - 1, yrow, pltpu.roll(plane, cy - 1, 0))
                else:
                    plane = jnp.where(row == 0, yrow, pltpu.roll(plane, 1, 0))
            out.append(plane)
        return out

    def flush(p):
        rs = pl.ds(p * cy, cy)
        pltpu.make_async_copy(fin.at[:, rs, :], out_ref.at[:, rs, :], out_sem.at[p]).start()

    def step(s, src, dst, level):
        for p in range(cx):
            if s == 1 and p >= 1:
                flush(p - 1)
            rs = pl.ds(p * cy, cy)
            pulled = pulled_plane(s, src, p)
            rho = rho_ref[level, rs, :]
            ux = vel_ref[level, 0, rs, :]
            uy = vel_ref[level, 1, rs, :]
            uz = vel_ref[level, 2, rs, :]
            fluid = mask_ref[rs, :] > 0
            layers, sens = _collide(pulled, rho, ux, uy, uz, fluid)
            for i in range(19):
                dst[i, rs, :] = layers[i]
            if s == 0:
                sfin[rs, :] = sens
            else:
                sfin[rs, :] = sfin[rs, :] + sens

    def indicator(a, off):
        n = sizes[a]
        if off < 0:
            return (me[a] + n - 1) // n
        if off > 0:
            return (2 * n - 2 - me[a]) // n
        return 1

    peers = 0
    for d in NEIGHBOURS:
        term = 1
        for a in range(3):
            term = term * indicator(a, d[a])
        peers = peers + term
    loads[0].wait()
    prepare(0, adj_ref)
    pl.semaphore_wait(barrier, peers)
    send(0, adj_ref)
    for copy in loads[1:]:
        copy.wait()
    finish(0, adj_ref)
    step(0, adj_ref, mid, 1)
    prepare(1, mid)
    send(1, mid)
    finish(1, mid)
    step(1, mid, fin, 0)
    flush(cx - 1)
    sens_copy = pltpu.make_async_copy(sfin, sens_ref, out_sem.at[cx])
    sens_copy.start()
    for p in range(cx):
        rs = pl.ds(p * cy, cy)
        pltpu.make_async_copy(fin.at[:, rs, :], out_ref.at[:, rs, :], out_sem.at[p]).wait()
    sens_copy.wait()


def _writer(chunks, part_hbm, sens_hbm, out_hbm, sens_out, sems):
    npop = part_hbm.shape[0]
    step = -(-npop // chunks)
    spans = [(k, min(k + step, npop)) for k in range(0, npop, step)]
    copies = [
        pltpu.make_async_copy(part_hbm.at[pl.ds(a, b - a)], out_hbm.at[pl.ds(a, b - a)], sems.at[j])
        for j, (a, b) in enumerate(spans)
    ]
    copies.append(pltpu.make_async_copy(sens_hbm, sens_out, sems.at[len(spans)]))
    for copy in copies:
        copy.start()
    for copy in copies:
        copy.wait()


def _write_out(part, sens, chunks=8):
    npop, rows, cz = part.shape
    nspan = len(range(0, npop, -(-npop // chunks)))
    hbm = pl.BlockSpec(memory_space=pltpu.HBM)
    return pl.pallas_call(
        functools.partial(_writer, chunks),
        out_shape=(
            jax.ShapeDtypeStruct(part.shape, jnp.float32),
            jax.ShapeDtypeStruct(sens.shape, jnp.float32),
        ),
        in_specs=[hbm, hbm],
        out_specs=(hbm, hbm),
        scratch_shapes=[pltpu.SemaphoreType.DMA((nspan + 1,))],
        compiler_params=pltpu.CompilerParams(vmem_limit_bytes=67043328),
    )(part, sens)


def solution(mesh):
    nx, ny, nz = mesh.shape["gx"], mesh.shape["gy"], mesh.shape["gz"]
    nmsg = len(_messages(8, 16))

    def shards(adjoint, density, velocity, pore_mask):
        npop, cx, cy, cz = adjoint.shape
        assert (cx, cy, cz) == (8, 16, 128)
        rows = cx * cy
        adj = adjoint.reshape(npop, rows, cz)
        rho = density.reshape(2, rows, cz)
        vel = velocity.reshape(2, 3, rows, cz)
        mask = pore_mask.reshape(rows, cz)
        vspec = pl.BlockSpec(memory_space=pltpu.VMEM)
        out, sens = pl.pallas_call(
            functools.partial(_kernel, (nx, ny, nz)),
            out_shape=(
                jax.ShapeDtypeStruct((npop, rows, cz), jnp.float32),
                jax.ShapeDtypeStruct((rows, cz), jnp.float32),
            ),
            in_specs=[pl.BlockSpec(memory_space=pltpu.HBM)] * 4,
            out_specs=(pl.BlockSpec(memory_space=pltpu.HBM), pl.BlockSpec(memory_space=pltpu.HBM)),
            scratch_shapes=[
                pltpu.VMEM((npop, rows, cz), jnp.float32),
                pltpu.VMEM((2, rows, cz), jnp.float32),
                pltpu.VMEM((2, 3, rows, cz), jnp.float32),
                pltpu.VMEM((rows, cz), jnp.int32),
                pltpu.SemaphoreType.DMA((4,)),
                pltpu.VMEM((npop, rows, cz), jnp.float32),
                pltpu.VMEM((npop, rows, cz), jnp.float32),
                pltpu.VMEM((rows, cz), jnp.float32),
                pltpu.SemaphoreType.DMA((cx + 1,)),
                pltpu.VMEM((2, 2, 5, cy, cz), jnp.float32),
                pltpu.VMEM((2, 2, 5, cx, cz), jnp.float32),
                pltpu.VMEM((2, 4, 8, cz), jnp.float32),
                pltpu.VMEM((2, 2, 5, cx, cz), jnp.float32),
                pltpu.VMEM((2, 2, 5, cy, cz), jnp.float32),
                pltpu.VMEM((2, rows, cz), jnp.float32),
                pltpu.VMEM((2, 2, rows, cz), jnp.float32),
                pltpu.VMEM((2, 2, rows, cz), jnp.float32),
                pltpu.SemaphoreType.DMA((2, nmsg)),
                pltpu.SemaphoreType.DMA((2, nmsg)),
            ],
            compiler_params=pltpu.CompilerParams(
                collective_id=0, has_side_effects=True, vmem_limit_bytes=67043328
            ),
        )(adj, rho, vel, mask)
        out, sens = _write_out(out, sens)
        return out.reshape(npop, cx, cy, cz), sens.reshape(cx, cy, cz)

    placed = (
        P(None, "gx", "gy", "gz"),
        P(None, "gx", "gy", "gz"),
        P(None, None, "gx", "gy", "gz"),
        P("gx", "gy", "gz"),
    )
    return jax.shard_map(
        shards,
        mesh=mesh,
        in_specs=placed,
        out_specs=(P(None, "gx", "gy", "gz"), P("gx", "gy", "gz")),
        check_vma=False,
    )
```

```python
import functools

import jax
import jax.numpy as jnp
from jax import lax
from jax.experimental import pallas as pl
from jax.experimental.pallas import tpu as pltpu
from jax.sharding import PartitionSpec as P

VELOCITIES = [
    (0, 0, 0),
    (1, 0, 0),
    (-1, 0, 0),
    (0, 1, 0),
    (0, -1, 0),
    (0, 0, 1),
    (0, 0, -1),
    (1, 1, 0),
    (-1, -1, 0),
    (1, -1, 0),
    (-1, 1, 0),
    (1, 0, 1),
    (-1, 0, -1),
    (1, 0, -1),
    (-1, 0, 1),
    (0, 1, 1),
    (0, -1, -1),
    (0, 1, -1),
    (0, -1, 1),
]
WEIGHTS = [1.0 / 3.0] + [1.0 / 18.0] * 6 + [1.0 / 36.0] * 12
OPPOSITE = [0, 2, 1, 4, 3, 6, 5, 8, 7, 10, 9, 12, 11, 14, 13, 16, 15, 18, 17]
OMEGA = 1.25
MESH = pl.DeviceIdType.MESH

CXP = [1, 7, 9, 11, 13]
CXM = [2, 8, 10, 12, 14]
CYP = [3, 7, 10, 15, 17]
CYM = [4, 8, 9, 16, 18]
ZCOLS = [(5, 0), (11, 0), (14, 0), (15, 0), (18, 0), (6, -1), (12, -1), (13, -1), (16, -1), (17, -1)]
ZFACE_COL = {5: 0, 11: 8, 14: 16, 15: 24, 18: 32, 6: 0, 12: 8, 13: 16, 16: 24, 17: 32}
XZ_EDGE = {11: (40, 0), 14: (48, -16), 12: (40, -16), 13: (48, 0)}
YZ_CORNER = {15: (56, 0), 18: (64, -1), 16: (56, -1), 17: (64, 0)}
XY_EDGE = {7: (0, 0), 8: (1, 7), 9: (2, 7), 10: (3, 0)}


def _messages(cx, cy):
    rows = cx * cy
    msgs = []
    msgs.append(((0, -1, 0), ("SY", 0), ("YH", 1)))
    msgs.append(((0, 1, 0), ("SY", 1), ("YH", 0)))
    msgs.append(((0, -1, -1), ("NT", 24, 8), ("MH", 1, 56, 8)))
    msgs.append(((0, 1, -1), ("NT", 32, 8), ("MH", 1, 64, 8)))
    msgs.append(((0, 1, 1), ("NT", 64, 8), ("MH", 0, 56, 8)))
    msgs.append(((0, -1, 1), ("NT", 72, 8), ("MH", 0, 64, 8)))
    msgs.append(((-1, -1, 0), ("S", 7, 0, 8), ("EXY", 0)))
    msgs.append(((1, 1, 0), ("S", 8, rows - 8, 8), ("EXY", 1)))
    msgs.append(((-1, 1, 0), ("S", 9, cy - 8, 8), ("EXY", 2)))
    msgs.append(((1, -1, 0), ("S", 10, rows - cy, 8), ("EXY", 3)))
    msgs.append(((0, 0, -1), ("NT", 0, 40), ("MH", 1, 0, 40)))
    msgs.append(((0, 0, 1), ("NT", 40, 40), ("MH", 0, 0, 40)))
    msgs.append(((-1, 0, -1), ("NT", 8, 8), ("MH", 1, 40, 8)))
    msgs.append(((1, 0, -1), ("NT", 16, 8), ("MH", 1, 48, 8)))
    msgs.append(((1, 0, 1), ("NT", 48, 8), ("MH", 0, 40, 8)))
    msgs.append(((-1, 0, 1), ("NT", 56, 8), ("MH", 0, 48, 8)))
    msgs.append(((-1, 0, 0), ("SX", 0), ("XH", 1)))
    msgs.append(((1, 0, 0), ("SX", 1), ("XH", 0)))
    return msgs


NEIGHBOURS = sorted(
    {d for d, _, _ in _messages(8, 16)} | {tuple(-v for v in d) for d, _, _ in _messages(8, 16)}
)


def _comb(vals, fn):
    total = None
    for weight in (1.0 / 3.0, 1.0 / 18.0, 1.0 / 36.0):
        part = None
        for i in range(19):
            if WEIGHTS[i] != weight:
                continue
            k = fn(VELOCITIES[i])
            if k == 0:
                continue
            if part is None:
                part = vals[i] if k > 0 else -vals[i]
            else:
                part = part + vals[i] if k > 0 else part - vals[i]
        if part is not None:
            term = part * weight
            total = term if total is None else total + term
    return total


def _collide(pulled, rho, ux, uy, uz, fluid):
    p0 = _comb(pulled, lambda c: 1)
    p1 = [_comb(pulled, lambda c, a=a: c[a]) for a in range(3)]
    q = {}
    for a in range(3):
        for b in range(a, 3):
            q[a, b] = _comb(pulled, lambda c, a=a, b=b: c[a] * c[b])
            q[b, a] = q[a, b]
    u = (ux, uy, uz)
    usq = ux * ux + uy * uy + uz * uz
    qu = [q[a, 0] * ux + q[a, 1] * uy + q[a, 2] * uz for a in range(3)]
    p1u = p1[0] * ux + p1[1] * uy + p1[2] * uz
    uqu = ux * qu[0] + uy * qu[1] + uz * qu[2]
    moment = p0 * (1.0 - 1.5 * usq) + 3.0 * p1u + 4.5 * uqu
    vec = [3.0 * p1[a] + 9.0 * qu[a] - 3.0 * u[a] * p0 for a in range(3)]
    vu = vec[0] * ux + vec[1] * uy + vec[2] * uz
    inv = 1.0 / rho
    base = OMEGA * (moment - vu) - ux * inv
    bases = {0: base, 1: base + inv, -1: base - inv}
    wv = [OMEGA * v for v in vec]
    combos = {}
    layers = []
    for i in range(19):
        c = VELOCITIES[i]
        key = tuple(c)
        terms = [(a, c[a]) for a in range(3) if c[a] != 0]
        cv = None
        if terms:
            if len(terms) == 1:
                a, s = terms[0]
                cv = wv[a] if s > 0 else -wv[a]
            else:
                (a, s), (b, t) = terms
                pos = (a, b, s * t)
                if pos not in combos:
                    combos[pos] = wv[a] + wv[b] if s * t > 0 else wv[a] - wv[b]
                cv = combos[pos] if s > 0 else -combos[pos]
        val = (1.0 - OMEGA) * pulled[i] + bases[c[0]]
        if cv is not None:
            val = val + cv
        layers.append(jnp.where(fluid, val, pulled[OPPOSITE[i]]))
    sens = None
    for i in range(1, 19, 2):
        c = VELOCITIES[i]
        along = None
        for a in range(3):
            if c[a] == 0:
                continue
            if along is None:
                along = u[a] if c[a] > 0 else -u[a]
            else:
                along = along + u[a] if c[a] > 0 else along - u[a]
        term = (6.0 * WEIGHTS[i]) * along * (pulled[OPPOSITE[i]] - pulled[i])
        sens = term if sens is None else sens + term
    sens = jnp.where(fluid, rho * sens, 0.0)
    return layers, sens


def _where(dims):
    me = (lax.axis_index("gx"), lax.axis_index("gy"), lax.axis_index("gz"))

    def exists(d):
        cond = None
        for a in range(3):
            if d[a] == 0:
                continue
            v = me[a] + d[a]
            c = (v >= 0) if d[a] < 0 else (v < dims[a])
            cond = c if cond is None else jnp.logical_and(cond, c)
        return cond

    def target(d):
        return tuple(me[a] + d[a] for a in range(3))

    return me, exists, target


def _zero_missing(exists, xh, yh, exy, mh):
    for d, so, de in _messages(8, 16):
        back = tuple(-v for v in d)

        @pl.when(jnp.logical_not(exists(back)))
        def _():
            if de[0] == "XH":
                xh[de[1]] = jnp.zeros(xh.shape[1:], jnp.float32)
            elif de[0] == "YH":
                yh[de[1]] = jnp.zeros(yh.shape[1:], jnp.float32)
            elif de[0] == "EXY":
                exy[de[1]] = jnp.zeros(exy.shape[1:], jnp.float32)
            else:
                mh[de[1], pl.ds(de[2], de[3]), :] = jnp.zeros((de[3], mh.shape[-1]), jnp.float32)


def _step(s, src, xh, yh, exy, mt, rho_ref, vel_ref, mask_ref, level, emit, before=None):
    cx, cy, cz = 8, 16, 128
    lane = lax.broadcasted_iota(jnp.int32, (cy, cz), 1)
    lane1 = lax.broadcasted_iota(jnp.int32, (1, cz), 1)
    row = lax.broadcasted_iota(jnp.int32, (cy, cz), 0)

    def pulled_plane(p):
        out = []
        for i in range(19):
            vx, vy, vz = VELOCITIES[i]
            q = p + vx
            if 0 <= q < cx:
                plane = src[i, pl.ds(q * cy, cy), :]
            elif q == cx:
                plane = xh[s, 1, CXP.index(i)]
            else:
                plane = xh[s, 0, CXM.index(i)]
            if vz != 0:
                side = 1 if vz > 0 else 0
                if 0 <= q < cx:
                    zc = mt[s, side, pl.ds(q * cy, cy), :]
                    col = ZFACE_COL[i]
                else:
                    col, r0 = XZ_EDGE[i]
                    zc = mt[s, side, pl.ds(r0 % (cx * cy), cy), :]
                if vz > 0:
                    plane = jnp.where(lane == cz - 1, pltpu.roll(zc, (cz - 1 - col) % cz, 1),
                                      pltpu.roll(plane, cz - 1, 1))
                else:
                    plane = jnp.where(lane == 0, pltpu.roll(zc, (cz - col) % cz, 1),
                                      pltpu.roll(plane, 1, 1))
            if vy != 0:
                side_y = 1 if vy > 0 else 0
                ky = CYP.index(i) if vy > 0 else CYM.index(i)
                if 0 <= q < cx:
                    yrow = yh[s, side_y, ky, pl.ds(q, 1), :]
                else:
                    e, r = XY_EDGE[i]
                    yrow = exy[s, e, pl.ds(r, 1), :]
                if vz != 0:
                    side = 1 if vz > 0 else 0
                    colc, yoff = YZ_CORNER[i]
                    crow = mt[s, side, pl.ds(p * cy + yoff % cy, 1), :]
                    if vz > 0:
                        yrow = jnp.where(lane1 == cz - 1, pltpu.roll(crow, (cz - 1 - colc) % cz, 1),
                                         pltpu.roll(yrow, cz - 1, 1))
                    else:
                        yrow = jnp.where(lane1 == 0, pltpu.roll(crow, (cz - colc) % cz, 1),
                                         pltpu.roll(yrow, 1, 1))
                if vy > 0:
                    plane = jnp.where(row == cy - 1, yrow, pltpu.roll(plane, cy - 1, 0))
                else:
                    plane = jnp.where(row == 0, yrow, pltpu.roll(plane, 1, 0))
            out.append(plane)
        return out

    for p in range(cx):
        if before is not None:
            before(p)
        rs = pl.ds(p * cy, cy)
        pulled = pulled_plane(p)
        rho = rho_ref[level, rs, :]
        ux = vel_ref[level, 0, rs, :]
        uy = vel_ref[level, 1, rs, :]
        uz = vel_ref[level, 2, rs, :]
        fluid = mask_ref[rs, :] > 0
        layers, sens = _collide(pulled, rho, ux, uy, uz, fluid)
        emit(p, rs, layers, sens)


def _kernel(dims, adj_hbm, rho_hbm, vel_hbm, mask_hbm,
            mid_out, sens_out, xh_out, yh_out, exy_out, mh_out,
            adj_ref, rho_ref, vel_ref, mask_ref, load_sem,
            mid, sfin, out_sem, xh, yh, exy, sy, sx, nt, mh, mt, send_sem, recv_sem):
    cx, cy, cz = 8, 16, 128
    rows = cx * cy
    me, exists, target = _where(dims)

    barrier = pltpu.get_barrier_semaphore()
    for d in NEIGHBOURS:
        @pl.when(exists(d))
        def _():
            pl.semaphore_signal(barrier, inc=1, device_id=target(d), device_id_type=MESH)

    loads = [
        pltpu.make_async_copy(src, dst, load_sem.at[k])
        for k, (src, dst) in enumerate(
            ((adj_hbm, adj_ref), (vel_hbm, vel_ref), (rho_hbm, rho_ref), (mask_hbm, mask_ref))
        )
    ]
    for copy in loads:
        copy.start()

    mh[0, :, pl.ds(72, rows - 72), :] = jnp.zeros((2, rows - 72, cz), jnp.float32)
    _zero_missing(exists, xh.at[0], yh.at[0], exy.at[0], mh.at[0])

    lane_big = lax.broadcasted_iota(jnp.int32, (rows, cz), 1)
    msgs = _messages(cx, cy)

    def prepare(s, src):
        for side, pops, q in ((0, CXP, 0), (1, CXM, cx - 1)):
            for k, pop in enumerate(pops):
                sx[s, side, k] = src[pop, pl.ds(q * cy, cy), :]
        for side, pops, y in ((0, CYP, 0), (1, CYM, cy - 1)):
            for k, pop in enumerate(pops):
                sy[s, side, k] = src[pop, pl.ds(y, cx, stride=cy), :]
        n = jnp.zeros((rows, cz), jnp.float32)
        for j, (pop, z) in enumerate(ZCOLS):
            zz = z % cz
            n = jnp.where(lane_big == 8 * j, pltpu.roll(src[pop], (8 * j - zz) % cz, 1), n)
        nt[s] = n.T

    def descriptor(s, src, t):
        d, so, de = msgs[t]
        if so[0] == "S":
            sref = src.at[so[1], pl.ds(so[2] % rows, so[3]), :]
        elif so[0] == "SY":
            sref = sy.at[s, so[1]]
        elif so[0] == "SX":
            sref = sx.at[s, so[1]]
        else:
            sref = nt.at[s, pl.ds(so[1], so[2]), :]
        bufs = {"XH": (xh.at[0], xh_out), "YH": (yh.at[0], yh_out), "EXY": (exy.at[0], exy_out),
                "MH": (mh.at[0], mh_out)}[de[0]][s]
        if de[0] == "MH":
            dref = bufs.at[de[1], pl.ds(de[2], de[3]), :]
        else:
            dref = bufs.at[de[1]]
        return pltpu.make_async_remote_copy(
            src_ref=sref, dst_ref=dref, send_sem=send_sem.at[s, t], recv_sem=recv_sem.at[s, t],
            device_id=target(d), device_id_type=MESH)

    def send(s, src):
        for t in range(len(msgs)):
            @pl.when(exists(msgs[t][0]))
            def _():
                descriptor(s, src, t).start()

    def finish(s, src):
        for t in range(len(msgs)):
            d = msgs[t][0]
            back = tuple(-v for v in d)

            @pl.when(exists(back))
            def _():
                descriptor(s, src, t).wait_recv()

            @pl.when(exists(d))
            def _():
                descriptor(s, src, t).wait_send()

    peers = 0
    for d in NEIGHBOURS:
        term = 1
        for a in range(3):
            n = dims[a]
            if d[a] < 0:
                term = term * ((me[a] + n - 1) // n)
            elif d[a] > 0:
                term = term * ((2 * n - 2 - me[a]) // n)
        peers = peers + term
    loads[0].wait()
    prepare(0, adj_ref)
    pl.semaphore_wait(barrier, peers)
    send(0, adj_ref)
    for copy in loads[1:]:
        copy.wait()
    finish(0, adj_ref)
    for side in range(2):
        mt[0, side] = mh[0, side].T

    def flush(p):
        rs = pl.ds(p * cy, cy)
        pltpu.make_async_copy(mid.at[:, rs, :], mid_out.at[:, rs, :], out_sem.at[p]).start()

    def emit(p, rs, layers, sens):
        for i in range(19):
            mid[i, rs, :] = layers[i]
        sfin[rs, :] = sens

    _step(0, adj_ref, xh, yh, exy, mt, rho_ref, vel_ref, mask_ref, 1, emit,
          before=lambda p: flush(p - 1) if p >= 1 else None)
    flush(cx - 1)
    sens_copy = pltpu.make_async_copy(sfin, sens_out, out_sem.at[cx])
    sens_copy.start()
    prepare(1, mid)
    send(1, mid)
    finish(1, mid)
    for p in range(cx):
        rs = pl.ds(p * cy, cy)
        pltpu.make_async_copy(mid.at[:, rs, :], mid_out.at[:, rs, :], out_sem.at[p]).wait()
    sens_copy.wait()


def _last(dims, mid_hbm, s1_hbm, xh_hbm, yh_hbm, exy_hbm, mh_hbm, rho_hbm, vel_hbm, mask_hbm,
          out_hbm, sens_hbm,
          mid, s1, xh, yh, exy, mh, mt, rho, vel, mask, fin, sfin, in_sem, out_sem):
    cx, cy, cz = 8, 16, 128
    rows = cx * cy
    me, exists, target = _where(dims)
    mh[...] = jnp.zeros(mh.shape, jnp.float32)
    used = 72
    loads = [
        pltpu.make_async_copy(xh_hbm, xh.at[0], in_sem.at[0]),
        pltpu.make_async_copy(yh_hbm, yh.at[0], in_sem.at[1]),
        pltpu.make_async_copy(exy_hbm, exy.at[0], in_sem.at[2]),
        pltpu.make_async_copy(mh_hbm.at[:, pl.ds(0, used), :], mh.at[:, pl.ds(0, used), :], in_sem.at[3]),
        pltpu.make_async_copy(rho_hbm.at[pl.ds(0, 1)], rho, in_sem.at[4]),
        pltpu.make_async_copy(vel_hbm.at[pl.ds(0, 1)], vel, in_sem.at[5]),
        pltpu.make_async_copy(mask_hbm, mask, in_sem.at[6]),
        pltpu.make_async_copy(s1_hbm, s1, in_sem.at[7]),
        pltpu.make_async_copy(mid_hbm, mid, in_sem.at[8]),
    ]
    for copy in loads:
        copy.start()
    for copy in loads:
        copy.wait()
    _zero_missing(exists, xh.at[0], yh.at[0], exy.at[0], mh)

    for side in range(2):
        mt[0, side] = mh[side].T

    def flush(p):
        rs = pl.ds(p * cy, cy)
        pltpu.make_async_copy(fin.at[:, rs, :], out_hbm.at[:, rs, :], out_sem.at[p]).start()

    def emit(p, rs, layers, sens):
        for i in range(19):
            fin[i, rs, :] = layers[i]
        sfin[rs, :] = s1[rs, :] + sens

    _step(0, mid, xh, yh, exy, mt, rho, vel, mask, 0, emit,
          before=lambda p: flush(p - 1) if p >= 1 else None)
    flush(cx - 1)
    sens_copy = pltpu.make_async_copy(sfin, sens_hbm, out_sem.at[cx])
    sens_copy.start()
    for p in range(cx):
        rs = pl.ds(p * cy, cy)
        pltpu.make_async_copy(fin.at[:, rs, :], out_hbm.at[:, rs, :], out_sem.at[p]).wait()
    sens_copy.wait()


def solution(mesh):
    dims = (mesh.shape["gx"], mesh.shape["gy"], mesh.shape["gz"])
    nmsg = len(_messages(8, 16))

    def shards(adjoint, density, velocity, pore_mask):
        npop, cx, cy, cz = adjoint.shape
        assert (cx, cy, cz) == (8, 16, 128)
        rows = cx * cy
        adj = adjoint.reshape(npop, rows, cz)
        rho = density.reshape(2, rows, cz)
        vel = velocity.reshape(2, 3, rows, cz)
        mask = pore_mask.reshape(rows, cz)
        hbm = pl.BlockSpec(memory_space=pltpu.HBM)
        f32 = jnp.float32
        halo_shapes = (
            jax.ShapeDtypeStruct((2, 5, cy, cz), f32),
            jax.ShapeDtypeStruct((2, 5, cx, cz), f32),
            jax.ShapeDtypeStruct((4, 8, cz), f32),
            jax.ShapeDtypeStruct((2, rows, cz), f32),
        )
        mid, s1, xh2, yh2, exy2, mh2 = pl.pallas_call(
            functools.partial(_kernel, dims),
            out_shape=(
                jax.ShapeDtypeStruct((npop, rows, cz), f32),
                jax.ShapeDtypeStruct((rows, cz), f32),
            ) + halo_shapes,
            in_specs=[hbm] * 4,
            out_specs=(hbm,) * 6,
            scratch_shapes=[
                pltpu.VMEM((npop, rows, cz), f32),
                pltpu.VMEM((2, rows, cz), f32),
                pltpu.VMEM((2, 3, rows, cz), f32),
                pltpu.VMEM((rows, cz), jnp.int32),
                pltpu.SemaphoreType.DMA((4,)),
                pltpu.VMEM((npop, rows, cz), f32),
                pltpu.VMEM((rows, cz), f32),
                pltpu.SemaphoreType.DMA((cx + 1,)),
                pltpu.VMEM((1, 2, 5, cy, cz), f32),
                pltpu.VMEM((1, 2, 5, cx, cz), f32),
                pltpu.VMEM((1, 4, 8, cz), f32),
                pltpu.VMEM((2, 2, 5, cx, cz), f32),
                pltpu.VMEM((2, 2, 5, cy, cz), f32),
                pltpu.VMEM((2, rows, cz), f32),
                pltpu.VMEM((1, 2, rows, cz), f32),
                pltpu.VMEM((1, 2, rows, cz), f32),
                pltpu.SemaphoreType.DMA((2, nmsg)),
                pltpu.SemaphoreType.DMA((2, nmsg)),
            ],
            compiler_params=pltpu.CompilerParams(
                collective_id=0, has_side_effects=True, vmem_limit_bytes=67043328
            ),
        )(adj, rho, vel, mask)
        out, sens = pl.pallas_call(
            functools.partial(_last, dims),
            out_shape=(
                jax.ShapeDtypeStruct((npop, rows, cz), f32),
                jax.ShapeDtypeStruct((rows, cz), f32),
            ),
            in_specs=[hbm] * 9,
            out_specs=(hbm, hbm),
            scratch_shapes=[
                pltpu.VMEM((npop, rows, cz), f32),
                pltpu.VMEM((rows, cz), f32),
                pltpu.VMEM((1, 2, 5, cy, cz), f32),
                pltpu.VMEM((1, 2, 5, cx, cz), f32),
                pltpu.VMEM((1, 4, 8, cz), f32),
                pltpu.VMEM((2, rows, cz), f32),
                pltpu.VMEM((1, 2, rows, cz), f32),
                pltpu.VMEM((1, rows, cz), f32),
                pltpu.VMEM((1, 3, rows, cz), f32),
                pltpu.VMEM((rows, cz), jnp.int32),
                pltpu.VMEM((npop, rows, cz), f32),
                pltpu.VMEM((rows, cz), f32),
                pltpu.SemaphoreType.DMA((9,)),
                pltpu.SemaphoreType.DMA((cx + 1,)),
            ],
            compiler_params=pltpu.CompilerParams(vmem_limit_bytes=67043328),
        )(mid, s1, xh2, yh2, exy2, mh2, rho, vel, mask)
        return out.reshape(npop, cx, cy, cz), sens.reshape(cx, cy, cz)

    placed = (
        P(None, "gx", "gy", "gz"),
        P(None, "gx", "gy", "gz"),
        P(None, None, "gx", "gy", "gz"),
        P("gx", "gy", "gz"),
    )
    return jax.shard_map(
        shards,
        mesh=mesh,
        in_specs=placed,
        out_specs=(P(None, "gx", "gy", "gz"), P("gx", "gy", "gz")),
        check_vma=False,
    )
```

```python
import functools

import jax
import jax.numpy as jnp
from jax import lax
from jax.experimental import pallas as pl
from jax.experimental.pallas import tpu as pltpu
from jax.sharding import PartitionSpec as P

VELOCITIES = [
    (0, 0, 0),
    (1, 0, 0),
    (-1, 0, 0),
    (0, 1, 0),
    (0, -1, 0),
    (0, 0, 1),
    (0, 0, -1),
    (1, 1, 0),
    (-1, -1, 0),
    (1, -1, 0),
    (-1, 1, 0),
    (1, 0, 1),
    (-1, 0, -1),
    (1, 0, -1),
    (-1, 0, 1),
    (0, 1, 1),
    (0, -1, -1),
    (0, 1, -1),
    (0, -1, 1),
]
WEIGHTS = [1.0 / 3.0] + [1.0 / 18.0] * 6 + [1.0 / 36.0] * 12
OPPOSITE = [0, 2, 1, 4, 3, 6, 5, 8, 7, 10, 9, 12, 11, 14, 13, 16, 15, 18, 17]
OMEGA = 1.25
MESH = pl.DeviceIdType.MESH

CXP = [1, 7, 9, 11, 13]
CXM = [2, 8, 10, 12, 14]
CYP = [3, 7, 10, 15, 17]
CYM = [4, 8, 9, 16, 18]
ZCOLS = [(5, 0), (11, 0), (14, 0), (15, 0), (18, 0), (6, -1), (12, -1), (13, -1), (16, -1), (17, -1)]
ZFACE_COL = {5: 0, 11: 8, 14: 16, 15: 24, 18: 32, 6: 0, 12: 8, 13: 16, 16: 24, 17: 32}
XZ_EDGE = {11: (40, 0), 14: (48, -16), 12: (40, -16), 13: (48, 0)}
YZ_CORNER = {15: (56, 0), 18: (64, -1), 16: (56, -1), 17: (64, 0)}
XY_EDGE = {7: (0, 0), 8: (1, 7), 9: (2, 7), 10: (3, 0)}


def _messages(cx, cy):
    rows = cx * cy
    msgs = []
    msgs.append(((0, -1, 0), ("SY", 0), ("YH", 1)))
    msgs.append(((0, 1, 0), ("SY", 1), ("YH", 0)))
    msgs.append(((0, -1, -1), ("NT", 24, 8), ("MH", 1, 56, 8)))
    msgs.append(((0, 1, -1), ("NT", 32, 8), ("MH", 1, 64, 8)))
    msgs.append(((0, 1, 1), ("NT", 64, 8), ("MH", 0, 56, 8)))
    msgs.append(((0, -1, 1), ("NT", 72, 8), ("MH", 0, 64, 8)))
    msgs.append(((-1, -1, 0), ("S", 7, 0, 8), ("EXY", 0)))
    msgs.append(((1, 1, 0), ("S", 8, rows - 8, 8), ("EXY", 1)))
    msgs.append(((-1, 1, 0), ("S", 9, cy - 8, 8), ("EXY", 2)))
    msgs.append(((1, -1, 0), ("S", 10, rows - cy, 8), ("EXY", 3)))
    msgs.append(((0, 0, -1), ("NT", 0, 40), ("MH", 1, 0, 40)))
    msgs.append(((0, 0, 1), ("NT", 40, 40), ("MH", 0, 0, 40)))
    msgs.append(((-1, 0, -1), ("NT", 8, 8), ("MH", 1, 40, 8)))
    msgs.append(((1, 0, -1), ("NT", 16, 8), ("MH", 1, 48, 8)))
    msgs.append(((1, 0, 1), ("NT", 48, 8), ("MH", 0, 40, 8)))
    msgs.append(((-1, 0, 1), ("NT", 56, 8), ("MH", 0, 48, 8)))
    msgs.append(((-1, 0, 0), ("SX", 0), ("XH", 1)))
    msgs.append(((1, 0, 0), ("SX", 1), ("XH", 0)))
    return msgs


NEIGHBOURS = sorted(
    {d for d, _, _ in _messages(8, 16)} | {tuple(-v for v in d) for d, _, _ in _messages(8, 16)}
)


def _comb(vals, fn):
    total = None
    for weight in (1.0 / 3.0, 1.0 / 18.0, 1.0 / 36.0):
        part = None
        for i in range(19):
            if WEIGHTS[i] != weight:
                continue
            k = fn(VELOCITIES[i])
            if k == 0:
                continue
            if part is None:
                part = vals[i] if k > 0 else -vals[i]
            else:
                part = part + vals[i] if k > 0 else part - vals[i]
        if part is not None:
            term = part * weight
            total = term if total is None else total + term
    return total


def _collide(pulled, rho, ux, uy, uz, fluid):
    p0 = _comb(pulled, lambda c: 1)
    p1 = [_comb(pulled, lambda c, a=a: c[a]) for a in range(3)]
    q = {}
    for a in range(3):
        for b in range(a, 3):
            q[a, b] = _comb(pulled, lambda c, a=a, b=b: c[a] * c[b])
            q[b, a] = q[a, b]
    u = (ux, uy, uz)
    usq = ux * ux + uy * uy + uz * uz
    qu = [q[a, 0] * ux + q[a, 1] * uy + q[a, 2] * uz for a in range(3)]
    p1u = p1[0] * ux + p1[1] * uy + p1[2] * uz
    uqu = ux * qu[0] + uy * qu[1] + uz * qu[2]
    moment = p0 * (1.0 - 1.5 * usq) + 3.0 * p1u + 4.5 * uqu
    vec = [3.0 * p1[a] + 9.0 * qu[a] - 3.0 * u[a] * p0 for a in range(3)]
    vu = vec[0] * ux + vec[1] * uy + vec[2] * uz
    inv = 1.0 / rho
    base = OMEGA * (moment - vu) - ux * inv
    bases = {0: base, 1: base + inv, -1: base - inv}
    wv = [OMEGA * v for v in vec]
    combos = {}
    layers = []
    for i in range(19):
        c = VELOCITIES[i]
        key = tuple(c)
        terms = [(a, c[a]) for a in range(3) if c[a] != 0]
        cv = None
        if terms:
            if len(terms) == 1:
                a, s = terms[0]
                cv = wv[a] if s > 0 else -wv[a]
            else:
                (a, s), (b, t) = terms
                pos = (a, b, s * t)
                if pos not in combos:
                    combos[pos] = wv[a] + wv[b] if s * t > 0 else wv[a] - wv[b]
                cv = combos[pos] if s > 0 else -combos[pos]
        val = (1.0 - OMEGA) * pulled[i] + bases[c[0]]
        if cv is not None:
            val = val + cv
        layers.append(jnp.where(fluid, val, pulled[OPPOSITE[i]]))
    sens = None
    for i in range(1, 19, 2):
        c = VELOCITIES[i]
        along = None
        for a in range(3):
            if c[a] == 0:
                continue
            if along is None:
                along = u[a] if c[a] > 0 else -u[a]
            else:
                along = along + u[a] if c[a] > 0 else along - u[a]
        term = (6.0 * WEIGHTS[i]) * along * (pulled[OPPOSITE[i]] - pulled[i])
        sens = term if sens is None else sens + term
    sens = jnp.where(fluid, rho * sens, 0.0)
    return layers, sens


def _where(dims):
    me = (lax.axis_index("gx"), lax.axis_index("gy"), lax.axis_index("gz"))

    def exists(d):
        cond = None
        for a in range(3):
            if d[a] == 0:
                continue
            v = me[a] + d[a]
            c = (v >= 0) if d[a] < 0 else (v < dims[a])
            cond = c if cond is None else jnp.logical_and(cond, c)
        return cond

    def target(d):
        return tuple(me[a] + d[a] for a in range(3))

    return me, exists, target


def _zero_missing(exists, xh, yh, exy, mh):
    for d, so, de in _messages(8, 16):
        back = tuple(-v for v in d)

        @pl.when(jnp.logical_not(exists(back)))
        def _():
            if de[0] == "XH":
                xh[de[1]] = jnp.zeros(xh.shape[1:], jnp.float32)
            elif de[0] == "YH":
                yh[de[1]] = jnp.zeros(yh.shape[1:], jnp.float32)
            elif de[0] == "EXY":
                exy[de[1]] = jnp.zeros(exy.shape[1:], jnp.float32)
            else:
                mh[de[1], pl.ds(de[2], de[3]), :] = jnp.zeros((de[3], mh.shape[-1]), jnp.float32)


def _step(s, src, xh, yh, exy, mt, rho_ref, vel_ref, mask_ref, level, emit, before=None):
    cx, cy, cz = 8, 16, 128
    lane = lax.broadcasted_iota(jnp.int32, (cy, cz), 1)
    lane1 = lax.broadcasted_iota(jnp.int32, (1, cz), 1)
    row = lax.broadcasted_iota(jnp.int32, (cy, cz), 0)

    def pulled_plane(p):
        out = []
        for i in range(19):
            vx, vy, vz = VELOCITIES[i]
            q = p + vx
            if 0 <= q < cx:
                plane = src[i, pl.ds(q * cy, cy), :]
            elif q == cx:
                plane = xh[s, 1, CXP.index(i)]
            else:
                plane = xh[s, 0, CXM.index(i)]
            if vz != 0:
                side = 1 if vz > 0 else 0
                if 0 <= q < cx:
                    zc = mt[s, side, pl.ds(q * cy, cy), :]
                    col = ZFACE_COL[i]
                else:
                    col, r0 = XZ_EDGE[i]
                    zc = mt[s, side, pl.ds(r0 % (cx * cy), cy), :]
                if vz > 0:
                    plane = jnp.where(lane == cz - 1, pltpu.roll(zc, (cz - 1 - col) % cz, 1),
                                      pltpu.roll(plane, cz - 1, 1))
                else:
                    plane = jnp.where(lane == 0, pltpu.roll(zc, (cz - col) % cz, 1),
                                      pltpu.roll(plane, 1, 1))
            if vy != 0:
                side_y = 1 if vy > 0 else 0
                ky = CYP.index(i) if vy > 0 else CYM.index(i)
                if 0 <= q < cx:
                    yrow = yh[s, side_y, ky, pl.ds(q, 1), :]
                else:
                    e, r = XY_EDGE[i]
                    yrow = exy[s, e, pl.ds(r, 1), :]
                if vz != 0:
                    side = 1 if vz > 0 else 0
                    colc, yoff = YZ_CORNER[i]
                    crow = mt[s, side, pl.ds(p * cy + yoff % cy, 1), :]
                    if vz > 0:
                        yrow = jnp.where(lane1 == cz - 1, pltpu.roll(crow, (cz - 1 - colc) % cz, 1),
                                         pltpu.roll(yrow, cz - 1, 1))
                    else:
                        yrow = jnp.where(lane1 == 0, pltpu.roll(crow, (cz - colc) % cz, 1),
                                         pltpu.roll(yrow, 1, 1))
                if vy > 0:
                    plane = jnp.where(row == cy - 1, yrow, pltpu.roll(plane, cy - 1, 0))
                else:
                    plane = jnp.where(row == 0, yrow, pltpu.roll(plane, 1, 0))
            out.append(plane)
        return out

    for p in range(cx):
        if before is not None:
            before(p)
        rs = pl.ds(p * cy, cy)
        pulled = pulled_plane(p)
        rho = rho_ref[level, rs, :]
        ux = vel_ref[level, 0, rs, :]
        uy = vel_ref[level, 1, rs, :]
        uz = vel_ref[level, 2, rs, :]
        fluid = mask_ref[rs, :] > 0
        layers, sens = _collide(pulled, rho, ux, uy, uz, fluid)
        emit(p, rs, layers, sens)


def _kernel(dims, adj_hbm, rho_hbm, vel_hbm, mask_hbm,
            mid_out, sens_out, xh_out, yh_out, exy_out, mh_out,
            adj_ref, rho_ref, vel_ref, mask_ref, load_sem,
            mid, sfin, out_sem, xh, yh, exy, sy, sx, nt, mh, mt, send_sem, recv_sem):
    cx, cy, cz = 8, 16, 128
    rows = cx * cy
    me, exists, target = _where(dims)

    barrier = pltpu.get_barrier_semaphore()
    for d in NEIGHBOURS:
        @pl.when(exists(d))
        def _():
            pl.semaphore_signal(barrier, inc=1, device_id=target(d), device_id_type=MESH)

    loads = [
        pltpu.make_async_copy(src, dst, load_sem.at[k])
        for k, (src, dst) in enumerate(
            ((adj_hbm, adj_ref), (vel_hbm, vel_ref), (rho_hbm, rho_ref), (mask_hbm, mask_ref))
        )
    ]
    for copy in loads:
        copy.start()

    mh[0, :, pl.ds(72, rows - 72), :] = jnp.zeros((2, rows - 72, cz), jnp.float32)
    _zero_missing(exists, xh.at[0], yh.at[0], exy.at[0], mh.at[0])

    lane_big = lax.broadcasted_iota(jnp.int32, (rows, cz), 1)
    msgs = _messages(cx, cy)

    def prepare(s, src):
        for side, pops, q in ((0, CXP, 0), (1, CXM, cx - 1)):
            for k, pop in enumerate(pops):
                sx[s, side, k] = src[pop, pl.ds(q * cy, cy), :]
        for side, pops, y in ((0, CYP, 0), (1, CYM, cy - 1)):
            for k, pop in enumerate(pops):
                sy[s, side, k] = src[pop, pl.ds(y, cx, stride=cy), :]
        n = jnp.zeros((rows, cz), jnp.float32)
        for j, (pop, z) in enumerate(ZCOLS):
            zz = z % cz
            n = jnp.where(lane_big == 8 * j, pltpu.roll(src[pop], (8 * j - zz) % cz, 1), n)
        nt[s] = n.T

    def descriptor(s, src, t):
        d, so, de = msgs[t]
        if so[0] == "S":
            sref = src.at[so[1], pl.ds(so[2] % rows, so[3]), :]
        elif so[0] == "SY":
            sref = sy.at[s, so[1]]
        elif so[0] == "SX":
            sref = sx.at[s, so[1]]
        else:
            sref = nt.at[s, pl.ds(so[1], so[2]), :]
        bufs = {"XH": (xh.at[0], xh_out), "YH": (yh.at[0], yh_out), "EXY": (exy.at[0], exy_out),
                "MH": (mh.at[0], mh_out)}[de[0]][s]
        if de[0] == "MH":
            dref = bufs.at[de[1], pl.ds(de[2], de[3]), :]
        else:
            dref = bufs.at[de[1]]
        return pltpu.make_async_remote_copy(
            src_ref=sref, dst_ref=dref, send_sem=send_sem.at[s, t], recv_sem=recv_sem.at[s, t],
            device_id=target(d), device_id_type=MESH)

    def send(s, src):
        for t in range(len(msgs)):
            @pl.when(exists(msgs[t][0]))
            def _():
                descriptor(s, src, t).start()

    def finish(s, src):
        for t in range(len(msgs)):
            d = msgs[t][0]
            back = tuple(-v for v in d)

            @pl.when(exists(back))
            def _():
                descriptor(s, src, t).wait_recv()

            @pl.when(exists(d))
            def _():
                descriptor(s, src, t).wait_send()

    peers = 0
    for d in NEIGHBOURS:
        term = 1
        for a in range(3):
            n = dims[a]
            if d[a] < 0:
                term = term * ((me[a] + n - 1) // n)
            elif d[a] > 0:
                term = term * ((2 * n - 2 - me[a]) // n)
        peers = peers + term
    loads[0].wait()
    prepare(0, adj_ref)
    pl.semaphore_wait(barrier, peers)
    send(0, adj_ref)
    for copy in loads[1:]:
        copy.wait()
    finish(0, adj_ref)
    for side in range(2):
        mt[0, side] = mh[0, side].T

    def flush(p):
        rs = pl.ds(p * cy, cy)
        pltpu.make_async_copy(mid.at[:, rs, :], mid_out.at[:, rs, :], out_sem.at[p]).start()

    def emit(p, rs, layers, sens):
        for i in range(19):
            mid[i, rs, :] = layers[i]
        sfin[rs, :] = sens

    _step(0, adj_ref, xh, yh, exy, mt, rho_ref, vel_ref, mask_ref, 1, emit,
          before=lambda p: flush(p - 1) if p >= 1 else None)
    flush(cx - 1)
    sens_copy = pltpu.make_async_copy(sfin, sens_out, out_sem.at[cx])
    sens_copy.start()
    prepare(1, mid)
    send(1, mid)
    finish(1, mid)
    for p in range(cx):
        rs = pl.ds(p * cy, cy)
        pltpu.make_async_copy(mid.at[:, rs, :], mid_out.at[:, rs, :], out_sem.at[p]).wait()
    sens_copy.wait()


def _last(dims, mid_hbm, s1_hbm, xh_hbm, yh_hbm, exy_hbm, mh_hbm, rho_hbm, vel_hbm, mask_hbm,
          out_hbm, sens_hbm,
          mid, s1, xh, yh, exy, mh, mt, rho, vel, mask, fin, sfin, in_sem, out_sem):
    cx, cy, cz = 8, 16, 128
    rows = cx * cy
    me, exists, target = _where(dims)
    mh[...] = jnp.zeros(mh.shape, jnp.float32)
    used = 72
    loads = [
        pltpu.make_async_copy(xh_hbm, xh.at[0], in_sem.at[0]),
        pltpu.make_async_copy(yh_hbm, yh.at[0], in_sem.at[1]),
        pltpu.make_async_copy(exy_hbm, exy.at[0], in_sem.at[2]),
        pltpu.make_async_copy(mh_hbm.at[:, pl.ds(0, used), :], mh.at[:, pl.ds(0, used), :], in_sem.at[3]),
        pltpu.make_async_copy(rho_hbm.at[pl.ds(0, 1)], rho, in_sem.at[4]),
        pltpu.make_async_copy(vel_hbm.at[pl.ds(0, 1)], vel, in_sem.at[5]),
        pltpu.make_async_copy(mask_hbm, mask, in_sem.at[6]),
        pltpu.make_async_copy(s1_hbm, s1, in_sem.at[7]),
    ]
    planes = [
        pltpu.make_async_copy(mid_hbm.at[:, pl.ds(p * cy, cy), :], mid.at[:, pl.ds(p * cy, cy), :],
                              in_sem.at[8 + p])
        for p in range(cx)
    ]
    for copy in loads:
        copy.start()
    for copy in planes:
        copy.start()
    for copy in loads:
        copy.wait()
    _zero_missing(exists, xh.at[0], yh.at[0], exy.at[0], mh)

    for side in range(2):
        mt[0, side] = mh[side].T

    def flush(p):
        rs = pl.ds(p * cy, cy)
        pltpu.make_async_copy(fin.at[:, rs, :], out_hbm.at[:, rs, :], out_sem.at[p]).start()

    def emit(p, rs, layers, sens):
        for i in range(19):
            fin[i, rs, :] = layers[i]
        sfin[rs, :] = s1[rs, :] + sens

    def before(p):
        if p == 0:
            planes[0].wait()
        if p + 1 < cx:
            planes[p + 1].wait()
        if p >= 1:
            flush(p - 1)

    _step(0, mid, xh, yh, exy, mt, rho, vel, mask, 0, emit, before=before)
    flush(cx - 1)
    sens_copy = pltpu.make_async_copy(sfin, sens_hbm, out_sem.at[cx])
    sens_copy.start()
    for p in range(cx):
        rs = pl.ds(p * cy, cy)
        pltpu.make_async_copy(fin.at[:, rs, :], out_hbm.at[:, rs, :], out_sem.at[p]).wait()
    sens_copy.wait()


def solution(mesh):
    dims = (mesh.shape["gx"], mesh.shape["gy"], mesh.shape["gz"])
    nmsg = len(_messages(8, 16))

    def shards(adjoint, density, velocity, pore_mask):
        npop, cx, cy, cz = adjoint.shape
        assert (cx, cy, cz) == (8, 16, 128)
        rows = cx * cy
        adj = adjoint.reshape(npop, rows, cz)
        rho = density.reshape(2, rows, cz)
        vel = velocity.reshape(2, 3, rows, cz)
        mask = pore_mask.reshape(rows, cz)
        hbm = pl.BlockSpec(memory_space=pltpu.HBM)
        f32 = jnp.float32
        halo_shapes = (
            jax.ShapeDtypeStruct((2, 5, cy, cz), f32),
            jax.ShapeDtypeStruct((2, 5, cx, cz), f32),
            jax.ShapeDtypeStruct((4, 8, cz), f32),
            jax.ShapeDtypeStruct((2, rows, cz), f32),
        )
        mid, s1, xh2, yh2, exy2, mh2 = pl.pallas_call(
            functools.partial(_kernel, dims),
            out_shape=(
                jax.ShapeDtypeStruct((npop, rows, cz), f32),
                jax.ShapeDtypeStruct((rows, cz), f32),
            ) + halo_shapes,
            in_specs=[hbm] * 4,
            out_specs=(hbm,) * 6,
            scratch_shapes=[
                pltpu.VMEM((npop, rows, cz), f32),
                pltpu.VMEM((2, rows, cz), f32),
                pltpu.VMEM((2, 3, rows, cz), f32),
                pltpu.VMEM((rows, cz), jnp.int32),
                pltpu.SemaphoreType.DMA((4,)),
                pltpu.VMEM((npop, rows, cz), f32),
                pltpu.VMEM((rows, cz), f32),
                pltpu.SemaphoreType.DMA((cx + 1,)),
                pltpu.VMEM((1, 2, 5, cy, cz), f32),
                pltpu.VMEM((1, 2, 5, cx, cz), f32),
                pltpu.VMEM((1, 4, 8, cz), f32),
                pltpu.VMEM((2, 2, 5, cx, cz), f32),
                pltpu.VMEM((2, 2, 5, cy, cz), f32),
                pltpu.VMEM((2, rows, cz), f32),
                pltpu.VMEM((1, 2, rows, cz), f32),
                pltpu.VMEM((1, 2, rows, cz), f32),
                pltpu.SemaphoreType.DMA((2, nmsg)),
                pltpu.SemaphoreType.DMA((2, nmsg)),
            ],
            compiler_params=pltpu.CompilerParams(
                collective_id=0, has_side_effects=True, vmem_limit_bytes=67043328
            ),
        )(adj, rho, vel, mask)
        out, sens = pl.pallas_call(
            functools.partial(_last, dims),
            out_shape=(
                jax.ShapeDtypeStruct((npop, rows, cz), f32),
                jax.ShapeDtypeStruct((rows, cz), f32),
            ),
            in_specs=[hbm] * 9,
            out_specs=(hbm, hbm),
            scratch_shapes=[
                pltpu.VMEM((npop, rows, cz), f32),
                pltpu.VMEM((rows, cz), f32),
                pltpu.VMEM((1, 2, 5, cy, cz), f32),
                pltpu.VMEM((1, 2, 5, cx, cz), f32),
                pltpu.VMEM((1, 4, 8, cz), f32),
                pltpu.VMEM((2, rows, cz), f32),
                pltpu.VMEM((1, 2, rows, cz), f32),
                pltpu.VMEM((1, rows, cz), f32),
                pltpu.VMEM((1, 3, rows, cz), f32),
                pltpu.VMEM((rows, cz), jnp.int32),
                pltpu.VMEM((npop, rows, cz), f32),
                pltpu.VMEM((rows, cz), f32),
                pltpu.SemaphoreType.DMA((8 + cx,)),
                pltpu.SemaphoreType.DMA((cx + 1,)),
            ],
            compiler_params=pltpu.CompilerParams(vmem_limit_bytes=67043328),
        )(mid, s1, xh2, yh2, exy2, mh2, rho, vel, mask)
        return out.reshape(npop, cx, cy, cz), sens.reshape(cx, cy, cz)

    placed = (
        P(None, "gx", "gy", "gz"),
        P(None, "gx", "gy", "gz"),
        P(None, None, "gx", "gy", "gz"),
        P("gx", "gy", "gz"),
    )
    return jax.shard_map(
        shards,
        mesh=mesh,
        in_specs=placed,
        out_specs=(P(None, "gx", "gy", "gz"), P("gx", "gy", "gz")),
        check_vma=False,
    )
```

```python
import functools

import jax
import jax.numpy as jnp
from jax import lax
from jax.experimental import pallas as pl
from jax.experimental.pallas import tpu as pltpu
from jax.sharding import PartitionSpec as P

VELOCITIES = [
    (0, 0, 0),
    (1, 0, 0),
    (-1, 0, 0),
    (0, 1, 0),
    (0, -1, 0),
    (0, 0, 1),
    (0, 0, -1),
    (1, 1, 0),
    (-1, -1, 0),
    (1, -1, 0),
    (-1, 1, 0),
    (1, 0, 1),
    (-1, 0, -1),
    (1, 0, -1),
    (-1, 0, 1),
    (0, 1, 1),
    (0, -1, -1),
    (0, 1, -1),
    (0, -1, 1),
]
WEIGHTS = [1.0 / 3.0] + [1.0 / 18.0] * 6 + [1.0 / 36.0] * 12
OPPOSITE = [0, 2, 1, 4, 3, 6, 5, 8, 7, 10, 9, 12, 11, 14, 13, 16, 15, 18, 17]
OMEGA = 1.25
MESH = pl.DeviceIdType.MESH

CXP = [1, 7, 9, 11, 13]
CXM = [2, 8, 10, 12, 14]
CYP = [3, 7, 10, 15, 17]
CYM = [4, 8, 9, 16, 18]
ZCOLS = [(5, 0), (11, 0), (14, 0), (15, 0), (18, 0), (6, -1), (12, -1), (13, -1), (16, -1), (17, -1)]
ZFACE_COL = {5: 0, 11: 8, 14: 16, 15: 24, 18: 32, 6: 0, 12: 8, 13: 16, 16: 24, 17: 32}
XZ_EDGE = {11: (40, 0), 14: (48, -16), 12: (40, -16), 13: (48, 0)}
YZ_CORNER = {15: (56, 0), 18: (64, -1), 16: (56, -1), 17: (64, 0)}
XY_EDGE = {7: (0, 0), 8: (1, 7), 9: (2, 7), 10: (3, 0)}


def _messages(cx, cy):
    rows = cx * cy
    msgs = []
    msgs.append(((0, -1, 0), ("SY", 0), ("YH", 1)))
    msgs.append(((0, 1, 0), ("SY", 1), ("YH", 0)))
    msgs.append(((0, -1, -1), ("NT", 24, 8), ("MH", 1, 56, 8)))
    msgs.append(((0, 1, -1), ("NT", 32, 8), ("MH", 1, 64, 8)))
    msgs.append(((0, 1, 1), ("NT", 64, 8), ("MH", 0, 56, 8)))
    msgs.append(((0, -1, 1), ("NT", 72, 8), ("MH", 0, 64, 8)))
    msgs.append(((-1, -1, 0), ("S", 7, 0, 8), ("EXY", 0)))
    msgs.append(((1, 1, 0), ("S", 8, rows - 8, 8), ("EXY", 1)))
    msgs.append(((-1, 1, 0), ("S", 9, cy - 8, 8), ("EXY", 2)))
    msgs.append(((1, -1, 0), ("S", 10, rows - cy, 8), ("EXY", 3)))
    msgs.append(((0, 0, -1), ("NT", 0, 40), ("MH", 1, 0, 40)))
    msgs.append(((0, 0, 1), ("NT", 40, 40), ("MH", 0, 0, 40)))
    msgs.append(((-1, 0, -1), ("NT", 8, 8), ("MH", 1, 40, 8)))
    msgs.append(((1, 0, -1), ("NT", 16, 8), ("MH", 1, 48, 8)))
    msgs.append(((1, 0, 1), ("NT", 48, 8), ("MH", 0, 40, 8)))
    msgs.append(((-1, 0, 1), ("NT", 56, 8), ("MH", 0, 48, 8)))
    msgs.append(((-1, 0, 0), ("SX", 0), ("XH", 1)))
    msgs.append(((1, 0, 0), ("SX", 1), ("XH", 0)))
    return msgs


NEIGHBOURS = sorted(
    {d for d, _, _ in _messages(8, 16)} | {tuple(-v for v in d) for d, _, _ in _messages(8, 16)}
)


def _comb(vals, fn):
    total = None
    for weight in (1.0 / 3.0, 1.0 / 18.0, 1.0 / 36.0):
        part = None
        for i in range(19):
            if WEIGHTS[i] != weight:
                continue
            k = fn(VELOCITIES[i])
            if k == 0:
                continue
            if part is None:
                part = vals[i] if k > 0 else -vals[i]
            else:
                part = part + vals[i] if k > 0 else part - vals[i]
        if part is not None:
            term = part * weight
            total = term if total is None else total + term
    return total


def _collide(pulled, rho, ux, uy, uz, fluid):
    p0 = _comb(pulled, lambda c: 1)
    p1 = [_comb(pulled, lambda c, a=a: c[a]) for a in range(3)]
    q = {}
    for a in range(3):
        for b in range(a, 3):
            q[a, b] = _comb(pulled, lambda c, a=a, b=b: c[a] * c[b])
            q[b, a] = q[a, b]
    u = (ux, uy, uz)
    usq = ux * ux + uy * uy + uz * uz
    qu = [q[a, 0] * ux + q[a, 1] * uy + q[a, 2] * uz for a in range(3)]
    p1u = p1[0] * ux + p1[1] * uy + p1[2] * uz
    uqu = ux * qu[0] + uy * qu[1] + uz * qu[2]
    moment = p0 * (1.0 - 1.5 * usq) + 3.0 * p1u + 4.5 * uqu
    vec = [3.0 * p1[a] + 9.0 * qu[a] - 3.0 * u[a] * p0 for a in range(3)]
    vu = vec[0] * ux + vec[1] * uy + vec[2] * uz
    inv = 1.0 / rho
    base = OMEGA * (moment - vu) - ux * inv
    bases = {0: base, 1: base + inv, -1: base - inv}
    wv = [OMEGA * v for v in vec]
    combos = {}
    layers = []
    for i in range(19):
        c = VELOCITIES[i]
        key = tuple(c)
        terms = [(a, c[a]) for a in range(3) if c[a] != 0]
        cv = None
        if terms:
            if len(terms) == 1:
                a, s = terms[0]
                cv = wv[a] if s > 0 else -wv[a]
            else:
                (a, s), (b, t) = terms
                pos = (a, b, s * t)
                if pos not in combos:
                    combos[pos] = wv[a] + wv[b] if s * t > 0 else wv[a] - wv[b]
                cv = combos[pos] if s > 0 else -combos[pos]
        val = (1.0 - OMEGA) * pulled[i] + bases[c[0]]
        if cv is not None:
            val = val + cv
        layers.append(jnp.where(fluid, val, pulled[OPPOSITE[i]]))
    sens = None
    for i in range(1, 19, 2):
        c = VELOCITIES[i]
        along = None
        for a in range(3):
            if c[a] == 0:
                continue
            if along is None:
                along = u[a] if c[a] > 0 else -u[a]
            else:
                along = along + u[a] if c[a] > 0 else along - u[a]
        term = (6.0 * WEIGHTS[i]) * along * (pulled[OPPOSITE[i]] - pulled[i])
        sens = term if sens is None else sens + term
    sens = jnp.where(fluid, rho * sens, 0.0)
    return layers, sens


def _where(dims):
    me = (lax.axis_index("gx"), lax.axis_index("gy"), lax.axis_index("gz"))

    def exists(d):
        cond = None
        for a in range(3):
            if d[a] == 0:
                continue
            v = me[a] + d[a]
            c = (v >= 0) if d[a] < 0 else (v < dims[a])
            cond = c if cond is None else jnp.logical_and(cond, c)
        return cond

    def target(d):
        return tuple(me[a] + d[a] for a in range(3))

    return me, exists, target


def _zero_missing(exists, xh, yh, exy, mh):
    for d, so, de in _messages(8, 16):
        back = tuple(-v for v in d)

        @pl.when(jnp.logical_not(exists(back)))
        def _():
            if de[0] == "XH":
                xh[de[1]] = jnp.zeros(xh.shape[1:], jnp.float32)
            elif de[0] == "YH":
                yh[de[1]] = jnp.zeros(yh.shape[1:], jnp.float32)
            elif de[0] == "EXY":
                exy[de[1]] = jnp.zeros(exy.shape[1:], jnp.float32)
            else:
                mh[de[1], pl.ds(de[2], de[3]), :] = jnp.zeros((de[3], mh.shape[-1]), jnp.float32)


def _step(s, src, xh, yh, exy, mt, rho_ref, vel_ref, mask_ref, level, emit, before=None):
    cx, cy, cz = 8, 16, 128
    lane = lax.broadcasted_iota(jnp.int32, (cy, cz), 1)
    lane1 = lax.broadcasted_iota(jnp.int32, (1, cz), 1)
    row = lax.broadcasted_iota(jnp.int32, (cy, cz), 0)

    def pulled_plane(p):
        out = []
        for i in range(19):
            vx, vy, vz = VELOCITIES[i]
            q = p + vx
            if 0 <= q < cx:
                plane = src[i, pl.ds(q * cy, cy), :]
            elif q == cx:
                plane = xh[s, 1, CXP.index(i)]
            else:
                plane = xh[s, 0, CXM.index(i)]
            if vz != 0:
                side = 1 if vz > 0 else 0
                if 0 <= q < cx:
                    zc = mt[s, side, pl.ds(q * cy, cy), :]
                    col = ZFACE_COL[i]
                else:
                    col, r0 = XZ_EDGE[i]
                    zc = mt[s, side, pl.ds(r0 % (cx * cy), cy), :]
                if vz > 0:
                    plane = jnp.where(lane == cz - 1, pltpu.roll(zc, (cz - 1 - col) % cz, 1),
                                      pltpu.roll(plane, cz - 1, 1))
                else:
                    plane = jnp.where(lane == 0, pltpu.roll(zc, (cz - col) % cz, 1),
                                      pltpu.roll(plane, 1, 1))
            if vy != 0:
                side_y = 1 if vy > 0 else 0
                ky = CYP.index(i) if vy > 0 else CYM.index(i)
                if 0 <= q < cx:
                    yrow = yh[s, side_y, ky, pl.ds(q, 1), :]
                else:
                    e, r = XY_EDGE[i]
                    yrow = exy[s, e, pl.ds(r, 1), :]
                if vz != 0:
                    side = 1 if vz > 0 else 0
                    colc, yoff = YZ_CORNER[i]
                    crow = mt[s, side, pl.ds(p * cy + yoff % cy, 1), :]
                    if vz > 0:
                        yrow = jnp.where(lane1 == cz - 1, pltpu.roll(crow, (cz - 1 - colc) % cz, 1),
                                         pltpu.roll(yrow, cz - 1, 1))
                    else:
                        yrow = jnp.where(lane1 == 0, pltpu.roll(crow, (cz - colc) % cz, 1),
                                         pltpu.roll(yrow, 1, 1))
                if vy > 0:
                    plane = jnp.where(row == cy - 1, yrow, pltpu.roll(plane, cy - 1, 0))
                else:
                    plane = jnp.where(row == 0, yrow, pltpu.roll(plane, 1, 0))
            out.append(plane)
        return out

    for p in range(cx):
        if before is not None:
            before(p)
        rs = pl.ds(p * cy, cy)
        pulled = pulled_plane(p)
        rho = rho_ref[level, rs, :]
        ux = vel_ref[level, 0, rs, :]
        uy = vel_ref[level, 1, rs, :]
        uz = vel_ref[level, 2, rs, :]
        fluid = mask_ref[rs, :] > 0
        layers, sens = _collide(pulled, rho, ux, uy, uz, fluid)
        emit(p, rs, layers, sens)


def _kernel(dims, adj_hbm, rho_hbm, vel_hbm, mask_hbm,
            mid_out, sens_out, xh_out, yh_out, exy_out, mh_out,
            adj_ref, rho_ref, vel_ref, mask_ref, load_sem,
            mid, sfin, out_sem, xh, yh, exy, sy, sx, nt, mh, mt, send_sem, recv_sem):
    cx, cy, cz = 8, 16, 128
    rows = cx * cy
    me, exists, target = _where(dims)

    barrier = pltpu.get_barrier_semaphore()
    for d in NEIGHBOURS:
        @pl.when(exists(d))
        def _():
            pl.semaphore_signal(barrier, inc=1, device_id=target(d), device_id_type=MESH)

    loads = [
        pltpu.make_async_copy(src, dst, load_sem.at[k])
        for k, (src, dst) in enumerate(
            ((adj_hbm, adj_ref), (vel_hbm, vel_ref), (rho_hbm, rho_ref), (mask_hbm, mask_ref))
        )
    ]
    for copy in loads:
        copy.start()

    mh[0, :, pl.ds(72, rows - 72), :] = jnp.zeros((2, rows - 72, cz), jnp.float32)
    _zero_missing(exists, xh.at[0], yh.at[0], exy.at[0], mh.at[0])

    lane_big = lax.broadcasted_iota(jnp.int32, (rows, cz), 1)
    msgs = _messages(cx, cy)

    def prepare(s, src):
        for side, pops, q in ((0, CXP, 0), (1, CXM, cx - 1)):
            for k, pop in enumerate(pops):
                sx[s, side, k] = src[pop, pl.ds(q * cy, cy), :]
        for side, pops, y in ((0, CYP, 0), (1, CYM, cy - 1)):
            for k, pop in enumerate(pops):
                sy[s, side, k] = src[pop, pl.ds(y, cx, stride=cy), :]
        n = jnp.zeros((rows, cz), jnp.float32)
        for j, (pop, z) in enumerate(ZCOLS):
            zz = z % cz
            n = jnp.where(lane_big == 8 * j, pltpu.roll(src[pop], (8 * j - zz) % cz, 1), n)
        nt[s] = n.T

    def descriptor(s, src, t):
        d, so, de = msgs[t]
        if so[0] == "S":
            sref = src.at[so[1], pl.ds(so[2] % rows, so[3]), :]
        elif so[0] == "SY":
            sref = sy.at[s, so[1]]
        elif so[0] == "SX":
            sref = sx.at[s, so[1]]
        else:
            sref = nt.at[s, pl.ds(so[1], so[2]), :]
        bufs = {"XH": (xh.at[0], xh_out), "YH": (yh.at[0], yh_out), "EXY": (exy.at[0], exy_out),
                "MH": (mh.at[0], mh_out)}[de[0]][s]
        if de[0] == "MH":
            dref = bufs.at[de[1], pl.ds(de[2], de[3]), :]
        else:
            dref = bufs.at[de[1]]
        return pltpu.make_async_remote_copy(
            src_ref=sref, dst_ref=dref, send_sem=send_sem.at[s, t], recv_sem=recv_sem.at[s, t],
            device_id=target(d), device_id_type=MESH)

    def send(s, src):
        for t in range(len(msgs)):
            @pl.when(exists(msgs[t][0]))
            def _():
                descriptor(s, src, t).start()

    def finish(s, src):
        for t in range(len(msgs)):
            d = msgs[t][0]
            back = tuple(-v for v in d)

            @pl.when(exists(back))
            def _():
                descriptor(s, src, t).wait_recv()

            @pl.when(exists(d))
            def _():
                descriptor(s, src, t).wait_send()

    peers = 0
    for d in NEIGHBOURS:
        term = 1
        for a in range(3):
            n = dims[a]
            if d[a] < 0:
                term = term * ((me[a] + n - 1) // n)
            elif d[a] > 0:
                term = term * ((2 * n - 2 - me[a]) // n)
        peers = peers + term
    loads[0].wait()
    prepare(0, adj_ref)
    pl.semaphore_wait(barrier, peers)
    send(0, adj_ref)
    for copy in loads[1:]:
        copy.wait()
    finish(0, adj_ref)
    for side in range(2):
        mt[0, side] = mh[0, side].T

    def flush(p):
        rs = pl.ds(p * cy, cy)
        pltpu.make_async_copy(mid.at[:, rs, :], mid_out.at[:, rs, :], out_sem.at[p]).start()

    def emit(p, rs, layers, sens):
        for i in range(19):
            mid[i, rs, :] = layers[i]
        sfin[rs, :] = sens

    _step(0, adj_ref, xh, yh, exy, mt, rho_ref, vel_ref, mask_ref, 1, emit,
          before=lambda p: flush(p - 1) if p >= 1 else None)
    prepare(1, mid)
    send(1, mid)
    flush(cx - 1)
    sens_copy = pltpu.make_async_copy(sfin, sens_out, out_sem.at[cx])
    sens_copy.start()
    finish(1, mid)
    for p in range(cx):
        rs = pl.ds(p * cy, cy)
        pltpu.make_async_copy(mid.at[:, rs, :], mid_out.at[:, rs, :], out_sem.at[p]).wait()
    sens_copy.wait()


def _last(dims, mid_hbm, s1_hbm, xh_hbm, yh_hbm, exy_hbm, mh_hbm, rho_hbm, vel_hbm, mask_hbm,
          out_hbm, sens_hbm,
          mid, s1, xh, yh, exy, mh, mt, rho, vel, mask, fin, sfin, in_sem, out_sem):
    cx, cy, cz = 8, 16, 128
    rows = cx * cy
    me, exists, target = _where(dims)
    mh[...] = jnp.zeros(mh.shape, jnp.float32)
    used = 72
    loads = [
        pltpu.make_async_copy(xh_hbm, xh.at[0], in_sem.at[0]),
        pltpu.make_async_copy(yh_hbm, yh.at[0], in_sem.at[1]),
        pltpu.make_async_copy(exy_hbm, exy.at[0], in_sem.at[2]),
        pltpu.make_async_copy(mh_hbm.at[:, pl.ds(0, used), :], mh.at[:, pl.ds(0, used), :], in_sem.at[3]),
        pltpu.make_async_copy(rho_hbm.at[pl.ds(0, 1)], rho, in_sem.at[4]),
        pltpu.make_async_copy(vel_hbm.at[pl.ds(0, 1)], vel, in_sem.at[5]),
        pltpu.make_async_copy(mask_hbm, mask, in_sem.at[6]),
        pltpu.make_async_copy(s1_hbm, s1, in_sem.at[7]),
        pltpu.make_async_copy(mid_hbm, mid, in_sem.at[8]),
    ]
    for copy in loads:
        copy.start()
    for copy in loads:
        copy.wait()
    _zero_missing(exists, xh.at[0], yh.at[0], exy.at[0], mh)

    for side in range(2):
        mt[0, side] = mh[side].T

    def flush(p):
        rs = pl.ds(p * cy, cy)
        pltpu.make_async_copy(fin.at[:, rs, :], out_hbm.at[:, rs, :], out_sem.at[p]).start()

    def emit(p, rs, layers, sens):
        for i in range(19):
            fin[i, rs, :] = layers[i]
        sfin[rs, :] = s1[rs, :] + sens

    _step(0, mid, xh, yh, exy, mt, rho, vel, mask, 0, emit,
          before=lambda p: flush(p - 1) if p >= 1 else None)
    flush(cx - 1)
    sens_copy = pltpu.make_async_copy(sfin, sens_hbm, out_sem.at[cx])
    sens_copy.start()
    for p in range(cx):
        rs = pl.ds(p * cy, cy)
        pltpu.make_async_copy(fin.at[:, rs, :], out_hbm.at[:, rs, :], out_sem.at[p]).wait()
    sens_copy.wait()


def solution(mesh):
    dims = (mesh.shape["gx"], mesh.shape["gy"], mesh.shape["gz"])
    nmsg = len(_messages(8, 16))

    def shards(adjoint, density, velocity, pore_mask):
        npop, cx, cy, cz = adjoint.shape
        assert (cx, cy, cz) == (8, 16, 128)
        rows = cx * cy
        adj = adjoint.reshape(npop, rows, cz)
        rho = density.reshape(2, rows, cz)
        vel = velocity.reshape(2, 3, rows, cz)
        mask = pore_mask.reshape(rows, cz)
        hbm = pl.BlockSpec(memory_space=pltpu.HBM)
        f32 = jnp.float32
        halo_shapes = (
            jax.ShapeDtypeStruct((2, 5, cy, cz), f32),
            jax.ShapeDtypeStruct((2, 5, cx, cz), f32),
            jax.ShapeDtypeStruct((4, 8, cz), f32),
            jax.ShapeDtypeStruct((2, rows, cz), f32),
        )
        mid, s1, xh2, yh2, exy2, mh2 = pl.pallas_call(
            functools.partial(_kernel, dims),
            out_shape=(
                jax.ShapeDtypeStruct((npop, rows, cz), f32),
                jax.ShapeDtypeStruct((rows, cz), f32),
            ) + halo_shapes,
            in_specs=[hbm] * 4,
            out_specs=(hbm,) * 6,
            scratch_shapes=[
                pltpu.VMEM((npop, rows, cz), f32),
                pltpu.VMEM((2, rows, cz), f32),
                pltpu.VMEM((2, 3, rows, cz), f32),
                pltpu.VMEM((rows, cz), jnp.int32),
                pltpu.SemaphoreType.DMA((4,)),
                pltpu.VMEM((npop, rows, cz), f32),
                pltpu.VMEM((rows, cz), f32),
                pltpu.SemaphoreType.DMA((cx + 1,)),
                pltpu.VMEM((1, 2, 5, cy, cz), f32),
                pltpu.VMEM((1, 2, 5, cx, cz), f32),
                pltpu.VMEM((1, 4, 8, cz), f32),
                pltpu.VMEM((2, 2, 5, cx, cz), f32),
                pltpu.VMEM((2, 2, 5, cy, cz), f32),
                pltpu.VMEM((2, rows, cz), f32),
                pltpu.VMEM((1, 2, rows, cz), f32),
                pltpu.VMEM((1, 2, rows, cz), f32),
                pltpu.SemaphoreType.DMA((2, nmsg)),
                pltpu.SemaphoreType.DMA((2, nmsg)),
            ],
            compiler_params=pltpu.CompilerParams(
                collective_id=0, has_side_effects=True, vmem_limit_bytes=67043328
            ),
        )(adj, rho, vel, mask)
        out, sens = pl.pallas_call(
            functools.partial(_last, dims),
            out_shape=(
                jax.ShapeDtypeStruct((npop, rows, cz), f32),
                jax.ShapeDtypeStruct((rows, cz), f32),
            ),
            in_specs=[hbm] * 9,
            out_specs=(hbm, hbm),
            scratch_shapes=[
                pltpu.VMEM((npop, rows, cz), f32),
                pltpu.VMEM((rows, cz), f32),
                pltpu.VMEM((1, 2, 5, cy, cz), f32),
                pltpu.VMEM((1, 2, 5, cx, cz), f32),
                pltpu.VMEM((1, 4, 8, cz), f32),
                pltpu.VMEM((2, rows, cz), f32),
                pltpu.VMEM((1, 2, rows, cz), f32),
                pltpu.VMEM((1, rows, cz), f32),
                pltpu.VMEM((1, 3, rows, cz), f32),
                pltpu.VMEM((rows, cz), jnp.int32),
                pltpu.VMEM((npop, rows, cz), f32),
                pltpu.VMEM((rows, cz), f32),
                pltpu.SemaphoreType.DMA((9,)),
                pltpu.SemaphoreType.DMA((cx + 1,)),
            ],
            compiler_params=pltpu.CompilerParams(vmem_limit_bytes=67043328),
        )(mid, s1, xh2, yh2, exy2, mh2, rho, vel, mask)
        return out.reshape(npop, cx, cy, cz), sens.reshape(cx, cy, cz)

    placed = (
        P(None, "gx", "gy", "gz"),
        P(None, "gx", "gy", "gz"),
        P(None, None, "gx", "gy", "gz"),
        P("gx", "gy", "gz"),
    )
    return jax.shard_map(
        shards,
        mesh=mesh,
        in_specs=placed,
        out_specs=(P(None, "gx", "gy", "gz"), P("gx", "gy", "gz")),
        check_vma=False,
    )
```

```python
import functools

import jax
import jax.numpy as jnp
from jax import lax
from jax.experimental import pallas as pl
from jax.experimental.pallas import tpu as pltpu
from jax.sharding import PartitionSpec as P

VELOCITIES = [
    (0, 0, 0),
    (1, 0, 0),
    (-1, 0, 0),
    (0, 1, 0),
    (0, -1, 0),
    (0, 0, 1),
    (0, 0, -1),
    (1, 1, 0),
    (-1, -1, 0),
    (1, -1, 0),
    (-1, 1, 0),
    (1, 0, 1),
    (-1, 0, -1),
    (1, 0, -1),
    (-1, 0, 1),
    (0, 1, 1),
    (0, -1, -1),
    (0, 1, -1),
    (0, -1, 1),
]
WEIGHTS = [1.0 / 3.0] + [1.0 / 18.0] * 6 + [1.0 / 36.0] * 12
OPPOSITE = [0, 2, 1, 4, 3, 6, 5, 8, 7, 10, 9, 12, 11, 14, 13, 16, 15, 18, 17]
OMEGA = 1.25
MESH = pl.DeviceIdType.MESH

CXP = [1, 7, 9, 11, 13]
CXM = [2, 8, 10, 12, 14]
CYP = [3, 7, 10, 15, 17]
CYM = [4, 8, 9, 16, 18]
ZCOLS = [(5, 0), (11, 0), (14, 0), (15, 0), (18, 0), (6, -1), (12, -1), (13, -1), (16, -1), (17, -1)]
ZFACE_COL = {5: 0, 11: 8, 14: 16, 15: 24, 18: 32, 6: 0, 12: 8, 13: 16, 16: 24, 17: 32}
XZ_EDGE = {11: (40, 0), 14: (48, -16), 12: (40, -16), 13: (48, 0)}
YZ_CORNER = {15: (56, 0), 18: (64, -1), 16: (56, -1), 17: (64, 0)}
XY_EDGE = {7: (0, 0), 8: (1, 7), 9: (2, 7), 10: (3, 0)}


def _messages(cx, cy):
    rows = cx * cy
    msgs = []
    msgs.append(((0, -1, 0), ("SY", 0), ("YH", 1)))
    msgs.append(((0, 1, 0), ("SY", 1), ("YH", 0)))
    msgs.append(((0, -1, -1), ("NT", 24, 8), ("MH", 1, 56, 8)))
    msgs.append(((0, 1, -1), ("NT", 32, 8), ("MH", 1, 64, 8)))
    msgs.append(((0, 1, 1), ("NT", 64, 8), ("MH", 0, 56, 8)))
    msgs.append(((0, -1, 1), ("NT", 72, 8), ("MH", 0, 64, 8)))
    msgs.append(((-1, -1, 0), ("S", 7, 0, 8), ("EXY", 0)))
    msgs.append(((1, 1, 0), ("S", 8, rows - 8, 8), ("EXY", 1)))
    msgs.append(((-1, 1, 0), ("S", 9, cy - 8, 8), ("EXY", 2)))
    msgs.append(((1, -1, 0), ("S", 10, rows - cy, 8), ("EXY", 3)))
    msgs.append(((0, 0, -1), ("NT", 0, 40), ("MH", 1, 0, 40)))
    msgs.append(((0, 0, 1), ("NT", 40, 40), ("MH", 0, 0, 40)))
    msgs.append(((-1, 0, -1), ("NT", 8, 8), ("MH", 1, 40, 8)))
    msgs.append(((1, 0, -1), ("NT", 16, 8), ("MH", 1, 48, 8)))
    msgs.append(((1, 0, 1), ("NT", 48, 8), ("MH", 0, 40, 8)))
    msgs.append(((-1, 0, 1), ("NT", 56, 8), ("MH", 0, 48, 8)))
    msgs.append(((-1, 0, 0), ("SX", 0), ("XH", 1)))
    msgs.append(((1, 0, 0), ("SX", 1), ("XH", 0)))
    return msgs


NEIGHBOURS = sorted(
    {d for d, _, _ in _messages(8, 16)} | {tuple(-v for v in d) for d, _, _ in _messages(8, 16)}
)


def _comb(vals, fn):
    total = None
    for weight in (1.0 / 3.0, 1.0 / 18.0, 1.0 / 36.0):
        part = None
        for i in range(19):
            if WEIGHTS[i] != weight:
                continue
            k = fn(VELOCITIES[i])
            if k == 0:
                continue
            if part is None:
                part = vals[i] if k > 0 else -vals[i]
            else:
                part = part + vals[i] if k > 0 else part - vals[i]
        if part is not None:
            term = part * weight
            total = term if total is None else total + term
    return total


def _collide(pulled, rho, ux, uy, uz, fluid):
    u = (ux, uy, uz)
    pair = {i: pulled[i] + pulled[i + 1] for i in range(1, 19, 2)}
    diff = {i: pulled[i] - pulled[i + 1] for i in range(1, 19, 2)}
    w1, w2 = 1.0 / 18.0, 1.0 / 36.0

    def signed(terms, table):
        total = None
        for i, sgn in terms:
            v = table[i]
            if total is None:
                total = v if sgn > 0 else -v
            else:
                total = total + v if sgn > 0 else total - v
        return total

    edges = [i for i in range(7, 19, 2)]
    p0 = pulled[0] * (1.0 / 3.0) + (pair[1] + pair[3] + pair[5]) * w1 + signed([(i, 1) for i in edges], pair) * w2
    p1 = []
    q = {}
    for a, axis_pop in enumerate((1, 3, 5)):
        edge = [i for i in edges if VELOCITIES[i][a] != 0]
        p1.append(diff[axis_pop] * w1 + signed([(i, VELOCITIES[i][a]) for i in edge], diff) * w2)
        q[a, a] = pair[axis_pop] * w1 + signed([(i, 1) for i in edge], pair) * w2
    for a in range(3):
        for b in range(a + 1, 3):
            edge = [i for i in edges if VELOCITIES[i][a] != 0 and VELOCITIES[i][b] != 0]
            q[a, b] = signed([(i, VELOCITIES[i][a] * VELOCITIES[i][b]) for i in edge], pair) * w2
            q[b, a] = q[a, b]
    usq = ux * ux + uy * uy + uz * uz
    qu = [q[a, 0] * ux + q[a, 1] * uy + q[a, 2] * uz for a in range(3)]
    p1u = p1[0] * ux + p1[1] * uy + p1[2] * uz
    uqu = ux * qu[0] + uy * qu[1] + uz * qu[2]
    moment = p0 * (1.0 - 1.5 * usq) + 3.0 * p1u + 4.5 * uqu
    vec = [3.0 * p1[a] + 9.0 * qu[a] - 3.0 * u[a] * p0 for a in range(3)]
    vu = vec[0] * ux + vec[1] * uy + vec[2] * uz
    inv = 1.0 / rho
    base = OMEGA * (moment - vu) - ux * inv
    bases = {0: base, 1: base + inv, -1: base - inv}
    wv = [OMEGA * v for v in vec]
    combos = {}
    layers = []
    for i in range(19):
        c = VELOCITIES[i]
        terms = [(a, c[a]) for a in range(3) if c[a] != 0]
        cv = None
        if terms:
            if len(terms) == 1:
                a, s = terms[0]
                cv = wv[a] if s > 0 else -wv[a]
            else:
                (a, s), (b, t) = terms
                pos = (a, b, s * t)
                if pos not in combos:
                    combos[pos] = wv[a] + wv[b] if s * t > 0 else wv[a] - wv[b]
                cv = combos[pos] if s > 0 else -combos[pos]
        val = (1.0 - OMEGA) * pulled[i] + bases[c[0]]
        if cv is not None:
            val = val + cv
        layers.append(jnp.where(fluid, val, pulled[OPPOSITE[i]]))
    sens = None
    for i in range(1, 19, 2):
        c = VELOCITIES[i]
        along = None
        for a in range(3):
            if c[a] == 0:
                continue
            if along is None:
                along = u[a] if c[a] > 0 else -u[a]
            else:
                along = along + u[a] if c[a] > 0 else along - u[a]
        term = (6.0 * WEIGHTS[i]) * along * diff[i]
        sens = term if sens is None else sens + term
    sens = jnp.where(fluid, -(rho * sens), 0.0)
    return layers, sens


def _where(dims):
    me = (lax.axis_index("gx"), lax.axis_index("gy"), lax.axis_index("gz"))

    def exists(d):
        cond = None
        for a in range(3):
            if d[a] == 0:
                continue
            v = me[a] + d[a]
            c = (v >= 0) if d[a] < 0 else (v < dims[a])
            cond = c if cond is None else jnp.logical_and(cond, c)
        return cond

    def target(d):
        return tuple(me[a] + d[a] for a in range(3))

    return me, exists, target


def _zero_missing(exists, xh, yh, exy, mh):
    for d, so, de in _messages(8, 16):
        back = tuple(-v for v in d)

        @pl.when(jnp.logical_not(exists(back)))
        def _():
            if de[0] == "XH":
                xh[de[1]] = jnp.zeros(xh.shape[1:], jnp.float32)
            elif de[0] == "YH":
                yh[de[1]] = jnp.zeros(yh.shape[1:], jnp.float32)
            elif de[0] == "EXY":
                exy[de[1]] = jnp.zeros(exy.shape[1:], jnp.float32)
            else:
                mh[de[1], pl.ds(de[2], de[3]), :] = jnp.zeros((de[3], mh.shape[-1]), jnp.float32)


def _step(s, src, xh, yh, exy, mt, rho_ref, vel_ref, mask_ref, level, emit, before=None):
    cx, cy, cz = 8, 16, 128
    lane = lax.broadcasted_iota(jnp.int32, (cy, cz), 1)
    lane1 = lax.broadcasted_iota(jnp.int32, (1, cz), 1)
    row = lax.broadcasted_iota(jnp.int32, (cy, cz), 0)

    def pulled_plane(p):
        out = []
        for i in range(19):
            vx, vy, vz = VELOCITIES[i]
            q = p + vx
            if 0 <= q < cx:
                plane = src[i, pl.ds(q * cy, cy), :]
            elif q == cx:
                plane = xh[s, 1, CXP.index(i)]
            else:
                plane = xh[s, 0, CXM.index(i)]
            if vz != 0:
                side = 1 if vz > 0 else 0
                if 0 <= q < cx:
                    zc = mt[s, side, pl.ds(q * cy, cy), :]
                    col = ZFACE_COL[i]
                else:
                    col, r0 = XZ_EDGE[i]
                    zc = mt[s, side, pl.ds(r0 % (cx * cy), cy), :]
                if vz > 0:
                    plane = jnp.where(lane == cz - 1, pltpu.roll(zc, (cz - 1 - col) % cz, 1),
                                      pltpu.roll(plane, cz - 1, 1))
                else:
                    plane = jnp.where(lane == 0, pltpu.roll(zc, (cz - col) % cz, 1),
                                      pltpu.roll(plane, 1, 1))
            if vy != 0:
                side_y = 1 if vy > 0 else 0
                ky = CYP.index(i) if vy > 0 else CYM.index(i)
                if 0 <= q < cx:
                    yrow = yh[s, side_y, ky, pl.ds(q, 1), :]
                else:
                    e, r = XY_EDGE[i]
                    yrow = exy[s, e, pl.ds(r, 1), :]
                if vz != 0:
                    side = 1 if vz > 0 else 0
                    colc, yoff = YZ_CORNER[i]
                    crow = mt[s, side, pl.ds(p * cy + yoff % cy, 1), :]
                    if vz > 0:
                        yrow = jnp.where(lane1 == cz - 1, pltpu.roll(crow, (cz - 1 - colc) % cz, 1),
                                         pltpu.roll(yrow, cz - 1, 1))
                    else:
                        yrow = jnp.where(lane1 == 0, pltpu.roll(crow, (cz - colc) % cz, 1),
                                         pltpu.roll(yrow, 1, 1))
                if vy > 0:
                    plane = jnp.where(row == cy - 1, yrow, pltpu.roll(plane, cy - 1, 0))
                else:
                    plane = jnp.where(row == 0, yrow, pltpu.roll(plane, 1, 0))
            out.append(plane)
        return out

    for p in range(cx):
        if before is not None:
            before(p)
        rs = pl.ds(p * cy, cy)
        pulled = pulled_plane(p)
        rho = rho_ref[level, rs, :]
        ux = vel_ref[level, 0, rs, :]
        uy = vel_ref[level, 1, rs, :]
        uz = vel_ref[level, 2, rs, :]
        fluid = mask_ref[rs, :] > 0
        layers, sens = _collide(pulled, rho, ux, uy, uz, fluid)
        emit(p, rs, layers, sens)


def _kernel(dims, adj_hbm, rho_hbm, vel_hbm, mask_hbm,
            mid_out, sens_out, xh_out, yh_out, exy_out, mh_out,
            adj_ref, rho_ref, vel_ref, mask_ref, load_sem,
            mid, sfin, out_sem, xh, yh, exy, sy, sx, nt, mh, mt, send_sem, recv_sem):
    cx, cy, cz = 8, 16, 128
    rows = cx * cy
    me, exists, target = _where(dims)

    barrier = pltpu.get_barrier_semaphore()
    for d in NEIGHBOURS:
        @pl.when(exists(d))
        def _():
            pl.semaphore_signal(barrier, inc=1, device_id=target(d), device_id_type=MESH)

    loads = [
        pltpu.make_async_copy(src, dst, load_sem.at[k])
        for k, (src, dst) in enumerate(
            ((adj_hbm, adj_ref), (vel_hbm, vel_ref), (rho_hbm, rho_ref), (mask_hbm, mask_ref))
        )
    ]
    for copy in loads:
        copy.start()

    mh[0, :, pl.ds(72, rows - 72), :] = jnp.zeros((2, rows - 72, cz), jnp.float32)
    _zero_missing(exists, xh.at[0], yh.at[0], exy.at[0], mh.at[0])

    lane_big = lax.broadcasted_iota(jnp.int32, (rows, cz), 1)
    msgs = _messages(cx, cy)

    def prepare(s, src):
        for side, pops, q in ((0, CXP, 0), (1, CXM, cx - 1)):
            for k, pop in enumerate(pops):
                sx[s, side, k] = src[pop, pl.ds(q * cy, cy), :]
        for side, pops, y in ((0, CYP, 0), (1, CYM, cy - 1)):
            for k, pop in enumerate(pops):
                sy[s, side, k] = src[pop, pl.ds(y, cx, stride=cy), :]
        n = jnp.zeros((rows, cz), jnp.float32)
        for j, (pop, z) in enumerate(ZCOLS):
            zz = z % cz
            n = jnp.where(lane_big == 8 * j, pltpu.roll(src[pop], (8 * j - zz) % cz, 1), n)
        nt[s] = n.T

    def descriptor(s, src, t):
        d, so, de = msgs[t]
        if so[0] == "S":
            sref = src.at[so[1], pl.ds(so[2] % rows, so[3]), :]
        elif so[0] == "SY":
            sref = sy.at[s, so[1]]
        elif so[0] == "SX":
            sref = sx.at[s, so[1]]
        else:
            sref = nt.at[s, pl.ds(so[1], so[2]), :]
        bufs = {"XH": (xh.at[0], xh_out), "YH": (yh.at[0], yh_out), "EXY": (exy.at[0], exy_out),
                "MH": (mh.at[0], mh_out)}[de[0]][s]
        if de[0] == "MH":
            dref = bufs.at[de[1], pl.ds(de[2], de[3]), :]
        else:
            dref = bufs.at[de[1]]
        return pltpu.make_async_remote_copy(
            src_ref=sref, dst_ref=dref, send_sem=send_sem.at[s, t], recv_sem=recv_sem.at[s, t],
            device_id=target(d), device_id_type=MESH)

    def send(s, src):
        for t in range(len(msgs)):
            @pl.when(exists(msgs[t][0]))
            def _():
                descriptor(s, src, t).start()

    def finish(s, src):
        for t in range(len(msgs)):
            d = msgs[t][0]
            back = tuple(-v for v in d)

            @pl.when(exists(back))
            def _():
                descriptor(s, src, t).wait_recv()

            @pl.when(exists(d))
            def _():
                descriptor(s, src, t).wait_send()

    peers = 0
    for d in NEIGHBOURS:
        term = 1
        for a in range(3):
            n = dims[a]
            if d[a] < 0:
                term = term * ((me[a] + n - 1) // n)
            elif d[a] > 0:
                term = term * ((2 * n - 2 - me[a]) // n)
        peers = peers + term
    loads[0].wait()
    prepare(0, adj_ref)
    pl.semaphore_wait(barrier, peers)
    send(0, adj_ref)
    for copy in loads[1:]:
        copy.wait()
    finish(0, adj_ref)
    for side in range(2):
        mt[0, side] = mh[0, side].T

    def flush(p):
        rs = pl.ds(p * cy, cy)
        pltpu.make_async_copy(mid.at[:, rs, :], mid_out.at[:, rs, :], out_sem.at[p]).start()

    def emit(p, rs, layers, sens):
        for i in range(19):
            mid[i, rs, :] = layers[i]
        sfin[rs, :] = sens

    _step(0, adj_ref, xh, yh, exy, mt, rho_ref, vel_ref, mask_ref, 1, emit,
          before=lambda p: flush(p - 1) if p >= 1 else None)
    prepare(1, mid)
    send(1, mid)
    flush(cx - 1)
    sens_copy = pltpu.make_async_copy(sfin, sens_out, out_sem.at[cx])
    sens_copy.start()
    finish(1, mid)
    for p in range(cx):
        rs = pl.ds(p * cy, cy)
        pltpu.make_async_copy(mid.at[:, rs, :], mid_out.at[:, rs, :], out_sem.at[p]).wait()
    sens_copy.wait()


def _last(dims, mid_hbm, s1_hbm, xh_hbm, yh_hbm, exy_hbm, mh_hbm, rho_hbm, vel_hbm, mask_hbm,
          out_hbm, sens_hbm,
          mid, s1, xh, yh, exy, mh, mt, rho, vel, mask, fin, sfin, in_sem, out_sem):
    cx, cy, cz = 8, 16, 128
    rows = cx * cy
    me, exists, target = _where(dims)
    mh[...] = jnp.zeros(mh.shape, jnp.float32)
    used = 72
    loads = [
        pltpu.make_async_copy(xh_hbm, xh.at[0], in_sem.at[0]),
        pltpu.make_async_copy(yh_hbm, yh.at[0], in_sem.at[1]),
        pltpu.make_async_copy(exy_hbm, exy.at[0], in_sem.at[2]),
        pltpu.make_async_copy(mh_hbm.at[:, pl.ds(0, used), :], mh.at[:, pl.ds(0, used), :], in_sem.at[3]),
        pltpu.make_async_copy(rho_hbm.at[pl.ds(0, 1)], rho, in_sem.at[4]),
        pltpu.make_async_copy(vel_hbm.at[pl.ds(0, 1)], vel, in_sem.at[5]),
        pltpu.make_async_copy(mask_hbm, mask, in_sem.at[6]),
        pltpu.make_async_copy(s1_hbm, s1, in_sem.at[7]),
        pltpu.make_async_copy(mid_hbm, mid, in_sem.at[8]),
    ]
    for copy in loads:
        copy.start()
    for copy in loads:
        copy.wait()
    _zero_missing(exists, xh.at[0], yh.at[0], exy.at[0], mh)

    for side in range(2):
        mt[0, side] = mh[side].T

    def flush(p):
        rs = pl.ds(p * cy, cy)
        pltpu.make_async_copy(fin.at[:, rs, :], out_hbm.at[:, rs, :], out_sem.at[p]).start()

    def emit(p, rs, layers, sens):
        for i in range(19):
            fin[i, rs, :] = layers[i]
        sfin[rs, :] = s1[rs, :] + sens

    _step(0, mid, xh, yh, exy, mt, rho, vel, mask, 0, emit,
          before=lambda p: flush(p - 1) if p >= 1 else None)
    flush(cx - 1)
    sens_copy = pltpu.make_async_copy(sfin, sens_hbm, out_sem.at[cx])
    sens_copy.start()
    for p in range(cx):
        rs = pl.ds(p * cy, cy)
        pltpu.make_async_copy(fin.at[:, rs, :], out_hbm.at[:, rs, :], out_sem.at[p]).wait()
    sens_copy.wait()


def solution(mesh):
    dims = (mesh.shape["gx"], mesh.shape["gy"], mesh.shape["gz"])
    nmsg = len(_messages(8, 16))

    def shards(adjoint, density, velocity, pore_mask):
        npop, cx, cy, cz = adjoint.shape
        assert (cx, cy, cz) == (8, 16, 128)
        rows = cx * cy
        adj = adjoint.reshape(npop, rows, cz)
        rho = density.reshape(2, rows, cz)
        vel = velocity.reshape(2, 3, rows, cz)
        mask = pore_mask.reshape(rows, cz)
        hbm = pl.BlockSpec(memory_space=pltpu.HBM)
        f32 = jnp.float32
        halo_shapes = (
            jax.ShapeDtypeStruct((2, 5, cy, cz), f32),
            jax.ShapeDtypeStruct((2, 5, cx, cz), f32),
            jax.ShapeDtypeStruct((4, 8, cz), f32),
            jax.ShapeDtypeStruct((2, rows, cz), f32),
        )
        mid, s1, xh2, yh2, exy2, mh2 = pl.pallas_call(
            functools.partial(_kernel, dims),
            out_shape=(
                jax.ShapeDtypeStruct((npop, rows, cz), f32),
                jax.ShapeDtypeStruct((rows, cz), f32),
            ) + halo_shapes,
            in_specs=[hbm] * 4,
            out_specs=(hbm,) * 6,
            scratch_shapes=[
                pltpu.VMEM((npop, rows, cz), f32),
                pltpu.VMEM((2, rows, cz), f32),
                pltpu.VMEM((2, 3, rows, cz), f32),
                pltpu.VMEM((rows, cz), jnp.int32),
                pltpu.SemaphoreType.DMA((4,)),
                pltpu.VMEM((npop, rows, cz), f32),
                pltpu.VMEM((rows, cz), f32),
                pltpu.SemaphoreType.DMA((cx + 1,)),
                pltpu.VMEM((1, 2, 5, cy, cz), f32),
                pltpu.VMEM((1, 2, 5, cx, cz), f32),
                pltpu.VMEM((1, 4, 8, cz), f32),
                pltpu.VMEM((2, 2, 5, cx, cz), f32),
                pltpu.VMEM((2, 2, 5, cy, cz), f32),
                pltpu.VMEM((2, rows, cz), f32),
                pltpu.VMEM((1, 2, rows, cz), f32),
                pltpu.VMEM((1, 2, rows, cz), f32),
                pltpu.SemaphoreType.DMA((2, nmsg)),
                pltpu.SemaphoreType.DMA((2, nmsg)),
            ],
            compiler_params=pltpu.CompilerParams(
                collective_id=0, has_side_effects=True, vmem_limit_bytes=67043328
            ),
        )(adj, rho, vel, mask)
        out, sens = pl.pallas_call(
            functools.partial(_last, dims),
            out_shape=(
                jax.ShapeDtypeStruct((npop, rows, cz), f32),
                jax.ShapeDtypeStruct((rows, cz), f32),
            ),
            in_specs=[hbm] * 9,
            out_specs=(hbm, hbm),
            scratch_shapes=[
                pltpu.VMEM((npop, rows, cz), f32),
                pltpu.VMEM((rows, cz), f32),
                pltpu.VMEM((1, 2, 5, cy, cz), f32),
                pltpu.VMEM((1, 2, 5, cx, cz), f32),
                pltpu.VMEM((1, 4, 8, cz), f32),
                pltpu.VMEM((2, rows, cz), f32),
                pltpu.VMEM((1, 2, rows, cz), f32),
                pltpu.VMEM((1, rows, cz), f32),
                pltpu.VMEM((1, 3, rows, cz), f32),
                pltpu.VMEM((rows, cz), jnp.int32),
                pltpu.VMEM((npop, rows, cz), f32),
                pltpu.VMEM((rows, cz), f32),
                pltpu.SemaphoreType.DMA((9,)),
                pltpu.SemaphoreType.DMA((cx + 1,)),
            ],
            compiler_params=pltpu.CompilerParams(vmem_limit_bytes=67043328),
        )(mid, s1, xh2, yh2, exy2, mh2, rho, vel, mask)
        return out.reshape(npop, cx, cy, cz), sens.reshape(cx, cy, cz)

    placed = (
        P(None, "gx", "gy", "gz"),
        P(None, "gx", "gy", "gz"),
        P(None, None, "gx", "gy", "gz"),
        P("gx", "gy", "gz"),
    )
    return jax.shard_map(
        shards,
        mesh=mesh,
        in_specs=placed,
        out_specs=(P(None, "gx", "gy", "gz"), P("gx", "gy", "gz")),
        check_vma=False,
    )
```

```python
import functools

import jax
import jax.numpy as jnp
from jax import lax
from jax.experimental import pallas as pl
from jax.experimental.pallas import tpu as pltpu
from jax.sharding import PartitionSpec as P

VELOCITIES = [
    (0, 0, 0),
    (1, 0, 0),
    (-1, 0, 0),
    (0, 1, 0),
    (0, -1, 0),
    (0, 0, 1),
    (0, 0, -1),
    (1, 1, 0),
    (-1, -1, 0),
    (1, -1, 0),
    (-1, 1, 0),
    (1, 0, 1),
    (-1, 0, -1),
    (1, 0, -1),
    (-1, 0, 1),
    (0, 1, 1),
    (0, -1, -1),
    (0, 1, -1),
    (0, -1, 1),
]
WEIGHTS = [1.0 / 3.0] + [1.0 / 18.0] * 6 + [1.0 / 36.0] * 12
OPPOSITE = [0, 2, 1, 4, 3, 6, 5, 8, 7, 10, 9, 12, 11, 14, 13, 16, 15, 18, 17]
OMEGA = 1.25
MESH = pl.DeviceIdType.MESH

CXP = [1, 7, 9, 11, 13]
CXM = [2, 8, 10, 12, 14]
CYP = [3, 7, 10, 15, 17]
CYM = [4, 8, 9, 16, 18]
ZCOLS = [(5, 0), (11, 0), (14, 0), (15, 0), (18, 0), (6, -1), (12, -1), (13, -1), (16, -1), (17, -1)]
ZFACE_COL = {5: 0, 11: 8, 14: 16, 15: 24, 18: 32, 6: 0, 12: 8, 13: 16, 16: 24, 17: 32}
XZ_EDGE = {11: (40, 0), 14: (48, -16), 12: (40, -16), 13: (48, 0)}
YZ_CORNER = {15: (56, 0), 18: (64, -1), 16: (56, -1), 17: (64, 0)}
XY_EDGE = {7: (0, 0), 8: (1, 7), 9: (2, 7), 10: (3, 0)}


def _messages(cx, cy):
    rows = cx * cy
    msgs = []
    msgs.append(((0, -1, 0), ("SY", 0), ("YH", 1)))
    msgs.append(((0, 1, 0), ("SY", 1), ("YH", 0)))
    msgs.append(((0, -1, -1), ("NT", 24, 8), ("MH", 1, 56, 8)))
    msgs.append(((0, 1, -1), ("NT", 32, 8), ("MH", 1, 64, 8)))
    msgs.append(((0, 1, 1), ("NT", 64, 8), ("MH", 0, 56, 8)))
    msgs.append(((0, -1, 1), ("NT", 72, 8), ("MH", 0, 64, 8)))
    msgs.append(((-1, -1, 0), ("S", 7, 0, 8), ("EXY", 0)))
    msgs.append(((1, 1, 0), ("S", 8, rows - 8, 8), ("EXY", 1)))
    msgs.append(((-1, 1, 0), ("S", 9, cy - 8, 8), ("EXY", 2)))
    msgs.append(((1, -1, 0), ("S", 10, rows - cy, 8), ("EXY", 3)))
    msgs.append(((0, 0, -1), ("NT", 0, 40), ("MH", 1, 0, 40)))
    msgs.append(((0, 0, 1), ("NT", 40, 40), ("MH", 0, 0, 40)))
    msgs.append(((-1, 0, -1), ("NT", 8, 8), ("MH", 1, 40, 8)))
    msgs.append(((1, 0, -1), ("NT", 16, 8), ("MH", 1, 48, 8)))
    msgs.append(((1, 0, 1), ("NT", 48, 8), ("MH", 0, 40, 8)))
    msgs.append(((-1, 0, 1), ("NT", 56, 8), ("MH", 0, 48, 8)))
    msgs.append(((-1, 0, 0), ("SX", 0), ("XH", 1)))
    msgs.append(((1, 0, 0), ("SX", 1), ("XH", 0)))
    return msgs


NEIGHBOURS = sorted(
    {d for d, _, _ in _messages(8, 16)} | {tuple(-v for v in d) for d, _, _ in _messages(8, 16)}
)


def _comb(vals, fn):
    total = None
    for weight in (1.0 / 3.0, 1.0 / 18.0, 1.0 / 36.0):
        part = None
        for i in range(19):
            if WEIGHTS[i] != weight:
                continue
            k = fn(VELOCITIES[i])
            if k == 0:
                continue
            if part is None:
                part = vals[i] if k > 0 else -vals[i]
            else:
                part = part + vals[i] if k > 0 else part - vals[i]
        if part is not None:
            term = part * weight
            total = term if total is None else total + term
    return total


def _collide(pulled, rho, ux, uy, uz, fluid):
    u = (ux, uy, uz)
    pair = {i: pulled[i] + pulled[i + 1] for i in range(1, 19, 2)}
    diff = {i: pulled[i] - pulled[i + 1] for i in range(1, 19, 2)}
    w1, w2 = 1.0 / 18.0, 1.0 / 36.0

    def signed(terms, table):
        total = None
        for i, sgn in terms:
            v = table[i]
            if total is None:
                total = v if sgn > 0 else -v
            else:
                total = total + v if sgn > 0 else total - v
        return total

    edges = [i for i in range(7, 19, 2)]
    p0 = pulled[0] * (1.0 / 3.0) + (pair[1] + pair[3] + pair[5]) * w1 + signed([(i, 1) for i in edges], pair) * w2
    p1 = []
    q = {}
    for a, axis_pop in enumerate((1, 3, 5)):
        edge = [i for i in edges if VELOCITIES[i][a] != 0]
        p1.append(diff[axis_pop] * w1 + signed([(i, VELOCITIES[i][a]) for i in edge], diff) * w2)
        q[a, a] = pair[axis_pop] * w1 + signed([(i, 1) for i in edge], pair) * w2
    for a in range(3):
        for b in range(a + 1, 3):
            edge = [i for i in edges if VELOCITIES[i][a] != 0 and VELOCITIES[i][b] != 0]
            q[a, b] = signed([(i, VELOCITIES[i][a] * VELOCITIES[i][b]) for i in edge], pair) * w2
            q[b, a] = q[a, b]
    usq = ux * ux + uy * uy + uz * uz
    qu = [q[a, 0] * ux + q[a, 1] * uy + q[a, 2] * uz for a in range(3)]
    p1u = p1[0] * ux + p1[1] * uy + p1[2] * uz
    uqu = ux * qu[0] + uy * qu[1] + uz * qu[2]
    moment = p0 * (1.0 - 1.5 * usq) + 3.0 * p1u + 4.5 * uqu
    vec = [3.0 * p1[a] + 9.0 * qu[a] - 3.0 * u[a] * p0 for a in range(3)]
    vu = vec[0] * ux + vec[1] * uy + vec[2] * uz
    inv = 1.0 / rho
    base = OMEGA * (moment - vu) - ux * inv
    bases = {0: base, 1: base + inv, -1: base - inv}
    wv = [OMEGA * v for v in vec]
    combos = {}
    layers = []
    for i in range(19):
        c = VELOCITIES[i]
        terms = [(a, c[a]) for a in range(3) if c[a] != 0]
        cv = None
        if terms:
            if len(terms) == 1:
                a, s = terms[0]
                cv = wv[a] if s > 0 else -wv[a]
            else:
                (a, s), (b, t) = terms
                pos = (a, b, s * t)
                if pos not in combos:
                    combos[pos] = wv[a] + wv[b] if s * t > 0 else wv[a] - wv[b]
                cv = combos[pos] if s > 0 else -combos[pos]
        val = (1.0 - OMEGA) * pulled[i] + bases[c[0]]
        if cv is not None:
            val = val + cv
        layers.append(jnp.where(fluid, val, pulled[OPPOSITE[i]]))
    sens = None
    for i in range(1, 19, 2):
        c = VELOCITIES[i]
        along = None
        for a in range(3):
            if c[a] == 0:
                continue
            if along is None:
                along = u[a] if c[a] > 0 else -u[a]
            else:
                along = along + u[a] if c[a] > 0 else along - u[a]
        term = (6.0 * WEIGHTS[i]) * along * diff[i]
        sens = term if sens is None else sens + term
    sens = jnp.where(fluid, -(rho * sens), 0.0)
    return layers, sens


def _where(dims):
    me = (lax.axis_index("gx"), lax.axis_index("gy"), lax.axis_index("gz"))

    def exists(d):
        cond = None
        for a in range(3):
            if d[a] == 0:
                continue
            v = me[a] + d[a]
            c = (v >= 0) if d[a] < 0 else (v < dims[a])
            cond = c if cond is None else jnp.logical_and(cond, c)
        return cond

    def target(d):
        return tuple(me[a] + d[a] for a in range(3))

    return me, exists, target


def _zero_missing(exists, xh, yh, exy, mh):
    for d, so, de in _messages(8, 16):
        back = tuple(-v for v in d)

        @pl.when(jnp.logical_not(exists(back)))
        def _():
            if de[0] == "XH":
                xh[de[1]] = jnp.zeros(xh.shape[1:], jnp.float32)
            elif de[0] == "YH":
                yh[de[1]] = jnp.zeros(yh.shape[1:], jnp.float32)
            elif de[0] == "EXY":
                exy[de[1]] = jnp.zeros(exy.shape[1:], jnp.float32)
            else:
                mh[de[1], pl.ds(de[2], de[3]), :] = jnp.zeros((de[3], mh.shape[-1]), jnp.float32)


def _step(s, src, xh, yh, exy, mt, rho_ref, vel_ref, mask_ref, level, emit, before=None):
    cx, cy, cz = 8, 16, 128
    lane = lax.broadcasted_iota(jnp.int32, (cy, cz), 1)
    lane1 = lax.broadcasted_iota(jnp.int32, (1, cz), 1)
    row = lax.broadcasted_iota(jnp.int32, (cy, cz), 0)

    def pulled_plane(p):
        out = []
        for i in range(19):
            vx, vy, vz = VELOCITIES[i]
            q = p + vx
            if 0 <= q < cx:
                plane = src[i, pl.ds(q * cy, cy), :]
            elif q == cx:
                plane = xh[s, 1, CXP.index(i)]
            else:
                plane = xh[s, 0, CXM.index(i)]
            if vz != 0:
                side = 1 if vz > 0 else 0
                if 0 <= q < cx:
                    zc = mt[s, side, pl.ds(q * cy, cy), :]
                    col = ZFACE_COL[i]
                else:
                    col, r0 = XZ_EDGE[i]
                    zc = mt[s, side, pl.ds(r0 % (cx * cy), cy), :]
                if vz > 0:
                    plane = jnp.where(lane == cz - 1, pltpu.roll(zc, (cz - 1 - col) % cz, 1),
                                      pltpu.roll(plane, cz - 1, 1))
                else:
                    plane = jnp.where(lane == 0, pltpu.roll(zc, (cz - col) % cz, 1),
                                      pltpu.roll(plane, 1, 1))
            if vy != 0:
                side_y = 1 if vy > 0 else 0
                ky = CYP.index(i) if vy > 0 else CYM.index(i)
                if 0 <= q < cx:
                    yrow = yh[s, side_y, ky, pl.ds(q, 1), :]
                else:
                    e, r = XY_EDGE[i]
                    yrow = exy[s, e, pl.ds(r, 1), :]
                if vz != 0:
                    side = 1 if vz > 0 else 0
                    colc, yoff = YZ_CORNER[i]
                    crow = mt[s, side, pl.ds(p * cy + yoff % cy, 1), :]
                    if vz > 0:
                        yrow = jnp.where(lane1 == cz - 1, pltpu.roll(crow, (cz - 1 - colc) % cz, 1),
                                         pltpu.roll(yrow, cz - 1, 1))
                    else:
                        yrow = jnp.where(lane1 == 0, pltpu.roll(crow, (cz - colc) % cz, 1),
                                         pltpu.roll(yrow, 1, 1))
                if vy > 0:
                    plane = jnp.where(row == cy - 1, yrow, pltpu.roll(plane, cy - 1, 0))
                else:
                    plane = jnp.where(row == 0, yrow, pltpu.roll(plane, 1, 0))
            out.append(plane)
        return out

    for p in range(cx):
        if before is not None:
            before(p)
        rs = pl.ds(p * cy, cy)
        pulled = pulled_plane(p)
        rho = rho_ref[level, rs, :]
        ux = vel_ref[level, 0, rs, :]
        uy = vel_ref[level, 1, rs, :]
        uz = vel_ref[level, 2, rs, :]
        fluid = mask_ref[rs, :] > 0
        layers, sens = _collide(pulled, rho, ux, uy, uz, fluid)
        emit(p, rs, layers, sens)


def _kernel(dims, adj_hbm, rho_hbm, vel_hbm, mask_hbm,
            mid_out, sens_out, xh_out, yh_out, exy_out, mh_out,
            adj_ref, rho_ref, vel_ref, mask_ref, load_sem,
            mid, sfin, out_sem, xh, yh, exy, sy, sx, nt, mh, mt, send_sem, recv_sem):
    cx, cy, cz = 8, 16, 128
    rows = cx * cy
    me, exists, target = _where(dims)

    barrier = pltpu.get_barrier_semaphore()
    for d in NEIGHBOURS:
        @pl.when(exists(d))
        def _():
            pl.semaphore_signal(barrier, inc=1, device_id=target(d), device_id_type=MESH)

    loads = [
        pltpu.make_async_copy(src, dst, load_sem.at[k])
        for k, (src, dst) in enumerate(
            ((adj_hbm, adj_ref), (vel_hbm, vel_ref), (rho_hbm, rho_ref), (mask_hbm, mask_ref))
        )
    ]
    for copy in loads:
        copy.start()

    mh[0, :, pl.ds(72, rows - 72), :] = jnp.zeros((2, rows - 72, cz), jnp.float32)
    _zero_missing(exists, xh.at[0], yh.at[0], exy.at[0], mh.at[0])

    lane_big = lax.broadcasted_iota(jnp.int32, (rows, cz), 1)
    msgs = _messages(cx, cy)

    def prepare(s, src):
        for side, pops, q in ((0, CXP, 0), (1, CXM, cx - 1)):
            for k, pop in enumerate(pops):
                sx[s, side, k] = src[pop, pl.ds(q * cy, cy), :]
        for side, pops, y in ((0, CYP, 0), (1, CYM, cy - 1)):
            for k, pop in enumerate(pops):
                sy[s, side, k] = src[pop, pl.ds(y, cx, stride=cy), :]
        n = jnp.zeros((rows, cz), jnp.float32)
        for j, (pop, z) in enumerate(ZCOLS):
            zz = z % cz
            n = jnp.where(lane_big == 8 * j, pltpu.roll(src[pop], (8 * j - zz) % cz, 1), n)
        nt[s] = n.T

    def descriptor(s, src, t):
        d, so, de = msgs[t]
        if so[0] == "S":
            sref = src.at[so[1], pl.ds(so[2] % rows, so[3]), :]
        elif so[0] == "SY":
            sref = sy.at[s, so[1]]
        elif so[0] == "SX":
            sref = sx.at[s, so[1]]
        else:
            sref = nt.at[s, pl.ds(so[1], so[2]), :]
        bufs = {"XH": (xh.at[0], xh_out), "YH": (yh.at[0], yh_out), "EXY": (exy.at[0], exy_out),
                "MH": (mh.at[0], mh_out)}[de[0]][s]
        if de[0] == "MH":
            dref = bufs.at[de[1], pl.ds(de[2], de[3]), :]
        else:
            dref = bufs.at[de[1]]
        return pltpu.make_async_remote_copy(
            src_ref=sref, dst_ref=dref, send_sem=send_sem.at[s, t], recv_sem=recv_sem.at[s, t],
            device_id=target(d), device_id_type=MESH)

    def send(s, src):
        for t in range(len(msgs)):
            @pl.when(exists(msgs[t][0]))
            def _():
                descriptor(s, src, t).start()

    def finish(s, src):
        for t in range(len(msgs)):
            d = msgs[t][0]
            back = tuple(-v for v in d)

            @pl.when(exists(back))
            def _():
                descriptor(s, src, t).wait_recv()

            @pl.when(exists(d))
            def _():
                descriptor(s, src, t).wait_send()

    peers = 0
    for d in NEIGHBOURS:
        term = 1
        for a in range(3):
            n = dims[a]
            if d[a] < 0:
                term = term * ((me[a] + n - 1) // n)
            elif d[a] > 0:
                term = term * ((2 * n - 2 - me[a]) // n)
        peers = peers + term
    loads[0].wait()
    prepare(0, adj_ref)
    pl.semaphore_wait(barrier, peers)
    send(0, adj_ref)
    for copy in loads[1:]:
        copy.wait()
    finish(0, adj_ref)
    for side in range(2):
        mt[0, side] = mh[0, side].T

    def flush(p):
        rs = pl.ds(p * cy, cy)
        pltpu.make_async_copy(mid.at[:, rs, :], mid_out.at[p], out_sem.at[p]).start()

    def emit(p, rs, layers, sens):
        for i in range(19):
            mid[i, rs, :] = layers[i]
        sfin[rs, :] = sens

    _step(0, adj_ref, xh, yh, exy, mt, rho_ref, vel_ref, mask_ref, 1, emit,
          before=lambda p: flush(p - 1) if p >= 1 else None)
    prepare(1, mid)
    send(1, mid)
    flush(cx - 1)
    sens_copy = pltpu.make_async_copy(sfin, sens_out, out_sem.at[cx])
    sens_copy.start()
    finish(1, mid)
    for p in range(cx):
        rs = pl.ds(p * cy, cy)
        pltpu.make_async_copy(mid.at[:, rs, :], mid_out.at[p], out_sem.at[p]).wait()
    sens_copy.wait()


def _last(dims, mid_hbm, s1_hbm, xh_hbm, yh_hbm, exy_hbm, mh_hbm, rho_hbm, vel_hbm, mask_hbm,
          out_hbm, sens_hbm,
          mid, s1, xh, yh, exy, mh, mt, rho, vel, mask, fin, sfin, in_sem, out_sem):
    cx, cy, cz = 8, 16, 128
    rows = cx * cy
    me, exists, target = _where(dims)
    mh[...] = jnp.zeros(mh.shape, jnp.float32)
    used = 72
    loads = [
        pltpu.make_async_copy(xh_hbm, xh.at[0], in_sem.at[0]),
        pltpu.make_async_copy(yh_hbm, yh.at[0], in_sem.at[1]),
        pltpu.make_async_copy(exy_hbm, exy.at[0], in_sem.at[2]),
        pltpu.make_async_copy(mh_hbm.at[:, pl.ds(0, used), :], mh.at[:, pl.ds(0, used), :], in_sem.at[3]),
        pltpu.make_async_copy(rho_hbm.at[pl.ds(0, 1)], rho, in_sem.at[4]),
        pltpu.make_async_copy(vel_hbm.at[pl.ds(0, 1)], vel, in_sem.at[5]),
        pltpu.make_async_copy(mask_hbm, mask, in_sem.at[6]),
        pltpu.make_async_copy(s1_hbm, s1, in_sem.at[7]),
    ]
    planes = [
        pltpu.make_async_copy(mid_hbm.at[p], mid.at[:, pl.ds(p * cy, cy), :], in_sem.at[8 + p])
        for p in range(cx)
    ]
    for copy in planes[:2]:
        copy.start()
    for copy in loads:
        copy.start()
    for copy in planes[2:]:
        copy.start()
    for copy in loads:
        copy.wait()
    _zero_missing(exists, xh.at[0], yh.at[0], exy.at[0], mh)

    for side in range(2):
        mt[0, side] = mh[side].T

    def flush(p):
        rs = pl.ds(p * cy, cy)
        pltpu.make_async_copy(fin.at[:, rs, :], out_hbm.at[:, rs, :], out_sem.at[p]).start()

    def emit(p, rs, layers, sens):
        for i in range(19):
            fin[i, rs, :] = layers[i]
        sfin[rs, :] = s1[rs, :] + sens

    def before(p):
        if p == 0:
            planes[0].wait()
        if p + 1 < cx:
            planes[p + 1].wait()
        if p >= 1:
            flush(p - 1)

    _step(0, mid, xh, yh, exy, mt, rho, vel, mask, 0, emit, before=before)
    flush(cx - 1)
    sens_copy = pltpu.make_async_copy(sfin, sens_hbm, out_sem.at[cx])
    sens_copy.start()
    for p in range(cx):
        rs = pl.ds(p * cy, cy)
        pltpu.make_async_copy(fin.at[:, rs, :], out_hbm.at[:, rs, :], out_sem.at[p]).wait()
    sens_copy.wait()


def solution(mesh):
    dims = (mesh.shape["gx"], mesh.shape["gy"], mesh.shape["gz"])
    nmsg = len(_messages(8, 16))

    def shards(adjoint, density, velocity, pore_mask):
        npop, cx, cy, cz = adjoint.shape
        assert (cx, cy, cz) == (8, 16, 128)
        rows = cx * cy
        adj = adjoint.reshape(npop, rows, cz)
        rho = density.reshape(2, rows, cz)
        vel = velocity.reshape(2, 3, rows, cz)
        mask = pore_mask.reshape(rows, cz)
        hbm = pl.BlockSpec(memory_space=pltpu.HBM)
        f32 = jnp.float32
        halo_shapes = (
            jax.ShapeDtypeStruct((2, 5, cy, cz), f32),
            jax.ShapeDtypeStruct((2, 5, cx, cz), f32),
            jax.ShapeDtypeStruct((4, 8, cz), f32),
            jax.ShapeDtypeStruct((2, rows, cz), f32),
        )
        mid, s1, xh2, yh2, exy2, mh2 = pl.pallas_call(
            functools.partial(_kernel, dims),
            out_shape=(
                jax.ShapeDtypeStruct((cx, npop, cy, cz), f32),
                jax.ShapeDtypeStruct((rows, cz), f32),
            ) + halo_shapes,
            in_specs=[hbm] * 4,
            out_specs=(hbm,) * 6,
            scratch_shapes=[
                pltpu.VMEM((npop, rows, cz), f32),
                pltpu.VMEM((2, rows, cz), f32),
                pltpu.VMEM((2, 3, rows, cz), f32),
                pltpu.VMEM((rows, cz), jnp.int32),
                pltpu.SemaphoreType.DMA((4,)),
                pltpu.VMEM((npop, rows, cz), f32),
                pltpu.VMEM((rows, cz), f32),
                pltpu.SemaphoreType.DMA((cx + 1,)),
                pltpu.VMEM((1, 2, 5, cy, cz), f32),
                pltpu.VMEM((1, 2, 5, cx, cz), f32),
                pltpu.VMEM((1, 4, 8, cz), f32),
                pltpu.VMEM((2, 2, 5, cx, cz), f32),
                pltpu.VMEM((2, 2, 5, cy, cz), f32),
                pltpu.VMEM((2, rows, cz), f32),
                pltpu.VMEM((1, 2, rows, cz), f32),
                pltpu.VMEM((1, 2, rows, cz), f32),
                pltpu.SemaphoreType.DMA((2, nmsg)),
                pltpu.SemaphoreType.DMA((2, nmsg)),
            ],
            compiler_params=pltpu.CompilerParams(
                collective_id=0, has_side_effects=True, vmem_limit_bytes=67043328
            ),
        )(adj, rho, vel, mask)
        out, sens = pl.pallas_call(
            functools.partial(_last, dims),
            out_shape=(
                jax.ShapeDtypeStruct((npop, rows, cz), f32),
                jax.ShapeDtypeStruct((rows, cz), f32),
            ),
            in_specs=[hbm] * 9,
            out_specs=(hbm, hbm),
            scratch_shapes=[
                pltpu.VMEM((npop, rows, cz), f32),
                pltpu.VMEM((rows, cz), f32),
                pltpu.VMEM((1, 2, 5, cy, cz), f32),
                pltpu.VMEM((1, 2, 5, cx, cz), f32),
                pltpu.VMEM((1, 4, 8, cz), f32),
                pltpu.VMEM((2, rows, cz), f32),
                pltpu.VMEM((1, 2, rows, cz), f32),
                pltpu.VMEM((1, rows, cz), f32),
                pltpu.VMEM((1, 3, rows, cz), f32),
                pltpu.VMEM((rows, cz), jnp.int32),
                pltpu.VMEM((npop, rows, cz), f32),
                pltpu.VMEM((rows, cz), f32),
                pltpu.SemaphoreType.DMA((8 + cx,)),
                pltpu.SemaphoreType.DMA((cx + 1,)),
            ],
            compiler_params=pltpu.CompilerParams(vmem_limit_bytes=67043328),
        )(mid, s1, xh2, yh2, exy2, mh2, rho, vel, mask)
        return out.reshape(npop, cx, cy, cz), sens.reshape(cx, cy, cz)

    placed = (
        P(None, "gx", "gy", "gz"),
        P(None, "gx", "gy", "gz"),
        P(None, None, "gx", "gy", "gz"),
        P("gx", "gy", "gz"),
    )
    return jax.shard_map(
        shards,
        mesh=mesh,
        in_specs=placed,
        out_specs=(P(None, "gx", "gy", "gz"), P("gx", "gy", "gz")),
        check_vma=False,
    )
```

```python
import functools

import jax
import jax.numpy as jnp
from jax import lax
from jax.experimental import pallas as pl
from jax.experimental.pallas import tpu as pltpu
from jax.sharding import PartitionSpec as P

VELOCITIES = [
    (0, 0, 0),
    (1, 0, 0),
    (-1, 0, 0),
    (0, 1, 0),
    (0, -1, 0),
    (0, 0, 1),
    (0, 0, -1),
    (1, 1, 0),
    (-1, -1, 0),
    (1, -1, 0),
    (-1, 1, 0),
    (1, 0, 1),
    (-1, 0, -1),
    (1, 0, -1),
    (-1, 0, 1),
    (0, 1, 1),
    (0, -1, -1),
    (0, 1, -1),
    (0, -1, 1),
]
WEIGHTS = [1.0 / 3.0] + [1.0 / 18.0] * 6 + [1.0 / 36.0] * 12
OPPOSITE = [0, 2, 1, 4, 3, 6, 5, 8, 7, 10, 9, 12, 11, 14, 13, 16, 15, 18, 17]
OMEGA = 1.25
MESH = pl.DeviceIdType.MESH

CXP = [1, 7, 9, 11, 13]
CXM = [2, 8, 10, 12, 14]
CYP = [3, 7, 10, 15, 17]
CYM = [4, 8, 9, 16, 18]
ZCOLS = [(5, 0), (11, 0), (14, 0), (15, 0), (18, 0), (6, -1), (12, -1), (13, -1), (16, -1), (17, -1)]
ZFACE_COL = {5: 0, 11: 8, 14: 16, 15: 24, 18: 32, 6: 0, 12: 8, 13: 16, 16: 24, 17: 32}
XZ_EDGE = {11: (40, 0), 14: (48, -16), 12: (40, -16), 13: (48, 0)}
YZ_CORNER = {15: (56, 0), 18: (64, -1), 16: (56, -1), 17: (64, 0)}
XY_EDGE = {7: (0, 0), 8: (1, 7), 9: (2, 7), 10: (3, 0)}


def _messages(cx, cy):
    rows = cx * cy
    msgs = []
    msgs.append(((0, -1, 0), ("SY", 0), ("YH", 1)))
    msgs.append(((0, 1, 0), ("SY", 1), ("YH", 0)))
    msgs.append(((0, -1, -1), ("NT", 24, 8), ("MH", 1, 56, 8)))
    msgs.append(((0, 1, -1), ("NT", 32, 8), ("MH", 1, 64, 8)))
    msgs.append(((0, 1, 1), ("NT", 64, 8), ("MH", 0, 56, 8)))
    msgs.append(((0, -1, 1), ("NT", 72, 8), ("MH", 0, 64, 8)))
    msgs.append(((-1, -1, 0), ("S", 7, 0, 8), ("EXY", 0)))
    msgs.append(((1, 1, 0), ("S", 8, rows - 8, 8), ("EXY", 1)))
    msgs.append(((-1, 1, 0), ("S", 9, cy - 8, 8), ("EXY", 2)))
    msgs.append(((1, -1, 0), ("S", 10, rows - cy, 8), ("EXY", 3)))
    msgs.append(((0, 0, -1), ("NT", 0, 40), ("MH", 1, 0, 40)))
    msgs.append(((0, 0, 1), ("NT", 40, 40), ("MH", 0, 0, 40)))
    msgs.append(((-1, 0, -1), ("NT", 8, 8), ("MH", 1, 40, 8)))
    msgs.append(((1, 0, -1), ("NT", 16, 8), ("MH", 1, 48, 8)))
    msgs.append(((1, 0, 1), ("NT", 48, 8), ("MH", 0, 40, 8)))
    msgs.append(((-1, 0, 1), ("NT", 56, 8), ("MH", 0, 48, 8)))
    msgs.append(((-1, 0, 0), ("SX", 0), ("XH", 1)))
    msgs.append(((1, 0, 0), ("SX", 1), ("XH", 0)))
    return msgs


NEIGHBOURS = sorted(
    {d for d, _, _ in _messages(8, 16)} | {tuple(-v for v in d) for d, _, _ in _messages(8, 16)}
)


def _comb(vals, fn):
    total = None
    for weight in (1.0 / 3.0, 1.0 / 18.0, 1.0 / 36.0):
        part = None
        for i in range(19):
            if WEIGHTS[i] != weight:
                continue
            k = fn(VELOCITIES[i])
            if k == 0:
                continue
            if part is None:
                part = vals[i] if k > 0 else -vals[i]
            else:
                part = part + vals[i] if k > 0 else part - vals[i]
        if part is not None:
            term = part * weight
            total = term if total is None else total + term
    return total


def _collide(pulled, rho, ux, uy, uz, fluid):
    u = (ux, uy, uz)
    pair = {i: pulled[i] + pulled[i + 1] for i in range(1, 19, 2)}
    diff = {i: pulled[i] - pulled[i + 1] for i in range(1, 19, 2)}
    w1, w2 = 1.0 / 18.0, 1.0 / 36.0

    def signed(terms, table):
        total = None
        for i, sgn in terms:
            v = table[i]
            if total is None:
                total = v if sgn > 0 else -v
            else:
                total = total + v if sgn > 0 else total - v
        return total

    edges = [i for i in range(7, 19, 2)]
    p0 = pulled[0] * (1.0 / 3.0) + (pair[1] + pair[3] + pair[5]) * w1 + signed([(i, 1) for i in edges], pair) * w2
    p1 = []
    q = {}
    for a, axis_pop in enumerate((1, 3, 5)):
        edge = [i for i in edges if VELOCITIES[i][a] != 0]
        p1.append(diff[axis_pop] * w1 + signed([(i, VELOCITIES[i][a]) for i in edge], diff) * w2)
        q[a, a] = pair[axis_pop] * w1 + signed([(i, 1) for i in edge], pair) * w2
    for a in range(3):
        for b in range(a + 1, 3):
            edge = [i for i in edges if VELOCITIES[i][a] != 0 and VELOCITIES[i][b] != 0]
            q[a, b] = signed([(i, VELOCITIES[i][a] * VELOCITIES[i][b]) for i in edge], pair) * w2
            q[b, a] = q[a, b]
    usq = ux * ux + uy * uy + uz * uz
    qu = [q[a, 0] * ux + q[a, 1] * uy + q[a, 2] * uz for a in range(3)]
    p1u = p1[0] * ux + p1[1] * uy + p1[2] * uz
    uqu = ux * qu[0] + uy * qu[1] + uz * qu[2]
    moment = p0 * (1.0 - 1.5 * usq) + 3.0 * p1u + 4.5 * uqu
    vec = [3.0 * p1[a] + 9.0 * qu[a] - 3.0 * u[a] * p0 for a in range(3)]
    vu = vec[0] * ux + vec[1] * uy + vec[2] * uz
    inv = 1.0 / rho
    base = OMEGA * (moment - vu) - ux * inv
    bases = {0: base, 1: base + inv, -1: base - inv}
    wv = [OMEGA * v for v in vec]
    combos = {}
    layers = []
    for i in range(19):
        c = VELOCITIES[i]
        terms = [(a, c[a]) for a in range(3) if c[a] != 0]
        cv = None
        if terms:
            if len(terms) == 1:
                a, s = terms[0]
                cv = wv[a] if s > 0 else -wv[a]
            else:
                (a, s), (b, t) = terms
                pos = (a, b, s * t)
                if pos not in combos:
                    combos[pos] = wv[a] + wv[b] if s * t > 0 else wv[a] - wv[b]
                cv = combos[pos] if s > 0 else -combos[pos]
        val = (1.0 - OMEGA) * pulled[i] + bases[c[0]]
        if cv is not None:
            val = val + cv
        layers.append(jnp.where(fluid, val, pulled[OPPOSITE[i]]))
    sens = None
    for i in range(1, 19, 2):
        c = VELOCITIES[i]
        along = None
        for a in range(3):
            if c[a] == 0:
                continue
            if along is None:
                along = u[a] if c[a] > 0 else -u[a]
            else:
                along = along + u[a] if c[a] > 0 else along - u[a]
        term = (6.0 * WEIGHTS[i]) * along * diff[i]
        sens = term if sens is None else sens + term
    sens = jnp.where(fluid, -(rho * sens), 0.0)
    return layers, sens


def _where(dims):
    me = (lax.axis_index("gx"), lax.axis_index("gy"), lax.axis_index("gz"))

    def exists(d):
        cond = None
        for a in range(3):
            if d[a] == 0:
                continue
            v = me[a] + d[a]
            c = (v >= 0) if d[a] < 0 else (v < dims[a])
            cond = c if cond is None else jnp.logical_and(cond, c)
        return cond

    def target(d):
        return tuple(me[a] + d[a] for a in range(3))

    return me, exists, target


def _zero_missing(exists, xh, yh, exy, mh):
    for d, so, de in _messages(8, 16):
        back = tuple(-v for v in d)

        @pl.when(jnp.logical_not(exists(back)))
        def _():
            if de[0] == "XH":
                xh[de[1]] = jnp.zeros(xh.shape[1:], jnp.float32)
            elif de[0] == "YH":
                yh[de[1]] = jnp.zeros(yh.shape[1:], jnp.float32)
            elif de[0] == "EXY":
                exy[de[1]] = jnp.zeros(exy.shape[1:], jnp.float32)
            else:
                mh[de[1], pl.ds(de[2], de[3]), :] = jnp.zeros((de[3], mh.shape[-1]), jnp.float32)


def _step(s, src, xh, yh, exy, mt, rho_ref, vel_ref, mask_ref, level, emit, before=None):
    cx, cy, cz = 8, 16, 128
    lane = lax.broadcasted_iota(jnp.int32, (cy, cz), 1)
    lane1 = lax.broadcasted_iota(jnp.int32, (1, cz), 1)
    row = lax.broadcasted_iota(jnp.int32, (cy, cz), 0)

    def pulled_plane(p):
        out = []
        for i in range(19):
            vx, vy, vz = VELOCITIES[i]
            q = p + vx
            if 0 <= q < cx:
                plane = src[i, pl.ds(q * cy, cy), :]
            elif q == cx:
                plane = xh[s, 1, CXP.index(i)]
            else:
                plane = xh[s, 0, CXM.index(i)]
            if vz != 0:
                side = 1 if vz > 0 else 0
                if 0 <= q < cx:
                    zc = mt[s, side, pl.ds(q * cy, cy), :]
                    col = ZFACE_COL[i]
                else:
                    col, r0 = XZ_EDGE[i]
                    zc = mt[s, side, pl.ds(r0 % (cx * cy), cy), :]
                if vz > 0:
                    plane = jnp.where(lane == cz - 1, pltpu.roll(zc, (cz - 1 - col) % cz, 1),
                                      pltpu.roll(plane, cz - 1, 1))
                else:
                    plane = jnp.where(lane == 0, pltpu.roll(zc, (cz - col) % cz, 1),
                                      pltpu.roll(plane, 1, 1))
            if vy != 0:
                side_y = 1 if vy > 0 else 0
                ky = CYP.index(i) if vy > 0 else CYM.index(i)
                if 0 <= q < cx:
                    yrow = yh[s, side_y, ky, pl.ds(q, 1), :]
                else:
                    e, r = XY_EDGE[i]
                    yrow = exy[s, e, pl.ds(r, 1), :]
                if vz != 0:
                    side = 1 if vz > 0 else 0
                    colc, yoff = YZ_CORNER[i]
                    crow = mt[s, side, pl.ds(p * cy + yoff % cy, 1), :]
                    if vz > 0:
                        yrow = jnp.where(lane1 == cz - 1, pltpu.roll(crow, (cz - 1 - colc) % cz, 1),
                                         pltpu.roll(yrow, cz - 1, 1))
                    else:
                        yrow = jnp.where(lane1 == 0, pltpu.roll(crow, (cz - colc) % cz, 1),
                                         pltpu.roll(yrow, 1, 1))
                if vy > 0:
                    plane = jnp.where(row == cy - 1, yrow, pltpu.roll(plane, cy - 1, 0))
                else:
                    plane = jnp.where(row == 0, yrow, pltpu.roll(plane, 1, 0))
            out.append(plane)
        return out

    for p in range(cx):
        if before is not None:
            before(p)
        rs = pl.ds(p * cy, cy)
        pulled = pulled_plane(p)
        rho = rho_ref[level, rs, :]
        ux = vel_ref[level, 0, rs, :]
        uy = vel_ref[level, 1, rs, :]
        uz = vel_ref[level, 2, rs, :]
        fluid = mask_ref[rs, :] > 0
        layers, sens = _collide(pulled, rho, ux, uy, uz, fluid)
        emit(p, rs, layers, sens)


def _kernel(dims, adj_hbm, rho_hbm, vel_hbm, mask_hbm,
            mid_out, sens_out, xh_out, yh_out, exy_out, mh_out,
            adj_ref, rho_ref, vel_ref, mask_ref, load_sem,
            mid, sfin, out_sem, xh, yh, exy, sy, sx, nt, mh, mt, send_sem, recv_sem):
    cx, cy, cz = 8, 16, 128
    rows = cx * cy
    me, exists, target = _where(dims)

    barrier = pltpu.get_barrier_semaphore()
    for d in NEIGHBOURS:
        @pl.when(exists(d))
        def _():
            pl.semaphore_signal(barrier, inc=1, device_id=target(d), device_id_type=MESH)

    loads = [
        pltpu.make_async_copy(src, dst, load_sem.at[k])
        for k, (src, dst) in enumerate(
            ((adj_hbm, adj_ref), (vel_hbm, vel_ref), (rho_hbm, rho_ref), (mask_hbm, mask_ref))
        )
    ]
    for copy in loads:
        copy.start()

    mh[0, :, pl.ds(72, rows - 72), :] = jnp.zeros((2, rows - 72, cz), jnp.float32)
    _zero_missing(exists, xh.at[0], yh.at[0], exy.at[0], mh.at[0])

    lane_big = lax.broadcasted_iota(jnp.int32, (rows, cz), 1)
    msgs = _messages(cx, cy)

    def prepare(s, src):
        for side, pops, q in ((0, CXP, 0), (1, CXM, cx - 1)):
            for k, pop in enumerate(pops):
                sx[s, side, k] = src[pop, pl.ds(q * cy, cy), :]
        for side, pops, y in ((0, CYP, 0), (1, CYM, cy - 1)):
            for k, pop in enumerate(pops):
                sy[s, side, k] = src[pop, pl.ds(y, cx, stride=cy), :]
        n = jnp.zeros((rows, cz), jnp.float32)
        for j, (pop, z) in enumerate(ZCOLS):
            zz = z % cz
            n = jnp.where(lane_big == 8 * j, pltpu.roll(src[pop], (8 * j - zz) % cz, 1), n)
        nt[s] = n.T

    def descriptor(s, src, t):
        d, so, de = msgs[t]
        if so[0] == "S":
            sref = src.at[so[1], pl.ds(so[2] % rows, so[3]), :]
        elif so[0] == "SY":
            sref = sy.at[s, so[1]]
        elif so[0] == "SX":
            sref = sx.at[s, so[1]]
        else:
            sref = nt.at[s, pl.ds(so[1], so[2]), :]
        bufs = {"XH": (xh.at[0], xh_out), "YH": (yh.at[0], yh_out), "EXY": (exy.at[0], exy_out),
                "MH": (mh.at[0], mh_out)}[de[0]][s]
        if de[0] == "MH":
            dref = bufs.at[de[1], pl.ds(de[2], de[3]), :]
        else:
            dref = bufs.at[de[1]]
        return pltpu.make_async_remote_copy(
            src_ref=sref, dst_ref=dref, send_sem=send_sem.at[s, t], recv_sem=recv_sem.at[s, t],
            device_id=target(d), device_id_type=MESH)

    def send(s, src):
        for t in range(len(msgs)):
            @pl.when(exists(msgs[t][0]))
            def _():
                descriptor(s, src, t).start()

    def finish(s, src):
        for t in range(len(msgs)):
            d = msgs[t][0]
            back = tuple(-v for v in d)

            @pl.when(exists(back))
            def _():
                descriptor(s, src, t).wait_recv()

            @pl.when(exists(d))
            def _():
                descriptor(s, src, t).wait_send()

    peers = 0
    for d in NEIGHBOURS:
        term = 1
        for a in range(3):
            n = dims[a]
            if d[a] < 0:
                term = term * ((me[a] + n - 1) // n)
            elif d[a] > 0:
                term = term * ((2 * n - 2 - me[a]) // n)
        peers = peers + term
    loads[0].wait()
    prepare(0, adj_ref)
    pl.semaphore_wait(barrier, peers)
    send(0, adj_ref)
    for copy in loads[1:]:
        copy.wait()
    finish(0, adj_ref)
    for side in range(2):
        mt[0, side] = mh[0, side].T

    def flush(p):
        rs = pl.ds(p * cy, cy)
        pltpu.make_async_copy(mid.at[:, rs, :], mid_out.at[:, rs, :], out_sem.at[p]).start()

    def emit(p, rs, layers, sens):
        for i in range(19):
            mid[i, rs, :] = layers[i]
        sfin[rs, :] = sens

    _step(0, adj_ref, xh, yh, exy, mt, rho_ref, vel_ref, mask_ref, 1, emit,
          before=lambda p: flush(p - 1) if p >= 1 else None)
    prepare(1, mid)
    send(1, mid)
    flush(cx - 1)
    sens_copy = pltpu.make_async_copy(sfin, sens_out, out_sem.at[cx])
    sens_copy.start()
    finish(1, mid)
    for p in range(cx):
        rs = pl.ds(p * cy, cy)
        pltpu.make_async_copy(mid.at[:, rs, :], mid_out.at[:, rs, :], out_sem.at[p]).wait()
    sens_copy.wait()


def _last(dims, mid_hbm, s1_hbm, xh_hbm, yh_hbm, exy_hbm, mh_hbm, rho_hbm, vel_hbm, mask_hbm,
          out_hbm, sens_hbm,
          mid, s1, xh, yh, exy, mh, mt, rho, vel, mask, fin, sfin, in_sem, out_sem):
    cx, cy, cz = 8, 16, 128
    rows = cx * cy
    me, exists, target = _where(dims)
    mh[...] = jnp.zeros(mh.shape, jnp.float32)
    used = 72
    loads = [
        pltpu.make_async_copy(xh_hbm, xh.at[0], in_sem.at[0]),
        pltpu.make_async_copy(yh_hbm, yh.at[0], in_sem.at[1]),
        pltpu.make_async_copy(exy_hbm, exy.at[0], in_sem.at[2]),
        pltpu.make_async_copy(mh_hbm.at[:, pl.ds(0, used), :], mh.at[:, pl.ds(0, used), :], in_sem.at[3]),
        pltpu.make_async_copy(rho_hbm.at[pl.ds(0, 1)], rho, in_sem.at[4]),
        pltpu.make_async_copy(vel_hbm.at[pl.ds(0, 1)], vel, in_sem.at[5]),
        pltpu.make_async_copy(mask_hbm, mask, in_sem.at[6]),
        pltpu.make_async_copy(s1_hbm, s1, in_sem.at[7]),
        pltpu.make_async_copy(mid_hbm, mid, in_sem.at[8]),
    ]
    for copy in loads:
        copy.start()
    for copy in loads:
        copy.wait()
    _zero_missing(exists, xh.at[0], yh.at[0], exy.at[0], mh)

    for side in range(2):
        mt[0, side] = mh[side].T

    def flush(p):
        rs = pl.ds(p * cy, cy)
        pltpu.make_async_copy(fin.at[:, rs, :], out_hbm.at[:, rs, :], out_sem.at[p]).start()

    def emit(p, rs, layers, sens):
        for i in range(19):
            fin[i, rs, :] = layers[i]
        sfin[rs, :] = s1[rs, :] + sens

    _step(0, mid, xh, yh, exy, mt, rho, vel, mask, 0, emit)
    whole = pltpu.make_async_copy(fin, out_hbm, out_sem.at[0])
    whole.start()
    sens_copy = pltpu.make_async_copy(sfin, sens_hbm, out_sem.at[cx])
    sens_copy.start()
    whole.wait()
    sens_copy.wait()


def solution(mesh):
    dims = (mesh.shape["gx"], mesh.shape["gy"], mesh.shape["gz"])
    nmsg = len(_messages(8, 16))

    def shards(adjoint, density, velocity, pore_mask):
        npop, cx, cy, cz = adjoint.shape
        assert (cx, cy, cz) == (8, 16, 128)
        rows = cx * cy
        adj = adjoint.reshape(npop, rows, cz)
        rho = density.reshape(2, rows, cz)
        vel = velocity.reshape(2, 3, rows, cz)
        mask = pore_mask.reshape(rows, cz)
        hbm = pl.BlockSpec(memory_space=pltpu.HBM)
        f32 = jnp.float32
        halo_shapes = (
            jax.ShapeDtypeStruct((2, 5, cy, cz), f32),
            jax.ShapeDtypeStruct((2, 5, cx, cz), f32),
            jax.ShapeDtypeStruct((4, 8, cz), f32),
            jax.ShapeDtypeStruct((2, rows, cz), f32),
        )
        mid, s1, xh2, yh2, exy2, mh2 = pl.pallas_call(
            functools.partial(_kernel, dims),
            out_shape=(
                jax.ShapeDtypeStruct((npop, rows, cz), f32),
                jax.ShapeDtypeStruct((rows, cz), f32),
            ) + halo_shapes,
            in_specs=[hbm] * 4,
            out_specs=(hbm,) * 6,
            scratch_shapes=[
                pltpu.VMEM((npop, rows, cz), f32),
                pltpu.VMEM((2, rows, cz), f32),
                pltpu.VMEM((2, 3, rows, cz), f32),
                pltpu.VMEM((rows, cz), jnp.int32),
                pltpu.SemaphoreType.DMA((4,)),
                pltpu.VMEM((npop, rows, cz), f32),
                pltpu.VMEM((rows, cz), f32),
                pltpu.SemaphoreType.DMA((cx + 1,)),
                pltpu.VMEM((1, 2, 5, cy, cz), f32),
                pltpu.VMEM((1, 2, 5, cx, cz), f32),
                pltpu.VMEM((1, 4, 8, cz), f32),
                pltpu.VMEM((2, 2, 5, cx, cz), f32),
                pltpu.VMEM((2, 2, 5, cy, cz), f32),
                pltpu.VMEM((2, rows, cz), f32),
                pltpu.VMEM((1, 2, rows, cz), f32),
                pltpu.VMEM((1, 2, rows, cz), f32),
                pltpu.SemaphoreType.DMA((2, nmsg)),
                pltpu.SemaphoreType.DMA((2, nmsg)),
            ],
            compiler_params=pltpu.CompilerParams(
                collective_id=0, has_side_effects=True, vmem_limit_bytes=67043328
            ),
        )(adj, rho, vel, mask)
        out, sens = pl.pallas_call(
            functools.partial(_last, dims),
            out_shape=(
                jax.ShapeDtypeStruct((npop, rows, cz), f32),
                jax.ShapeDtypeStruct((rows, cz), f32),
            ),
            in_specs=[hbm] * 9,
            out_specs=(hbm, hbm),
            scratch_shapes=[
                pltpu.VMEM((npop, rows, cz), f32),
                pltpu.VMEM((rows, cz), f32),
                pltpu.VMEM((1, 2, 5, cy, cz), f32),
                pltpu.VMEM((1, 2, 5, cx, cz), f32),
                pltpu.VMEM((1, 4, 8, cz), f32),
                pltpu.VMEM((2, rows, cz), f32),
                pltpu.VMEM((1, 2, rows, cz), f32),
                pltpu.VMEM((1, rows, cz), f32),
                pltpu.VMEM((1, 3, rows, cz), f32),
                pltpu.VMEM((rows, cz), jnp.int32),
                pltpu.VMEM((npop, rows, cz), f32),
                pltpu.VMEM((rows, cz), f32),
                pltpu.SemaphoreType.DMA((9,)),
                pltpu.SemaphoreType.DMA((cx + 1,)),
            ],
            compiler_params=pltpu.CompilerParams(vmem_limit_bytes=67043328),
        )(mid, s1, xh2, yh2, exy2, mh2, rho, vel, mask)
        return out.reshape(npop, cx, cy, cz), sens.reshape(cx, cy, cz)

    placed = (
        P(None, "gx", "gy", "gz"),
        P(None, "gx", "gy", "gz"),
        P(None, None, "gx", "gy", "gz"),
        P("gx", "gy", "gz"),
    )
    return jax.shard_map(
        shards,
        mesh=mesh,
        in_specs=placed,
        out_specs=(P(None, "gx", "gy", "gz"), P("gx", "gy", "gz")),
        check_vma=False,
    )
```

```python
import functools

import jax
import jax.numpy as jnp
from jax import lax
from jax.experimental import pallas as pl
from jax.experimental.pallas import tpu as pltpu
from jax.sharding import PartitionSpec as P

VELOCITIES = [
    (0, 0, 0),
    (1, 0, 0),
    (-1, 0, 0),
    (0, 1, 0),
    (0, -1, 0),
    (0, 0, 1),
    (0, 0, -1),
    (1, 1, 0),
    (-1, -1, 0),
    (1, -1, 0),
    (-1, 1, 0),
    (1, 0, 1),
    (-1, 0, -1),
    (1, 0, -1),
    (-1, 0, 1),
    (0, 1, 1),
    (0, -1, -1),
    (0, 1, -1),
    (0, -1, 1),
]
WEIGHTS = [1.0 / 3.0] + [1.0 / 18.0] * 6 + [1.0 / 36.0] * 12
OPPOSITE = [0, 2, 1, 4, 3, 6, 5, 8, 7, 10, 9, 12, 11, 14, 13, 16, 15, 18, 17]
OMEGA = 1.25
MESH = pl.DeviceIdType.MESH

CXP = [1, 7, 9, 11, 13]
CXM = [2, 8, 10, 12, 14]
CYP = [3, 7, 10, 15, 17]
CYM = [4, 8, 9, 16, 18]
ZCOLS = [(5, 0), (11, 0), (14, 0), (15, 0), (18, 0), (6, -1), (12, -1), (13, -1), (16, -1), (17, -1)]
ZFACE_COL = {5: 0, 11: 8, 14: 16, 15: 24, 18: 32, 6: 0, 12: 8, 13: 16, 16: 24, 17: 32}
XZ_EDGE = {11: (40, 0), 14: (48, -16), 12: (40, -16), 13: (48, 0)}
YZ_CORNER = {15: (56, 0), 18: (64, -1), 16: (56, -1), 17: (64, 0)}
XY_EDGE = {7: (0, 0), 8: (1, 7), 9: (2, 7), 10: (3, 0)}


def _messages(cx, cy):
    rows = cx * cy
    msgs = []
    msgs.append(((0, -1, 0), ("SY", 0), ("YH", 1)))
    msgs.append(((0, 1, 0), ("SY", 1), ("YH", 0)))
    msgs.append(((0, -1, -1), ("NT", 24, 8), ("MH", 1, 56, 8)))
    msgs.append(((0, 1, -1), ("NT", 32, 8), ("MH", 1, 64, 8)))
    msgs.append(((0, 1, 1), ("NT", 64, 8), ("MH", 0, 56, 8)))
    msgs.append(((0, -1, 1), ("NT", 72, 8), ("MH", 0, 64, 8)))
    msgs.append(((-1, -1, 0), ("S", 7, 0, 8), ("EXY", 0)))
    msgs.append(((1, 1, 0), ("S", 8, rows - 8, 8), ("EXY", 1)))
    msgs.append(((-1, 1, 0), ("S", 9, cy - 8, 8), ("EXY", 2)))
    msgs.append(((1, -1, 0), ("S", 10, rows - cy, 8), ("EXY", 3)))
    msgs.append(((0, 0, -1), ("NT", 0, 40), ("MH", 1, 0, 40)))
    msgs.append(((0, 0, 1), ("NT", 40, 40), ("MH", 0, 0, 40)))
    msgs.append(((-1, 0, -1), ("NT", 8, 8), ("MH", 1, 40, 8)))
    msgs.append(((1, 0, -1), ("NT", 16, 8), ("MH", 1, 48, 8)))
    msgs.append(((1, 0, 1), ("NT", 48, 8), ("MH", 0, 40, 8)))
    msgs.append(((-1, 0, 1), ("NT", 56, 8), ("MH", 0, 48, 8)))
    msgs.append(((-1, 0, 0), ("SX", 0), ("XH", 1)))
    msgs.append(((1, 0, 0), ("SX", 1), ("XH", 0)))
    return msgs


NEIGHBOURS = sorted(
    {d for d, _, _ in _messages(8, 16)} | {tuple(-v for v in d) for d, _, _ in _messages(8, 16)}
)


def _comb(vals, fn):
    total = None
    for weight in (1.0 / 3.0, 1.0 / 18.0, 1.0 / 36.0):
        part = None
        for i in range(19):
            if WEIGHTS[i] != weight:
                continue
            k = fn(VELOCITIES[i])
            if k == 0:
                continue
            if part is None:
                part = vals[i] if k > 0 else -vals[i]
            else:
                part = part + vals[i] if k > 0 else part - vals[i]
        if part is not None:
            term = part * weight
            total = term if total is None else total + term
    return total


def _collide(pulled, rho, ux, uy, uz, fluid):
    u = (ux, uy, uz)
    pair = {i: pulled[i] + pulled[i + 1] for i in range(1, 19, 2)}
    diff = {i: pulled[i] - pulled[i + 1] for i in range(1, 19, 2)}
    w1, w2 = 1.0 / 18.0, 1.0 / 36.0

    def signed(terms, table):
        total = None
        for i, sgn in terms:
            v = table[i]
            if total is None:
                total = v if sgn > 0 else -v
            else:
                total = total + v if sgn > 0 else total - v
        return total

    edges = [i for i in range(7, 19, 2)]
    p0 = pulled[0] * (1.0 / 3.0) + (pair[1] + pair[3] + pair[5]) * w1 + signed([(i, 1) for i in edges], pair) * w2
    p1 = []
    q = {}
    for a, axis_pop in enumerate((1, 3, 5)):
        edge = [i for i in edges if VELOCITIES[i][a] != 0]
        p1.append(diff[axis_pop] * w1 + signed([(i, VELOCITIES[i][a]) for i in edge], diff) * w2)
        q[a, a] = pair[axis_pop] * w1 + signed([(i, 1) for i in edge], pair) * w2
    for a in range(3):
        for b in range(a + 1, 3):
            edge = [i for i in edges if VELOCITIES[i][a] != 0 and VELOCITIES[i][b] != 0]
            q[a, b] = signed([(i, VELOCITIES[i][a] * VELOCITIES[i][b]) for i in edge], pair) * w2
            q[b, a] = q[a, b]
    usq = ux * ux + uy * uy + uz * uz
    qu = [q[a, 0] * ux + q[a, 1] * uy + q[a, 2] * uz for a in range(3)]
    p1u = p1[0] * ux + p1[1] * uy + p1[2] * uz
    uqu = ux * qu[0] + uy * qu[1] + uz * qu[2]
    moment = p0 * (1.0 - 1.5 * usq) + 3.0 * p1u + 4.5 * uqu
    vec = [3.0 * p1[a] + 9.0 * qu[a] - 3.0 * u[a] * p0 for a in range(3)]
    vu = vec[0] * ux + vec[1] * uy + vec[2] * uz
    inv = 1.0 / rho
    base = OMEGA * (moment - vu) - ux * inv
    bases = {0: base, 1: base + inv, -1: base - inv}
    wv = [OMEGA * v for v in vec]
    combos = {}
    layers = []
    for i in range(19):
        c = VELOCITIES[i]
        terms = [(a, c[a]) for a in range(3) if c[a] != 0]
        cv = None
        if terms:
            if len(terms) == 1:
                a, s = terms[0]
                cv = wv[a] if s > 0 else -wv[a]
            else:
                (a, s), (b, t) = terms
                pos = (a, b, s * t)
                if pos not in combos:
                    combos[pos] = wv[a] + wv[b] if s * t > 0 else wv[a] - wv[b]
                cv = combos[pos] if s > 0 else -combos[pos]
        val = (1.0 - OMEGA) * pulled[i] + bases[c[0]]
        if cv is not None:
            val = val + cv
        layers.append(jnp.where(fluid, val, pulled[OPPOSITE[i]]))
    sens = None
    for i in range(1, 19, 2):
        c = VELOCITIES[i]
        along = None
        for a in range(3):
            if c[a] == 0:
                continue
            if along is None:
                along = u[a] if c[a] > 0 else -u[a]
            else:
                along = along + u[a] if c[a] > 0 else along - u[a]
        term = (6.0 * WEIGHTS[i]) * along * diff[i]
        sens = term if sens is None else sens + term
    sens = jnp.where(fluid, -(rho * sens), 0.0)
    return layers, sens


def _where(dims):
    me = (lax.axis_index("gx"), lax.axis_index("gy"), lax.axis_index("gz"))

    def exists(d):
        cond = None
        for a in range(3):
            if d[a] == 0:
                continue
            v = me[a] + d[a]
            c = (v >= 0) if d[a] < 0 else (v < dims[a])
            cond = c if cond is None else jnp.logical_and(cond, c)
        return cond

    def target(d):
        return tuple(me[a] + d[a] for a in range(3))

    return me, exists, target


def _zero_missing(exists, xh, yh, exy, mh):
    for d, so, de in _messages(8, 16):
        back = tuple(-v for v in d)

        @pl.when(jnp.logical_not(exists(back)))
        def _():
            if de[0] == "XH":
                xh[de[1]] = jnp.zeros(xh.shape[1:], jnp.float32)
            elif de[0] == "YH":
                yh[de[1]] = jnp.zeros(yh.shape[1:], jnp.float32)
            elif de[0] == "EXY":
                exy[de[1]] = jnp.zeros(exy.shape[1:], jnp.float32)
            else:
                mh[de[1], pl.ds(de[2], de[3]), :] = jnp.zeros((de[3], mh.shape[-1]), jnp.float32)


def _step(s, src, xh, yh, exy, mt, rho_ref, vel_ref, mask_ref, level, emit, before=None):
    cx, cy, cz = 8, 16, 128
    lane = lax.broadcasted_iota(jnp.int32, (cy, cz), 1)
    lane1 = lax.broadcasted_iota(jnp.int32, (1, cz), 1)
    row = lax.broadcasted_iota(jnp.int32, (cy, cz), 0)

    def pulled_plane(p):
        out = []
        for i in range(19):
            vx, vy, vz = VELOCITIES[i]
            q = p + vx
            if 0 <= q < cx:
                plane = src[i, pl.ds(q * cy, cy), :]
            elif q == cx:
                plane = xh[s, 1, CXP.index(i)]
            else:
                plane = xh[s, 0, CXM.index(i)]
            if vz != 0:
                side = 1 if vz > 0 else 0
                if 0 <= q < cx:
                    zc = mt[s, side, pl.ds(q * cy, cy), :]
                    col = ZFACE_COL[i]
                else:
                    col, r0 = XZ_EDGE[i]
                    zc = mt[s, side, pl.ds(r0 % (cx * cy), cy), :]
                if vz > 0:
                    plane = jnp.where(lane == cz - 1, pltpu.roll(zc, (cz - 1 - col) % cz, 1),
                                      pltpu.roll(plane, cz - 1, 1))
                else:
                    plane = jnp.where(lane == 0, pltpu.roll(zc, (cz - col) % cz, 1),
                                      pltpu.roll(plane, 1, 1))
            if vy != 0:
                side_y = 1 if vy > 0 else 0
                ky = CYP.index(i) if vy > 0 else CYM.index(i)
                if 0 <= q < cx:
                    yrow = yh[s, side_y, ky, pl.ds(q, 1), :]
                else:
                    e, r = XY_EDGE[i]
                    yrow = exy[s, e, pl.ds(r, 1), :]
                if vz != 0:
                    side = 1 if vz > 0 else 0
                    colc, yoff = YZ_CORNER[i]
                    crow = mt[s, side, pl.ds(p * cy + yoff % cy, 1), :]
                    if vz > 0:
                        yrow = jnp.where(lane1 == cz - 1, pltpu.roll(crow, (cz - 1 - colc) % cz, 1),
                                         pltpu.roll(yrow, cz - 1, 1))
                    else:
                        yrow = jnp.where(lane1 == 0, pltpu.roll(crow, (cz - colc) % cz, 1),
                                         pltpu.roll(yrow, 1, 1))
                if vy > 0:
                    plane = jnp.where(row == cy - 1, yrow, pltpu.roll(plane, cy - 1, 0))
                else:
                    plane = jnp.where(row == 0, yrow, pltpu.roll(plane, 1, 0))
            out.append(plane)
        return out

    for p in range(cx):
        if before is not None:
            before(p)
        rs = pl.ds(p * cy, cy)
        pulled = pulled_plane(p)
        rho = rho_ref[level, rs, :]
        ux = vel_ref[level, 0, rs, :]
        uy = vel_ref[level, 1, rs, :]
        uz = vel_ref[level, 2, rs, :]
        fluid = mask_ref[rs, :] > 0
        layers, sens = _collide(pulled, rho, ux, uy, uz, fluid)
        emit(p, rs, layers, sens)


def _kernel(dims, adj_hbm, rho_hbm, vel_hbm, mask_hbm,
            mid_out, sens_out, xh_out, yh_out, exy_out, mh_out,
            adj_ref, rho_ref, vel_ref, mask_ref, load_sem,
            mid, sfin, out_sem, xh, yh, exy, sy, sx, nt, mh, mt, send_sem, recv_sem):
    cx, cy, cz = 8, 16, 128
    rows = cx * cy
    me, exists, target = _where(dims)

    barrier = pltpu.get_barrier_semaphore()
    for d in NEIGHBOURS:
        @pl.when(exists(d))
        def _():
            pl.semaphore_signal(barrier, inc=1, device_id=target(d), device_id_type=MESH)

    loads = [
        pltpu.make_async_copy(src, dst, load_sem.at[k])
        for k, (src, dst) in enumerate(
            ((adj_hbm, adj_ref), (vel_hbm, vel_ref), (rho_hbm, rho_ref), (mask_hbm, mask_ref))
        )
    ]
    for copy in loads:
        copy.start()

    mh[0, :, pl.ds(72, rows - 72), :] = jnp.zeros((2, rows - 72, cz), jnp.float32)
    _zero_missing(exists, xh.at[0], yh.at[0], exy.at[0], mh.at[0])

    lane_big = lax.broadcasted_iota(jnp.int32, (rows, cz), 1)
    msgs = _messages(cx, cy)

    def prepare(s, src):
        for side, pops, q in ((0, CXP, 0), (1, CXM, cx - 1)):
            for k, pop in enumerate(pops):
                sx[s, side, k] = src[pop, pl.ds(q * cy, cy), :]
        for side, pops, y in ((0, CYP, 0), (1, CYM, cy - 1)):
            for k, pop in enumerate(pops):
                sy[s, side, k] = src[pop, pl.ds(y, cx, stride=cy), :]
        n = jnp.zeros((rows, cz), jnp.float32)
        for j, (pop, z) in enumerate(ZCOLS):
            zz = z % cz
            n = jnp.where(lane_big == 8 * j, pltpu.roll(src[pop], (8 * j - zz) % cz, 1), n)
        nt[s] = n.T

    def descriptor(s, src, t):
        d, so, de = msgs[t]
        if so[0] == "S":
            sref = src.at[so[1], pl.ds(so[2] % rows, so[3]), :]
        elif so[0] == "SY":
            sref = sy.at[s, so[1]]
        elif so[0] == "SX":
            sref = sx.at[s, so[1]]
        else:
            sref = nt.at[s, pl.ds(so[1], so[2]), :]
        bufs = {"XH": (xh.at[0], xh_out), "YH": (yh.at[0], yh_out), "EXY": (exy.at[0], exy_out),
                "MH": (mh.at[0], mh_out)}[de[0]][s]
        if de[0] == "MH":
            dref = bufs.at[de[1], pl.ds(de[2], de[3]), :]
        else:
            dref = bufs.at[de[1]]
        return pltpu.make_async_remote_copy(
            src_ref=sref, dst_ref=dref, send_sem=send_sem.at[s, t], recv_sem=recv_sem.at[s, t],
            device_id=target(d), device_id_type=MESH)

    def send(s, src):
        for t in range(len(msgs)):
            @pl.when(exists(msgs[t][0]))
            def _():
                descriptor(s, src, t).start()

    def finish(s, src):
        for t in range(len(msgs)):
            d = msgs[t][0]
            back = tuple(-v for v in d)

            @pl.when(exists(back))
            def _():
                descriptor(s, src, t).wait_recv()

            @pl.when(exists(d))
            def _():
                descriptor(s, src, t).wait_send()

    peers = 0
    for d in NEIGHBOURS:
        term = 1
        for a in range(3):
            n = dims[a]
            if d[a] < 0:
                term = term * ((me[a] + n - 1) // n)
            elif d[a] > 0:
                term = term * ((2 * n - 2 - me[a]) // n)
        peers = peers + term
    loads[0].wait()
    prepare(0, adj_ref)
    pl.semaphore_wait(barrier, peers)
    send(0, adj_ref)
    for copy in loads[1:]:
        copy.wait()
    finish(0, adj_ref)
    for side in range(2):
        mt[0, side] = mh[0, side].T

    def flush(p):
        rs = pl.ds(p * cy, cy)
        pltpu.make_async_copy(mid.at[:, rs, :], mid_out.at[:, rs, :], out_sem.at[p]).start()

    def emit(p, rs, layers, sens):
        for i in range(19):
            mid[i, rs, :] = layers[i]
        sfin[rs, :] = sens

    _step(0, adj_ref, xh, yh, exy, mt, rho_ref, vel_ref, mask_ref, 1, emit,
          before=lambda p: flush(p - 1) if p >= 1 else None)
    prepare(1, mid)
    send(1, mid)
    flush(cx - 1)
    sens_copy = pltpu.make_async_copy(sfin, sens_out, out_sem.at[cx])
    sens_copy.start()
    finish(1, mid)
    for p in range(cx):
        rs = pl.ds(p * cy, cy)
        pltpu.make_async_copy(mid.at[:, rs, :], mid_out.at[:, rs, :], out_sem.at[p]).wait()
    sens_copy.wait()


def _last(dims, mid_hbm, s1_hbm, xh_hbm, yh_hbm, exy_hbm, mh_hbm, rho_hbm, vel_hbm, mask_hbm,
          out_hbm, sens_hbm,
          mid, s1, xh, yh, exy, mh, mt, rho, vel, mask, fin, sfin, in_sem, out_sem):
    cx, cy, cz = 8, 16, 128
    rows = cx * cy
    me, exists, target = _where(dims)
    mh[...] = jnp.zeros(mh.shape, jnp.float32)
    used = 72
    loads = [
        pltpu.make_async_copy(xh_hbm, xh.at[0], in_sem.at[0]),
        pltpu.make_async_copy(yh_hbm, yh.at[0], in_sem.at[1]),
        pltpu.make_async_copy(exy_hbm, exy.at[0], in_sem.at[2]),
        pltpu.make_async_copy(mh_hbm.at[:, pl.ds(0, used), :], mh.at[:, pl.ds(0, used), :], in_sem.at[3]),
        pltpu.make_async_copy(rho_hbm.at[pl.ds(0, 1)], rho, in_sem.at[4]),
        pltpu.make_async_copy(vel_hbm.at[pl.ds(0, 1)], vel, in_sem.at[5]),
        pltpu.make_async_copy(mask_hbm, mask, in_sem.at[6]),
        pltpu.make_async_copy(s1_hbm, s1, in_sem.at[7]),
        pltpu.make_async_copy(mid_hbm, mid, in_sem.at[8]),
    ]
    for copy in loads:
        copy.start()
    for copy in loads[:4]:
        copy.wait()
    _zero_missing(exists, xh.at[0], yh.at[0], exy.at[0], mh)

    for side in range(2):
        mt[0, side] = mh[side].T
    for copy in loads[4:]:
        copy.wait()

    def flush(p):
        rs = pl.ds(p * cy, cy)
        pltpu.make_async_copy(fin.at[:, rs, :], out_hbm.at[:, rs, :], out_sem.at[p]).start()

    def emit(p, rs, layers, sens):
        for i in range(19):
            fin[i, rs, :] = layers[i]
        sfin[rs, :] = s1[rs, :] + sens

    _step(0, mid, xh, yh, exy, mt, rho, vel, mask, 0, emit,
          before=lambda p: flush(p - 1) if p >= 1 else None)
    flush(cx - 1)
    sens_copy = pltpu.make_async_copy(sfin, sens_hbm, out_sem.at[cx])
    sens_copy.start()
    for p in range(cx):
        rs = pl.ds(p * cy, cy)
        pltpu.make_async_copy(fin.at[:, rs, :], out_hbm.at[:, rs, :], out_sem.at[p]).wait()
    sens_copy.wait()


def solution(mesh):
    dims = (mesh.shape["gx"], mesh.shape["gy"], mesh.shape["gz"])
    nmsg = len(_messages(8, 16))

    def shards(adjoint, density, velocity, pore_mask):
        npop, cx, cy, cz = adjoint.shape
        assert (cx, cy, cz) == (8, 16, 128)
        rows = cx * cy
        adj = adjoint.reshape(npop, rows, cz)
        rho = density.reshape(2, rows, cz)
        vel = velocity.reshape(2, 3, rows, cz)
        mask = pore_mask.reshape(rows, cz)
        hbm = pl.BlockSpec(memory_space=pltpu.HBM)
        f32 = jnp.float32
        halo_shapes = (
            jax.ShapeDtypeStruct((2, 5, cy, cz), f32),
            jax.ShapeDtypeStruct((2, 5, cx, cz), f32),
            jax.ShapeDtypeStruct((4, 8, cz), f32),
            jax.ShapeDtypeStruct((2, rows, cz), f32),
        )
        mid, s1, xh2, yh2, exy2, mh2 = pl.pallas_call(
            functools.partial(_kernel, dims),
            out_shape=(
                jax.ShapeDtypeStruct((npop, rows, cz), f32),
                jax.ShapeDtypeStruct((rows, cz), f32),
            ) + halo_shapes,
            in_specs=[hbm] * 4,
            out_specs=(hbm,) * 6,
            scratch_shapes=[
                pltpu.VMEM((npop, rows, cz), f32),
                pltpu.VMEM((2, rows, cz), f32),
                pltpu.VMEM((2, 3, rows, cz), f32),
                pltpu.VMEM((rows, cz), jnp.int32),
                pltpu.SemaphoreType.DMA((4,)),
                pltpu.VMEM((npop, rows, cz), f32),
                pltpu.VMEM((rows, cz), f32),
                pltpu.SemaphoreType.DMA((cx + 1,)),
                pltpu.VMEM((1, 2, 5, cy, cz), f32),
                pltpu.VMEM((1, 2, 5, cx, cz), f32),
                pltpu.VMEM((1, 4, 8, cz), f32),
                pltpu.VMEM((2, 2, 5, cx, cz), f32),
                pltpu.VMEM((2, 2, 5, cy, cz), f32),
                pltpu.VMEM((2, rows, cz), f32),
                pltpu.VMEM((1, 2, rows, cz), f32),
                pltpu.VMEM((1, 2, rows, cz), f32),
                pltpu.SemaphoreType.DMA((2, nmsg)),
                pltpu.SemaphoreType.DMA((2, nmsg)),
            ],
            compiler_params=pltpu.CompilerParams(
                collective_id=0, has_side_effects=True, vmem_limit_bytes=67043328
            ),
        )(adj, rho, vel, mask)
        out, sens = pl.pallas_call(
            functools.partial(_last, dims),
            out_shape=(
                jax.ShapeDtypeStruct((npop, rows, cz), f32),
                jax.ShapeDtypeStruct((rows, cz), f32),
            ),
            in_specs=[hbm] * 9,
            out_specs=(hbm, hbm),
            scratch_shapes=[
                pltpu.VMEM((npop, rows, cz), f32),
                pltpu.VMEM((rows, cz), f32),
                pltpu.VMEM((1, 2, 5, cy, cz), f32),
                pltpu.VMEM((1, 2, 5, cx, cz), f32),
                pltpu.VMEM((1, 4, 8, cz), f32),
                pltpu.VMEM((2, rows, cz), f32),
                pltpu.VMEM((1, 2, rows, cz), f32),
                pltpu.VMEM((1, rows, cz), f32),
                pltpu.VMEM((1, 3, rows, cz), f32),
                pltpu.VMEM((rows, cz), jnp.int32),
                pltpu.VMEM((npop, rows, cz), f32),
                pltpu.VMEM((rows, cz), f32),
                pltpu.SemaphoreType.DMA((9,)),
                pltpu.SemaphoreType.DMA((cx + 1,)),
            ],
            compiler_params=pltpu.CompilerParams(vmem_limit_bytes=67043328),
        )(mid, s1, xh2, yh2, exy2, mh2, rho, vel, mask)
        return out.reshape(npop, cx, cy, cz), sens.reshape(cx, cy, cz)

    placed = (
        P(None, "gx", "gy", "gz"),
        P(None, "gx", "gy", "gz"),
        P(None, None, "gx", "gy", "gz"),
        P("gx", "gy", "gz"),
    )
    return jax.shard_map(
        shards,
        mesh=mesh,
        in_specs=placed,
        out_specs=(P(None, "gx", "gy", "gz"), P("gx", "gy", "gz")),
        check_vma=False,
    )
```
